32 devices in a mesh: seq: 8 (over z, x), dp: 4 (over y, core).
Axes of the slice: x: 2, y: 2, z: 4, core: 2. Of those that a mesh axis runs over, the one named last changes fastest.
Arguments:
- layer_input: bfloat16 [4, 1024, 4096], P('dp', 'seq'), may hold values from -6 to 6
- projection: bfloat16 [4096, 256], replicated, may hold values from -0.09375 to 0.09375
- ssm_input: bfloat16 [4, 1024, 4096], P('dp', 'seq'), may hold values from -6 to 6
- step_logit: float32 [4, 1024, 64], P('dp', 'seq'), may hold values from -4 to 4
- decay_rate: float32 [64], replicated, may hold values from 0.00048828125 to 0.1
- output_grad: bfloat16 [4, 1024, 4096], P('dp', 'seq'), may hold values from -6 to 6
Outputs:
- input_grad: bfloat16 [4, 1024, 4096], P('dp', 'seq')
- step_grad: float32 [4, 1024, 64], P('dp', 'seq')
- rate_grad: float32 [64], replicated
- projection_grad: float32 [4096, 256], P('seq')
The draws below stay inside these ranges and needn't reach their ends.
All inputs are finite; a program needn't handle non-finite values.
Results may differ from the reference program's by a relative error of at most 0.011.
Values sent between devices are 32-bit elements; how exact they have to be, the bound alone decides.
A program may use at most 320 MiB of HBM per device.

```python
import math
import jax
import jax.numpy as jnp
from jax import lax

D = 4096
H = 64
P_SIZE = 64
N = 128
L_DEV = 128
HP = 4096
LENGTH = 1024
TRACES = 4


def shard_levels(stream_key, dims, split, smallest, high):
    level = 1.0
    for position, parts in split:
        heights = jax.random.uniform(jax.random.fold_in(jax.random.fold_in(stream_key, 6), position), (parts,), jnp.float32, smallest / len(split), high / len(split))
        level = level * jnp.repeat(jnp.exp(heights), dims[position] // parts).reshape((-1,) + (1,) * (len(dims) - 1 - position))
    return level


def bell_draw(own_key, shape, width, most, cuts=(), dtype=jnp.bfloat16):
    values = jax.random.normal(own_key, shape, jnp.float32) * width
    if len(cuts) > 0:
        values = shard_levels(own_key, shape, cuts, -0.22, 0.18) * values
    return jnp.clip(values, min=-most, max=most).astype(dtype)


def setup_inputs(seed: int = 0) -> dict:
    key_list = jax.random.split(jax.random.key(seed), 7)
    return {
        "layer_input": bell_draw(key_list[0], (TRACES, LENGTH, D), 1.0, 6.0, ((0, 4), (1, 8))),
        "projection": bell_draw(key_list[1], (D, 2 * N), D ** -0.5, 0.09375),
        "ssm_input": bell_draw(key_list[2], (TRACES, LENGTH, HP), 1.0, 6.0, ((0, 4), (1, 8))),
        "step_logit": bell_draw(key_list[3], (TRACES, LENGTH, H), 1.0, 4.0, ((0, 4), (1, 8)), jnp.float32),
        "decay_rate": jnp.clip(jnp.exp(jax.random.uniform(key_list[4], (H,), jnp.float32, math.log(0.00048828125), math.log(0.1))), 0.00048828125, 0.1),
        "output_grad": bell_draw(key_list[5], (TRACES, LENGTH, HP), 1.0, 6.0, ((0, 4), (1, 8))),
    }


def span_forward(ssm_block, b_block, c_block, logit_block, decay_rate, carry_in):
    row_count = ssm_block.shape[0]
    head_count = logit_block.shape[1]
    values = ssm_block.astype(jnp.float32).reshape(row_count, head_count, -1)
    b_vals = b_block.astype(jnp.float32)
    c_vals = c_block.astype(jnp.float32)
    dt_soft = jax.nn.softplus(logit_block)
    log_decay = jnp.cumsum(-decay_rate[None, :] * dt_soft, axis=0)
    causal = (lax.broadcasted_iota(jnp.int32, (row_count, row_count), 0) >= lax.broadcasted_iota(jnp.int32, (row_count, row_count), 1))[None, :, :]
    decay_heads = log_decay.T
    gap_log = decay_heads[:, :, None] - decay_heads[:, None, :]
    decays = jnp.exp(jnp.where(causal, gap_log, -jnp.inf))
    scores = jnp.einsum('tn,sn->ts', c_vals, b_vals, precision=lax.Precision.HIGHEST)
    weights = decays * scores[None, :, :] * dt_soft.T[:, None, :]
    inner = jnp.einsum('hts,shp->thp', weights, values, precision=lax.Precision.HIGHEST)
    outer = jnp.exp(log_decay)[:, :, None] * jnp.einsum('tn,hpn->thp', c_vals, carry_in, precision=lax.Precision.HIGHEST)
    to_end = jnp.exp(log_decay[-1][None, :] - log_decay) * dt_soft
    carry_out = jnp.exp(log_decay[-1])[:, None, None] * carry_in + jnp.einsum('sh,shp,sn->hpn', to_end, values, b_vals, precision=lax.Precision.HIGHEST)
    return (inner + outer, carry_out)

def reference(layer_input, projection, ssm_input, step_logit, decay_rate, output_grad):
    state_size = projection.shape[1] // 2

    def one_trace(items):
        tokens, x_rows, logit_rows, grad_rows = items
        projected = jnp.dot(tokens, projection, preferred_element_type=jnp.float32).astype(jnp.bfloat16)

        def forward(x_all, b_all, c_all, logit_all, rate_vec):
            blocks = (x_all.reshape(-1, L_DEV, x_all.shape[1]), b_all.reshape(-1, L_DEV, state_size), c_all.reshape(-1, L_DEV, state_size), logit_all.reshape(-1, L_DEV, logit_all.shape[1]))

            def advance(carry, block):
                result, carry_next = span_forward(block[0], block[1], block[2], block[3], rate_vec, carry)
                return (carry_next, result)
            start = jnp.zeros((H, P_SIZE, state_size), jnp.float32)
            unused, outputs = lax.scan(jax.checkpoint(advance), start, blocks)
            return outputs
        unused, pullback = jax.vjp(forward, x_rows, projected[:, :state_size], projected[:, state_size:], logit_rows, decay_rate)
        grad_x, grad_b, grad_c, grad_logit, grad_rate = pullback(grad_rows.astype(jnp.float32).reshape(-1, L_DEV, H, P_SIZE))
        grad_bc = jnp.concatenate([grad_b, grad_c], axis=1)
        grad_w = lax.dot_general(tokens, grad_bc, (((0,), (0,)), ((), ())), preferred_element_type=jnp.float32)
        return (grad_x, grad_logit, grad_rate, grad_w)
    grad_x, grad_logit, grad_rate, grad_w = lax.map(one_trace, (layer_input, ssm_input, step_logit, output_grad))
    return (grad_x, grad_logit, lax.optimization_barrier(jnp.sum(grad_rate, axis=0)), lax.optimization_barrier(jnp.sum(grad_w, axis=0)))
```

```python
import functools

import jax
import jax.numpy as jnp
from jax import lax
from jax.experimental import pallas as pl
from jax.experimental.pallas import tpu as pltpu
from jax.sharding import PartitionSpec as P

F32 = jnp.float32
BF16 = jnp.bfloat16
HEADS = 4


def dot(a, b, ca, cb):
    return lax.dot_general(a, b, (((ca,), (cb,)), ((), ())), preferred_element_type=F32)


def pair_columns(cols, j, size):
    rows = cols.shape[0]
    lane = lax.broadcasted_iota(jnp.int32, (rows, 2 * size), 1)
    return jnp.where(lane < size, cols[:, j : j + 1], cols[:, j + 1 : j + 2])


def layer_kernel(
    n, size, b_ref, c_ref, cf_ref, x_ref, g_ref, col_ref, row_ref, d_ref,
    dx_ref, rows_ref, cols_ref, ef_ref, gbc_ref,
    e_own, e_other, f_own, f_other, scores, d_scores, d_b, d_c, back, back_ef,
    d_in, cf_in, c_in, gs_snd, gs_in, e_in, f_in, e_snd, f_snd, back_in, back_ef_in,
    small_sem, gs_sem, e_sem, f_sem,
):
    chunks = gs_snd.shape[0]
    length = b_ref.shape[0]
    state = b_ref.shape[1]
    width = 2 * size
    group = HEADS * size
    heads = chunks * HEADS
    nz = n // 2
    me = lax.axis_index("seq")
    odd = lax.rem(me, 2)
    z = lax.div(me, 2)
    partner = me + 1 - 2 * odd
    first, last = z == 0, z == nz - 1
    barrier = pltpu.get_barrier_semaphore()

    def greet(who):
        pl.semaphore_signal(
            barrier, inc=1, device_id={"seq": who}, device_id_type=pl.DeviceIdType.MESH
        )

    greet(partner)
    pl.when(jnp.logical_not(first))(lambda: greet(me - 2))
    pl.when(jnp.logical_not(last))(lambda: greet(me + 2))

    def send(src, dst, sems, k, who):
        return pltpu.make_async_remote_copy(
            src_ref=src, dst_ref=dst, send_sem=sems.at[0, k], recv_sem=sems.at[1, k],
            device_id={"seq": who}, device_id_type=pl.DeviceIdType.MESH,
        )

    def copy_d():
        return send(d_ref, d_in, small_sem, 0, partner)

    def copy_c():
        return send(cf_ref, cf_in, small_sem, 1, partner)

    def copy_back():
        return send(back, back_in, small_sem, 2, partner)

    def copy_back_ef():
        return send(back_ef, back_ef_in, small_sem, 3, partner)

    def copy_g(k):
        return send(gs_snd.at[k], gs_in.at[k], gs_sem, k, partner)

    def copy_e(k):
        return send(e_snd.at[k], e_in.at[k], e_sem, k, me + 2)

    def copy_f(k):
        return send(f_snd.at[k], f_in.at[k], f_sem, k, me - 2)

    def pair_lanes(k, pair):
        return pl.ds(pl.multiple_of(k * group + pair * width, width), width)

    def scale(k, unused):
        cols = col_ref[k]
        for pair in range(HEADS // 2):
            grow = pair_columns(cols, 2 * pair + 3 * HEADS, size)
            gs_snd[k, :, pl.ds(pair * width, width)] = (
                g_ref[:, pair_lanes(k, pair)].astype(F32) * grow
            )
        copy_g(k).start()
        return unused

    end = jnp.logical_or(first, last)
    pl.when(end)(lambda: pl.semaphore_wait(barrier, min(nz, 2)))
    pl.when(jnp.logical_not(end))(lambda: pl.semaphore_wait(barrier, 3))
    copy_d().start()
    copy_c().start()
    lax.fori_loop(0, chunks, scale, 0)

    @pl.when(first)
    def _():
        e_in[...] = jnp.zeros_like(e_in)

    @pl.when(last)
    def _():
        f_in[...] = jnp.zeros_like(f_in)

    b, c = b_ref[...], c_ref[...]
    scores[...] = dot(b, c, 1, 1)
    d_scores[...] = jnp.zeros_like(d_scores)
    d_b[...] = jnp.zeros_like(d_b)
    d_c[...] = jnp.zeros_like(d_c)
    back[...] = jnp.zeros_like(back)
    cols_ref[...] = jnp.zeros_like(cols_ref)
    copy_d().wait_recv()
    copy_c().wait_recv()
    c_in[...] = cf_in[...].astype(BF16)

    def row(ref, k):
        return ref[k]

    def forward(k):
        cols = col_ref[k]
        value = e_in[k]
        parts = []
        for pair in range(HEADS // 2):
            j = 2 * pair
            weight = pair_columns(cols, j + HEADS, size) * pair_columns(cols, j + 2 * HEADS, size)
            parts.append((x_ref[:, pair_lanes(k, pair)].astype(F32) * weight).astype(BF16))
        near = dot(b_ref[...], jnp.concatenate(parts, axis=1), 0, 0)

        @pl.when(odd == 0)
        def _():
            e_own[k] = value.astype(BF16)
            middle = row(d_ref, k) * value + near
            e_other[k] = middle.astype(BF16)
            e_snd[k] = row(d_in, k) * middle

        @pl.when(odd == 1)
        def _():
            e_other[k] = value.astype(BF16)
            middle = row(d_in, k) * value
            e_own[k] = middle.astype(BF16)
            e_snd[k] = row(d_ref, k) * middle + near

    def backward(k):
        value = f_in[k]
        near = dot(c_ref[...], gs_snd[k].astype(BF16), 0, 0)
        far = dot(c_in[...], gs_in[k].astype(BF16), 0, 0)

        @pl.when(odd == 0)
        def _():
            f_other[k] = value.astype(BF16)
            middle = row(d_in, k) * value + far
            f_own[k] = middle.astype(BF16)
            f_snd[k] = row(d_ref, k) * middle + near

        @pl.when(odd == 1)
        def _():
            f_own[k] = value.astype(BF16)
            middle = row(d_ref, k) * value + near
            f_other[k] = middle.astype(BF16)
            f_snd[k] = row(d_in, k) * middle + far

    def gradients(k):
        cols = col_ref[k]
        rows = row_ref[k]
        k_st = scores[...]
        causal = lax.broadcasted_iota(jnp.int32, (length, length), 1) >= lax.broadcasted_iota(
            jnp.int32, (length, length), 0
        )
        low = lax.broadcasted_iota(jnp.int32, (length, width), 1) < size
        place = lax.broadcasted_iota(jnp.int32, cols_ref.shape, 1) - k * HEADS
        other_place = lax.broadcasted_iota(jnp.int32, (length, state), 1) - k * HEADS
        result = cols_ref[...]
        other = back[1]
        q_sum = d_scores[...]
        b_sum, c_sum, c_other = d_b[...], d_c[...], back[0]
        for pair in range(HEADS // 2):
            lanes = pl.ds(pair * width, width)
            wide = pair_lanes(k, pair)
            x2, g2 = x_ref[:, wide], g_ref[:, wide]
            x2f = x2.astype(F32)
            e2, f2 = e_own[k, :, lanes], f_own[k, :, lanes]
            e2o, f2o = e_other[k, :, lanes], f_other[k, :, lanes]
            gs, gso = gs_snd[k, :, lanes], gs_in[k, :, lanes]
            j = 2 * pair
            dt2 = pair_columns(cols, j + HEADS, size)
            end2 = pair_columns(cols, j + 2 * HEADS, size)
            g_low = jnp.where(low, g2, jnp.zeros_like(g2))
            g_high = jnp.where(low, jnp.zeros_like(g2), g2)
            g_both = jnp.concatenate([g_low, g_high], axis=0)
            gram = dot(x2, g_both, 1, 1)
            weights = []
            for side in range(2):
                h = j + side
                gap = rows[h : h + 1, :] - cols[:, h : h + 1]
                decay = jnp.exp(jnp.where(causal, gap, -jnp.inf))
                mg = decay * gram[:, side * length : (side + 1) * length]
                dt = cols[:, h + HEADS : h + HEADS + 1]
                q_sum = q_sum + mg * dt
                raw = mg * k_st
                rows_ref[k, h : h + 1, :] = jnp.sum(raw * dt, axis=0, keepdims=True)
                result = jnp.where(place == h, jnp.sum(raw, axis=1, keepdims=True), result)
                weights.append((decay * k_st).astype(BF16))
            z2 = dot(jnp.concatenate(weights, axis=1), g_both, 1, 0)
            z_in = dot(b, f2, 1, 0) * end2
            dx_ref[:, wide] = (dt2 * (z2 + z_in)).astype(dx_ref.dtype)
            xz = x2f * z_in
            gy = gs * dot(c, e2, 1, 0)
            gyo = gso * dot(c_in[...], e2o, 1, 0)
            zero = jnp.zeros_like(xz)
            for side in range(2):
                h = j + side
                mask = low if side == 0 else jnp.logical_not(low)
                xs = jnp.sum(jnp.where(mask, xz, zero), axis=1, keepdims=True)
                ys = jnp.sum(jnp.where(mask, gy, zero), axis=1, keepdims=True)
                yo = jnp.sum(jnp.where(mask, gyo, zero), axis=1, keepdims=True)
                result = jnp.where(place == h + heads, xs, result)
                result = jnp.where(place == h + 2 * heads, ys, result)
                other = jnp.where(other_place == h, yo, other)
            ef_ref[k, :, lanes] = jnp.sum(
                e2.astype(F32) * f2.astype(F32), axis=0, keepdims=True
            )
            back_ef[k, :, lanes] = jnp.sum(
                e2o.astype(F32) * f2o.astype(F32), axis=0, keepdims=True
            )
            b_sum = b_sum + dot((x2f * (end2 * dt2)).astype(BF16), f2, 1, 1)
            c_sum = c_sum + dot(gs.astype(BF16), e2, 1, 1)
            c_other = c_other + dot(gso.astype(BF16), e2o, 1, 1)
        cols_ref[...] = result
        back[1] = other
        d_scores[...] = q_sum
        d_b[...] = b_sum
        d_c[...] = c_sum
        back[0] = c_other

    def step(t, unused):
        kf = t - z

        @pl.when(jnp.logical_and(kf >= 0, kf < chunks))
        def _():
            pl.when(jnp.logical_not(first))(lambda: copy_e(kf).wait_recv())
            forward(kf)
            pl.when(jnp.logical_not(last))(lambda: copy_e(kf).start())

        kb = t - (nz - 1 - z)

        @pl.when(jnp.logical_and(kb >= 0, kb < chunks))
        def _():
            copy_g(kb).wait_recv()
            pl.when(jnp.logical_not(last))(lambda: copy_f(kb).wait_recv())
            backward(kb)
            pl.when(jnp.logical_not(first))(lambda: copy_f(kb).start())

        pl.when(t >= nz - 1)(lambda: gradients(t - (nz - 1)))
        return unused

    lax.fori_loop(0, chunks + nz - 1, step, 0)
    copy_back().start()
    copy_back_ef().start()
    dk = d_scores[...].astype(BF16)
    gbc_ref[:, :state] = (d_b[...] + dot(dk, c, 1, 0)).astype(gbc_ref.dtype)
    c_total = d_c[...] + dot(dk, b, 0, 0)
    copy_back().wait_recv()
    copy_back_ef().wait_recv()
    gbc_ref[:, state:] = (c_total + back_in[0]).astype(gbc_ref.dtype)
    cols_ref[:, 2 * heads :] += back_in[1, :, :heads]
    ef_ref[...] += back_ef_in[...]
    copy_d().wait_send()
    copy_c().wait_send()
    copy_back().wait_send()
    copy_back_ef().wait_send()

    def settle(k, unused):
        copy_g(k).wait_send()
        pl.when(jnp.logical_not(last))(lambda: copy_e(k).wait_send())
        pl.when(jnp.logical_not(first))(lambda: copy_f(k).wait_send())
        return unused

    lax.fori_loop(0, chunks, settle, 0)


def weight_kernel(
    n, m, t_ref, g_ref, rate_ref, out_ref, rate_out,
    acc, got, ring, r_acc, r_got, sem, out_sem, r_sem,
):
    chunks, blocks, rows = acc.shape[0], acc.shape[1], acc.shape[2]
    piece = chunks * rows
    seq, dp = lax.axis_index("seq"), lax.axis_index("dp")
    dp_steps, seq_steps, bit = [], [], 1
    while bit < m:
        dp_steps.append(("dp", bit, lax.rem(lax.div(dp, bit), 2)))
        bit *= 2
    bit = 1
    while bit < n:
        seq_steps.append(("seq", bit, lax.rem(lax.div(seq, bit), 2)))
        bit *= 2
    count = len(dp_steps) + len(seq_steps)
    orders = (dp_steps + seq_steps, dp_steps[:1] + seq_steps + dp_steps[1:])

    def peer(c, s):
        axis, bit, mine = orders[c % 2][s]
        return {axis: lax.axis_index(axis) + bit - 2 * bit * mine}

    def dp_peer(k):
        other, bit = dp, 1
        while bit < m:
            if k & bit:
                other = other + bit - 2 * bit * lax.rem(lax.div(dp, bit), 2)
            bit *= 2
        return {"dp": other}

    barrier = pltpu.get_barrier_semaphore()
    friends = [dp_peer(k) for k in range(1, m)] + [
        peer(0, s) for s in range(len(dp_steps), count)
    ]
    for friend in friends:
        pl.semaphore_signal(
            barrier, inc=1, device_id=friend, device_id_type=pl.DeviceIdType.MESH
        )

    starts, offsets = [], []
    for order in orders:
        base, width, total = 0, blocks, 0
        starts.append([])
        for unused, unused, mine in order:
            width //= 2
            starts[-1].append((base + width * mine, base + width * (1 - mine), width))
            base = base + width * mine
            if len(starts) == 1:
                offsets.append(total)
                total += width

    def copy(c, s):
        keep, give, size = starts[c % 2][s]
        return pltpu.make_async_remote_copy(
            src_ref=acc.at[c, pl.ds(give, size)],
            dst_ref=got.at[c, pl.ds(offsets[s], size)],
            send_sem=sem.at[0, c, s], recv_sem=sem.at[1, c, s],
            device_id=peer(c, s), device_id_type=pl.DeviceIdType.MESH,
        )

    def rate_copy(s):
        return pltpu.make_async_remote_copy(
            src_ref=r_acc.at[s], dst_ref=r_got.at[s],
            send_sem=r_sem.at[0, s], recv_sem=r_sem.at[1, s],
            device_id=peer(0, s), device_id_type=pl.DeviceIdType.MESH,
        )

    def out_copy(c, k):
        return pltpu.make_async_remote_copy(
            src_ref=ring.at[0, c], dst_ref=ring.at[k, c],
            send_sem=out_sem.at[0, c, k], recv_sem=out_sem.at[1, c, k],
            device_id=dp_peer(k), device_id_type=pl.DeviceIdType.MESH,
        )

    g = g_ref[...]
    r_acc[0] = rate_ref[...]
    block = 128
    for first in range(0, t_ref.shape[1], block):
        product = dot(t_ref[:, first : first + block], g, 0, 0)
        for part in range(0, block, rows):
            row = first + part
            owner, inner = row // (m * piece), row % (m * piece)
            chunk, place = inner % piece // rows, 0
            for axis, bit, unused in orders[chunk % 2]:
                index = inner // piece if axis == "dp" else owner
                place = 2 * place + index // bit % 2
            acc[chunk, place] = product[part : part + rows]
    pl.semaphore_wait(barrier, len(friends))
    for c in range(chunks):
        copy(c, 0).start()
    rate_copy(0).start()
    for s in range(count):
        for c in range(chunks):
            copy(c, s).wait_recv()
            keep, give, size = starts[c % 2][s]
            value = acc[c, pl.ds(keep, size)] + got[c, pl.ds(offsets[s], size)]
            if s + 1 < count:
                acc[c, pl.ds(keep, size)] = value
                copy(c, s + 1).start()
            else:
                ring[0, c] = value[0]
                for k in range(1, m):
                    out_copy(c, k).start()
        rate_copy(s).wait_recv()
        r_acc[s + 1] = r_acc[s] + r_got[s]
        if s + 1 < count:
            rate_copy(s + 1).start()
    rate_out[...] = r_acc[count]
    for c in range(chunks):
        for k in range(m):
            if k > 0:
                out_copy(c, k).wait_recv()
            where = dp_peer(k)["dp"] if k > 0 else dp
            out_ref[pl.ds(where * piece + c * rows, rows)] = ring[k, c]
    for c in range(chunks):
        for s in range(count):
            copy(c, s).wait_send()
        for k in range(1, m):
            out_copy(c, k).wait_send()
    for s in range(count):
        rate_copy(s).wait_send()


def shards(layer_input, projection, ssm_input, step_logit, decay_rate, output_grad):
    tokens, x_rows, logit, grad_rows = layer_input[0], ssm_input[0], step_logit[0], output_grad[0]
    length, full = x_rows.shape
    heads = logit.shape[1]
    size = full // heads
    state = projection.shape[1] // 2
    groups = heads // HEADS
    width = HEADS * size
    count = lax.axis_size("seq")
    projected = jnp.dot(tokens, projection, preferred_element_type=F32).astype(BF16)
    b_rows, c_rows = projected[:, :state], projected[:, state:]
    dt = jax.nn.softplus(logit)
    position = jnp.arange(length)
    until = (position[:, None] >= position[None, :]).astype(F32)
    log_decay = jnp.dot(until, -decay_rate[None, :] * dt, precision=lax.Precision.HIGHEST)
    to_end = jnp.exp(log_decay[-1][None, :] - log_decay)
    grow = jnp.exp(log_decay)
    span = grow[-1]

    def by_group(value):
        return value.reshape(length, groups, HEADS).transpose(1, 0, 2)

    cols = jnp.concatenate([by_group(v) for v in (log_decay, dt, to_end, grow)], axis=2)
    span_rows = jnp.broadcast_to(span[:, None], (heads, size)).reshape(groups, 1, width)
    limit = 60 * 2**20
    vmem = pl.BlockSpec(memory_space=pltpu.VMEM)
    slots = pltpu.VMEM((groups, state, width), F32)
    half = pltpu.VMEM((groups, state, width), BF16)
    square = pltpu.VMEM((length, length), F32)
    sums = pltpu.VMEM((length, state), F32)
    grad_x, row_sums, col_sums, inner, grad_bc = pl.pallas_call(
        functools.partial(layer_kernel, count, size),
        in_specs=[vmem] * 8,
        out_specs=[vmem] * 5,
        out_shape=[
            jax.ShapeDtypeStruct((length, full), BF16),
            jax.ShapeDtypeStruct((groups, HEADS, length), F32),
            jax.ShapeDtypeStruct((length, 3 * heads), F32),
            jax.ShapeDtypeStruct((groups, 1, width), F32),
            jax.ShapeDtypeStruct((length, 2 * state), BF16),
        ],
        scratch_shapes=[half] * 4 + [square, square, sums, sums]
        + [pltpu.VMEM((2, length, state), F32), pltpu.VMEM((groups, 1, width), F32)]
        + [pltpu.VMEM((groups, 1, width), F32), sums, pltpu.VMEM((length, state), BF16)]
        + [pltpu.VMEM((groups, length, width), F32)] * 2
        + [slots] * 4
        + [pltpu.VMEM((2, length, state), F32), pltpu.VMEM((groups, 1, width), F32)]
        + [pltpu.SemaphoreType.DMA((2, 4))]
        + [pltpu.SemaphoreType.DMA((2, groups))] * 3,
        compiler_params=pltpu.CompilerParams(
            collective_id=0, has_side_effects=True, vmem_limit_bytes=limit
        ),
        name="layer_gradients",
    )(
        b_rows, c_rows, c_rows.astype(F32), x_rows, grad_rows, cols,
        log_decay.T.reshape(groups, HEADS, length), span_rows,
    )
    row_sums = row_sums.reshape(heads, length)
    inside, x_in, g_in = (col_sums[:, i * heads : (i + 1) * heads] for i in range(3))
    both = span * jnp.sum(inner.reshape(heads, size), axis=1)
    earlier = (position[:, None] > position[None, :]).astype(F32)
    change = g_in + row_sums.T - dt * inside
    d_log = (
        both[None, :]
        + jnp.dot(earlier, dt * x_in, precision=lax.Precision.HIGHEST)
        + jnp.dot((position[:, None] <= position[None, :]).astype(F32), change, precision=lax.Precision.HIGHEST)
    )
    d_dt = inside + x_in - decay_rate[None, :] * d_log
    grad_logit = d_dt * jax.nn.sigmoid(logit)
    grad_rate = -jnp.sum(dt * d_log, axis=0)
    members = lax.axis_size("dp")
    blocks = count * members
    piece = tokens.shape[1] // blocks
    chunks = max(1, min(8, piece // 8))
    rows = piece // chunks
    levels = blocks.bit_length() - 1
    rate_rows = jnp.pad(grad_rate.reshape(1, heads), ((0, 7), (0, 128 - heads)))
    weight_rows, rate_sum = pl.pallas_call(
        functools.partial(weight_kernel, count, members),
        in_specs=[vmem] * 3,
        out_specs=[vmem] * 2,
        out_shape=[
            jax.ShapeDtypeStruct((members * piece, 2 * state), F32),
            jax.ShapeDtypeStruct((8, 128), F32),
        ],
        scratch_shapes=[
            pltpu.VMEM((chunks, blocks, rows, 2 * state), F32),
            pltpu.VMEM((chunks, blocks, rows, 2 * state), F32),
            pltpu.VMEM((members, chunks, rows, 2 * state), F32),
            pltpu.VMEM((levels + 1, 8, 128), F32),
            pltpu.VMEM((levels, 8, 128), F32),
            pltpu.SemaphoreType.DMA((2, chunks, levels)),
            pltpu.SemaphoreType.DMA((2, chunks, members)),
            pltpu.SemaphoreType.DMA((2, levels)),
        ],
        compiler_params=pltpu.CompilerParams(
            collective_id=1, has_side_effects=True, vmem_limit_bytes=limit
        ),
        name="weight_gradient",
    )(tokens, grad_bc, rate_rows)
    rate_sum = rate_sum[0, :heads]
    return (grad_x[None], grad_logit[None], rate_sum, weight_rows)


def solution(mesh):
    placed = (
        P("dp", "seq", None),
        P(),
        P("dp", "seq", None),
        P("dp", "seq", None),
        P(),
        P("dp", "seq", None),
    )
    return jax.shard_map(
        shards,
        mesh=mesh,
        in_specs=placed,
        out_specs=(P("dp", "seq", None), P("dp", "seq", None), P(), P("seq", None)),
        check_vma=False,
    )
```

```python
import functools

import jax
import jax.numpy as jnp
from jax import lax
from jax.experimental import pallas as pl
from jax.experimental.pallas import tpu as pltpu
from jax.sharding import PartitionSpec as P

F32 = jnp.float32
BF16 = jnp.bfloat16
HEADS = 2
LAG = 3


def dot(a, b, ca, cb):
    return lax.dot_general(a, b, (((ca,), (cb,)), ((), ())), preferred_element_type=F32)


def pair_columns(cols, j, size):
    rows = cols.shape[0]
    lane = lax.broadcasted_iota(jnp.int32, (rows, 2 * size), 1)
    return jnp.where(lane < size, cols[:, j : j + 1], cols[:, j + 1 : j + 2])


def layer_kernel(
    n, size, b_ref, c_ref, cf_ref, x_ref, g_ref, col_ref, row_ref, d_ref,
    dx_ref, rows_ref, cols_ref, ef_ref, gbc_ref,
    e_own, e_other, f_own, f_other, scores, d_scores, d_b, d_c, back, back_ef,
    d_in, cf_in, c_in, gs_snd, gs_in, e_in, f_in, e_snd, f_snd, back_in, back_ef_in,
    small_sem, gs_sem, e_sem, f_sem,
):
    chunks = gs_snd.shape[0]
    length = b_ref.shape[0]
    state = b_ref.shape[1]
    width = 2 * size
    group = HEADS * size
    heads = chunks * HEADS
    nz = n // 2
    me = lax.axis_index("seq")
    odd = lax.rem(me, 2)
    z = lax.div(me, 2)
    partner = me + 1 - 2 * odd
    first, last = z == 0, z == nz - 1
    barrier = pltpu.get_barrier_semaphore()

    def greet(who):
        pl.semaphore_signal(
            barrier, inc=1, device_id={"seq": who}, device_id_type=pl.DeviceIdType.MESH
        )

    greet(partner)
    pl.when(jnp.logical_not(first))(lambda: greet(me - 2))
    pl.when(jnp.logical_not(last))(lambda: greet(me + 2))

    def send(src, dst, sems, k, who):
        return pltpu.make_async_remote_copy(
            src_ref=src, dst_ref=dst, send_sem=sems.at[0, k], recv_sem=sems.at[1, k],
            device_id={"seq": who}, device_id_type=pl.DeviceIdType.MESH,
        )

    def copy_d():
        return send(d_ref, d_in, small_sem, 0, partner)

    def copy_c():
        return send(cf_ref, cf_in, small_sem, 1, partner)

    def copy_back():
        return send(back, back_in, small_sem, 2, partner)

    def copy_back_ef():
        return send(back_ef, back_ef_in, small_sem, 3, partner)

    def copy_g(k):
        return send(gs_snd.at[k], gs_in.at[k], gs_sem, k, partner)

    def copy_e(k):
        return send(e_snd.at[k], e_in.at[k], e_sem, k, me + 2)

    def copy_f(k):
        return send(f_snd.at[k], f_in.at[k], f_sem, k, me - 2)

    def pair_lanes(k, pair):
        return pl.ds(pl.multiple_of(k * group + pair * width, width), width)

    def scale(k, unused):
        cols = col_ref[k]
        for pair in range(HEADS // 2):
            grow = pair_columns(cols, 2 * pair + 3 * HEADS, size)
            gs_snd[k, :, pl.ds(pair * width, width)] = (
                g_ref[:, pair_lanes(k, pair)].astype(F32) * grow
            )
        copy_g(k).start()
        return unused

    end = jnp.logical_or(first, last)
    pl.when(end)(lambda: pl.semaphore_wait(barrier, min(nz, 2)))
    pl.when(jnp.logical_not(end))(lambda: pl.semaphore_wait(barrier, 3))
    copy_d().start()
    copy_c().start()
    lax.fori_loop(0, chunks, scale, 0)

    @pl.when(first)
    def _():
        e_in[...] = jnp.zeros_like(e_in)

    @pl.when(last)
    def _():
        f_in[...] = jnp.zeros_like(f_in)

    b, c = b_ref[...], c_ref[...]
    scores[...] = dot(b, c, 1, 1)
    d_scores[...] = jnp.zeros_like(d_scores)
    d_b[...] = jnp.zeros_like(d_b)
    d_c[...] = jnp.zeros_like(d_c)
    back[...] = jnp.zeros_like(back)
    cols_ref[...] = jnp.zeros_like(cols_ref)
    copy_d().wait_recv()
    copy_c().wait_recv()
    c_in[...] = cf_in[...].astype(BF16)

    def row(ref, k):
        return ref[k]

    def forward(k):
        cols = col_ref[k]
        value = e_in[k]
        parts = []
        for pair in range(HEADS // 2):
            j = 2 * pair
            weight = pair_columns(cols, j + HEADS, size) * pair_columns(cols, j + 2 * HEADS, size)
            parts.append((x_ref[:, pair_lanes(k, pair)].astype(F32) * weight).astype(BF16))
        near = dot(b_ref[...], jnp.concatenate(parts, axis=1), 0, 0)

        @pl.when(odd == 0)
        def _():
            e_own[k] = value.astype(BF16)
            middle = row(d_ref, k) * value + near
            e_other[k] = middle.astype(BF16)
            e_snd[k] = row(d_in, k) * middle

        @pl.when(odd == 1)
        def _():
            e_other[k] = value.astype(BF16)
            middle = row(d_in, k) * value
            e_own[k] = middle.astype(BF16)
            e_snd[k] = row(d_ref, k) * middle + near

    def backward(k):
        value = f_in[k]
        near = dot(c_ref[...], gs_snd[k].astype(BF16), 0, 0)
        far = dot(c_in[...], gs_in[k].astype(BF16), 0, 0)

        @pl.when(odd == 0)
        def _():
            f_other[k] = value.astype(BF16)
            middle = row(d_in, k) * value + far
            f_own[k] = middle.astype(BF16)
            f_snd[k] = row(d_ref, k) * middle + near

        @pl.when(odd == 1)
        def _():
            f_own[k] = value.astype(BF16)
            middle = row(d_ref, k) * value + near
            f_other[k] = middle.astype(BF16)
            f_snd[k] = row(d_in, k) * middle + far

    def gradients(k):
        cols = col_ref[k]
        rows = row_ref[k]
        k_st = scores[...]
        causal = lax.broadcasted_iota(jnp.int32, (length, length), 1) >= lax.broadcasted_iota(
            jnp.int32, (length, length), 0
        )
        low = lax.broadcasted_iota(jnp.int32, (length, width), 1) < size
        place = lax.broadcasted_iota(jnp.int32, cols_ref.shape, 1) - k * HEADS
        other_place = lax.broadcasted_iota(jnp.int32, (length, state), 1) - k * HEADS
        result = cols_ref[...]
        other = back[1]
        q_sum = d_scores[...]
        b_sum, c_sum, c_other = d_b[...], d_c[...], back[0]
        for pair in range(HEADS // 2):
            lanes = pl.ds(pair * width, width)
            wide = pair_lanes(k, pair)
            x2, g2 = x_ref[:, wide], g_ref[:, wide]
            x2f = x2.astype(F32)
            e2, f2 = e_own[k, :, lanes], f_own[k, :, lanes]
            e2o, f2o = e_other[k, :, lanes], f_other[k, :, lanes]
            gs, gso = gs_snd[k, :, lanes], gs_in[k, :, lanes]
            j = 2 * pair
            dt2 = pair_columns(cols, j + HEADS, size)
            end2 = pair_columns(cols, j + 2 * HEADS, size)
            g_low = jnp.where(low, g2, jnp.zeros_like(g2))
            g_high = jnp.where(low, jnp.zeros_like(g2), g2)
            g_both = jnp.concatenate([g_low, g_high], axis=0)
            gram = dot(x2, g_both, 1, 1)
            weights = []
            for side in range(2):
                h = j + side
                gap = rows[h : h + 1, :] - cols[:, h : h + 1]
                decay = jnp.exp(jnp.where(causal, gap, -jnp.inf))
                mg = decay * gram[:, side * length : (side + 1) * length]
                dt = cols[:, h + HEADS : h + HEADS + 1]
                q_sum = q_sum + mg * dt
                raw = mg * k_st
                rows_ref[k, h : h + 1, :] = jnp.sum(raw * dt, axis=0, keepdims=True)
                result = jnp.where(place == h, jnp.sum(raw, axis=1, keepdims=True), result)
                weights.append((decay * k_st).astype(BF16))
            z2 = dot(jnp.concatenate(weights, axis=1), g_both, 1, 0)
            z_in = dot(b, f2, 1, 0) * end2
            dx_ref[:, wide] = (dt2 * (z2 + z_in)).astype(dx_ref.dtype)
            xz = x2f * z_in
            gy = gs * dot(c, e2, 1, 0)
            gyo = gso * dot(c_in[...], e2o, 1, 0)
            zero = jnp.zeros_like(xz)
            for side in range(2):
                h = j + side
                mask = low if side == 0 else jnp.logical_not(low)
                xs = jnp.sum(jnp.where(mask, xz, zero), axis=1, keepdims=True)
                ys = jnp.sum(jnp.where(mask, gy, zero), axis=1, keepdims=True)
                yo = jnp.sum(jnp.where(mask, gyo, zero), axis=1, keepdims=True)
                result = jnp.where(place == h + heads, xs, result)
                result = jnp.where(place == h + 2 * heads, ys, result)
                other = jnp.where(other_place == h, yo, other)
            ef_ref[k, :, lanes] = jnp.sum(
                e2.astype(F32) * f2.astype(F32), axis=0, keepdims=True
            )
            back_ef[k, :, lanes] = jnp.sum(
                e2o.astype(F32) * f2o.astype(F32), axis=0, keepdims=True
            )
            b_sum = b_sum + dot((x2f * (end2 * dt2)).astype(BF16), f2, 1, 1)
            c_sum = c_sum + dot(gs.astype(BF16), e2, 1, 1)
            c_other = c_other + dot(gso.astype(BF16), e2o, 1, 1)
        cols_ref[...] = result
        back[1] = other
        d_scores[...] = q_sum
        d_b[...] = b_sum
        d_c[...] = c_sum
        back[0] = c_other

    def step(t, unused):
        kf = t - LAG * z

        @pl.when(jnp.logical_and(kf >= 0, kf < chunks))
        def _():
            pl.when(jnp.logical_not(first))(lambda: copy_e(kf).wait_recv())
            forward(kf)
            pl.when(jnp.logical_not(last))(lambda: copy_e(kf).start())

        kb = t - LAG * (nz - 1 - z)

        @pl.when(jnp.logical_and(kb >= 0, kb < chunks))
        def _():
            copy_g(kb).wait_recv()
            pl.when(jnp.logical_not(last))(lambda: copy_f(kb).wait_recv())
            backward(kb)
            pl.when(jnp.logical_not(first))(lambda: copy_f(kb).start())

        kg = t - delay
        pl.when(jnp.logical_and(kg >= 0, kg < chunks))(lambda: gradients(kg))
        return unused

    delay = LAG * lax.max(z, nz - 1 - z)
    lax.fori_loop(0, chunks + delay, step, 0)
    copy_back().start()
    copy_back_ef().start()
    dk = d_scores[...].astype(BF16)
    gbc_ref[:, :state] = (d_b[...] + dot(dk, c, 1, 0)).astype(gbc_ref.dtype)
    c_total = d_c[...] + dot(dk, b, 0, 0)
    copy_back().wait_recv()
    copy_back_ef().wait_recv()
    gbc_ref[:, state:] = (c_total + back_in[0]).astype(gbc_ref.dtype)
    cols_ref[:, 2 * heads :] += back_in[1, :, :heads]
    ef_ref[...] += back_ef_in[...]
    copy_d().wait_send()
    copy_c().wait_send()
    copy_back().wait_send()
    copy_back_ef().wait_send()

    def settle(k, unused):
        copy_g(k).wait_send()
        pl.when(jnp.logical_not(last))(lambda: copy_e(k).wait_send())
        pl.when(jnp.logical_not(first))(lambda: copy_f(k).wait_send())
        return unused

    lax.fori_loop(0, chunks, settle, 0)


def weight_kernel(
    n, m, t_ref, g_ref, rate_ref, out_ref, rate_out,
    acc, got, ring, r_acc, r_got, sem, out_sem, r_sem,
):
    chunks, blocks, rows = acc.shape[0], acc.shape[1], acc.shape[2]
    piece = chunks * rows
    seq, dp = lax.axis_index("seq"), lax.axis_index("dp")
    dp_steps, seq_steps, bit = [], [], 1
    while bit < m:
        dp_steps.append(("dp", bit, lax.rem(lax.div(dp, bit), 2)))
        bit *= 2
    bit = 1
    while bit < n:
        seq_steps.append(("seq", bit, lax.rem(lax.div(seq, bit), 2)))
        bit *= 2
    count = len(dp_steps) + len(seq_steps)
    orders = (dp_steps + seq_steps, dp_steps[:1] + seq_steps + dp_steps[1:])

    def peer(c, s):
        axis, bit, mine = orders[c % 2][s]
        return {axis: lax.axis_index(axis) + bit - 2 * bit * mine}

    def dp_peer(k):
        other, bit = dp, 1
        while bit < m:
            if k & bit:
                other = other + bit - 2 * bit * lax.rem(lax.div(dp, bit), 2)
            bit *= 2
        return {"dp": other}

    barrier = pltpu.get_barrier_semaphore()
    friends = [dp_peer(k) for k in range(1, m)] + [
        peer(0, s) for s in range(len(dp_steps), count)
    ]
    for friend in friends:
        pl.semaphore_signal(
            barrier, inc=1, device_id=friend, device_id_type=pl.DeviceIdType.MESH
        )

    starts, offsets = [], []
    for order in orders:
        base, width, total = 0, blocks, 0
        starts.append([])
        for unused, unused, mine in order:
            width //= 2
            starts[-1].append((base + width * mine, base + width * (1 - mine), width))
            base = base + width * mine
            if len(starts) == 1:
                offsets.append(total)
                total += width

    def copy(c, s):
        keep, give, size = starts[c % 2][s]
        return pltpu.make_async_remote_copy(
            src_ref=acc.at[c, pl.ds(give, size)],
            dst_ref=got.at[c, pl.ds(offsets[s], size)],
            send_sem=sem.at[0, c, s], recv_sem=sem.at[1, c, s],
            device_id=peer(c, s), device_id_type=pl.DeviceIdType.MESH,
        )

    def rate_copy(s):
        return pltpu.make_async_remote_copy(
            src_ref=r_acc.at[s], dst_ref=r_got.at[s],
            send_sem=r_sem.at[0, s], recv_sem=r_sem.at[1, s],
            device_id=peer(0, s), device_id_type=pl.DeviceIdType.MESH,
        )

    def out_copy(c, k):
        return pltpu.make_async_remote_copy(
            src_ref=ring.at[0, c], dst_ref=ring.at[k, c],
            send_sem=out_sem.at[0, c, k], recv_sem=out_sem.at[1, c, k],
            device_id=dp_peer(k), device_id_type=pl.DeviceIdType.MESH,
        )

    g = g_ref[...]
    r_acc[0] = rate_ref[...]
    block = 128
    for first in range(0, t_ref.shape[1], block):
        product = dot(t_ref[:, first : first + block], g, 0, 0)
        for part in range(0, block, rows):
            row = first + part
            owner, inner = row // (m * piece), row % (m * piece)
            chunk, place = inner % piece // rows, 0
            for axis, bit, unused in orders[chunk % 2]:
                index = inner // piece if axis == "dp" else owner
                place = 2 * place + index // bit % 2
            acc[chunk, place] = product[part : part + rows]
    pl.semaphore_wait(barrier, len(friends))
    for c in range(chunks):
        copy(c, 0).start()
    rate_copy(0).start()
    for s in range(count):
        for c in range(chunks):
            copy(c, s).wait_recv()
            keep, give, size = starts[c % 2][s]
            value = acc[c, pl.ds(keep, size)] + got[c, pl.ds(offsets[s], size)]
            if s + 1 < count:
                acc[c, pl.ds(keep, size)] = value
                copy(c, s + 1).start()
            else:
                ring[0, c] = value[0]
                for k in range(1, m):
                    out_copy(c, k).start()
        rate_copy(s).wait_recv()
        r_acc[s + 1] = r_acc[s] + r_got[s]
        if s + 1 < count:
            rate_copy(s + 1).start()
    rate_out[...] = r_acc[count]
    for c in range(chunks):
        for k in range(m):
            if k > 0:
                out_copy(c, k).wait_recv()
            where = dp_peer(k)["dp"] if k > 0 else dp
            out_ref[pl.ds(where * piece + c * rows, rows)] = ring[k, c]
    for c in range(chunks):
        for s in range(count):
            copy(c, s).wait_send()
        for k in range(1, m):
            out_copy(c, k).wait_send()
    for s in range(count):
        rate_copy(s).wait_send()


def shards(layer_input, projection, ssm_input, step_logit, decay_rate, output_grad):
    tokens, x_rows, logit, grad_rows = layer_input[0], ssm_input[0], step_logit[0], output_grad[0]
    length, full = x_rows.shape
    heads = logit.shape[1]
    size = full // heads
    state = projection.shape[1] // 2
    groups = heads // HEADS
    width = HEADS * size
    count = lax.axis_size("seq")
    projected = jnp.dot(tokens, projection, preferred_element_type=F32).astype(BF16)
    b_rows, c_rows = projected[:, :state], projected[:, state:]
    dt = jax.nn.softplus(logit)
    position = jnp.arange(length)
    until = (position[:, None] >= position[None, :]).astype(F32)
    log_decay = jnp.dot(until, -decay_rate[None, :] * dt, precision=lax.Precision.HIGHEST)
    to_end = jnp.exp(log_decay[-1][None, :] - log_decay)
    grow = jnp.exp(log_decay)
    span = grow[-1]

    def by_group(value):
        return value.reshape(length, groups, HEADS).transpose(1, 0, 2)

    cols = jnp.concatenate([by_group(v) for v in (log_decay, dt, to_end, grow)], axis=2)
    span_rows = jnp.broadcast_to(span[:, None], (heads, size)).reshape(groups, 1, width)
    limit = 60 * 2**20
    vmem = pl.BlockSpec(memory_space=pltpu.VMEM)
    slots = pltpu.VMEM((groups, state, width), F32)
    half = pltpu.VMEM((groups, state, width), BF16)
    square = pltpu.VMEM((length, length), F32)
    sums = pltpu.VMEM((length, state), F32)
    grad_x, row_sums, col_sums, inner, grad_bc = pl.pallas_call(
        functools.partial(layer_kernel, count, size),
        in_specs=[vmem] * 8,
        out_specs=[vmem] * 5,
        out_shape=[
            jax.ShapeDtypeStruct((length, full), BF16),
            jax.ShapeDtypeStruct((groups, HEADS, length), F32),
            jax.ShapeDtypeStruct((length, 3 * heads), F32),
            jax.ShapeDtypeStruct((groups, 1, width), F32),
            jax.ShapeDtypeStruct((length, 2 * state), BF16),
        ],
        scratch_shapes=[half] * 4 + [square, square, sums, sums]
        + [pltpu.VMEM((2, length, state), F32), pltpu.VMEM((groups, 1, width), F32)]
        + [pltpu.VMEM((groups, 1, width), F32), sums, pltpu.VMEM((length, state), BF16)]
        + [pltpu.VMEM((groups, length, width), F32)] * 2
        + [slots] * 4
        + [pltpu.VMEM((2, length, state), F32), pltpu.VMEM((groups, 1, width), F32)]
        + [pltpu.SemaphoreType.DMA((2, 4))]
        + [pltpu.SemaphoreType.DMA((2, groups))] * 3,
        compiler_params=pltpu.CompilerParams(
            collective_id=0, has_side_effects=True, vmem_limit_bytes=limit
        ),
        name="layer_gradients",
    )(
        b_rows, c_rows, c_rows.astype(F32), x_rows, grad_rows, cols,
        log_decay.T.reshape(groups, HEADS, length), span_rows,
    )
    row_sums = row_sums.reshape(heads, length)
    inside, x_in, g_in = (col_sums[:, i * heads : (i + 1) * heads] for i in range(3))
    both = span * jnp.sum(inner.reshape(heads, size), axis=1)
    earlier = (position[:, None] > position[None, :]).astype(F32)
    change = g_in + row_sums.T - dt * inside
    d_log = (
        both[None, :]
        + jnp.dot(earlier, dt * x_in, precision=lax.Precision.HIGHEST)
        + jnp.dot((position[:, None] <= position[None, :]).astype(F32), change, precision=lax.Precision.HIGHEST)
    )
    d_dt = inside + x_in - decay_rate[None, :] * d_log
    grad_logit = d_dt * jax.nn.sigmoid(logit)
    grad_rate = -jnp.sum(dt * d_log, axis=0)
    members = lax.axis_size("dp")
    blocks = count * members
    piece = tokens.shape[1] // blocks
    chunks = max(1, min(8, piece // 8))
    rows = piece // chunks
    levels = blocks.bit_length() - 1
    rate_rows = jnp.pad(grad_rate.reshape(1, heads), ((0, 7), (0, 128 - heads)))
    weight_rows, rate_sum = pl.pallas_call(
        functools.partial(weight_kernel, count, members),
        in_specs=[vmem] * 3,
        out_specs=[vmem] * 2,
        out_shape=[
            jax.ShapeDtypeStruct((members * piece, 2 * state), F32),
            jax.ShapeDtypeStruct((8, 128), F32),
        ],
        scratch_shapes=[
            pltpu.VMEM((chunks, blocks, rows, 2 * state), F32),
            pltpu.VMEM((chunks, blocks, rows, 2 * state), F32),
            pltpu.VMEM((members, chunks, rows, 2 * state), F32),
            pltpu.VMEM((levels + 1, 8, 128), F32),
            pltpu.VMEM((levels, 8, 128), F32),
            pltpu.SemaphoreType.DMA((2, chunks, levels)),
            pltpu.SemaphoreType.DMA((2, chunks, members)),
            pltpu.SemaphoreType.DMA((2, levels)),
        ],
        compiler_params=pltpu.CompilerParams(
            collective_id=1, has_side_effects=True, vmem_limit_bytes=limit
        ),
        name="weight_gradient",
    )(tokens, grad_bc, rate_rows)
    rate_sum = rate_sum[0, :heads]
    return (grad_x[None], grad_logit[None], rate_sum, weight_rows)


def solution(mesh):
    placed = (
        P("dp", "seq", None),
        P(),
        P("dp", "seq", None),
        P("dp", "seq", None),
        P(),
        P("dp", "seq", None),
    )
    return jax.shard_map(
        shards,
        mesh=mesh,
        in_specs=placed,
        out_specs=(P("dp", "seq", None), P("dp", "seq", None), P(), P("seq", None)),
        check_vma=False,
    )
```

```python
import functools

import jax
import jax.numpy as jnp
from jax import lax
from jax.experimental import pallas as pl
from jax.experimental.pallas import tpu as pltpu
from jax.sharding import PartitionSpec as P

F32 = jnp.float32
BF16 = jnp.bfloat16
HEADS = 2
LAG = 3
EARLY = 3


def dot(a, b, ca, cb):
    return lax.dot_general(a, b, (((ca,), (cb,)), ((), ())), preferred_element_type=F32)


def exact_dot(a, b, ca, cb):
    return lax.dot_general(
        a, b, (((ca,), (cb,)), ((), ())),
        preferred_element_type=F32, precision=lax.Precision.HIGHEST,
    )


def pair_columns(cols, j, size):
    lane = lax.broadcasted_iota(jnp.int32, (cols.shape[0], 2 * size), 1)
    return jnp.where(lane < size, cols[:, j : j + 1], cols[:, j + 1 : j + 2])


def layer_kernel(
    n, size, t_ref, w_ref, x_ref, g_ref, logit_ref, rate_ref,
    dx_ref, dlogit_ref, drate_ref, gbc_ref,
    b_ref, c_ref, c_in, cols1, cols2, rows_ref, span, span_in, cf, cf_in,
    e_own, e_other, f_own, f_other, scores, d_scores, d_b, d_c,
    sums1, sums2, row_sums, back, back_in,
    gs_snd, gs_in, e_in, f_in, e_snd, f_snd,
    small_sem, gs_sem, e_sem, f_sem,
):
    chunks = gs_snd.shape[0]
    length, state = b_ref.shape
    heads = logit_ref.shape[1]
    width = HEADS * size
    nz = n // 2
    me = lax.axis_index("seq")
    odd = lax.rem(me, 2)
    z = lax.div(me, 2)
    partner = me + 1 - 2 * odd
    first, last = z == 0, z == nz - 1
    barrier = pltpu.get_barrier_semaphore()

    def greet(who):
        pl.semaphore_signal(
            barrier, inc=1, device_id={"seq": who}, device_id_type=pl.DeviceIdType.MESH
        )

    greet(partner)
    pl.when(jnp.logical_not(first))(lambda: greet(me - 2))
    pl.when(jnp.logical_not(last))(lambda: greet(me + 2))

    def send(src, dst, sems, k, who):
        return pltpu.make_async_remote_copy(
            src_ref=src, dst_ref=dst, send_sem=sems.at[0, k], recv_sem=sems.at[1, k],
            device_id={"seq": who}, device_id_type=pl.DeviceIdType.MESH,
        )

    def copy_span():
        return send(span, span_in, small_sem, 0, partner)

    def copy_c():
        return send(cf, cf_in, small_sem, 1, partner)

    def copy_back(i):
        return send(back.at[i], back_in.at[i], small_sem, 2 + i, partner)

    def copy_g(k):
        return send(gs_snd.at[k], gs_in.at[k], gs_sem, k, partner)

    def copy_e(k):
        return send(e_snd.at[k], e_in.at[k], e_sem, k, me + 2)

    def copy_f(k):
        return send(f_snd.at[k], f_in.at[k], f_sem, k, me - 2)

    def turn(value, k):
        lanes = value.shape[1]
        return pltpu.roll(value, lax.rem(lanes - HEADS * k, lanes), 1)

    def wide(k):
        return pl.ds(pl.multiple_of(k * width, width), width)

    logit, rate = logit_ref[...], rate_ref[...]
    dt_all = jnp.maximum(logit, 0.0) + jnp.log1p(jnp.exp(-jnp.abs(logit)))
    row_at = lax.broadcasted_iota(jnp.int32, (length, length), 0)
    col_at = lax.broadcasted_iota(jnp.int32, (length, length), 1)
    until = (row_at >= col_at).astype(F32)
    log_decay = exact_dot(until, -rate * dt_all, 1, 0)
    to_end = jnp.exp(log_decay[length - 1 : length, :] - log_decay)
    grow_all = jnp.exp(log_decay)
    q1 = jnp.concatenate([log_decay, dt_all], axis=1)
    q2 = jnp.concatenate([to_end, grow_all], axis=1)
    span[...] = jnp.broadcast_to(q2[length - 1 : length, :], span.shape)
    by_head = q1.T
    for k in range(chunks):
        rows_ref[k] = by_head[HEADS * k : HEADS * (k + 1), :]

    def scale(k, unused):
        cols1[k] = turn(q1, k)
        cols = turn(q2, k)
        cols2[k] = cols
        gs_snd[k] = g_ref[:, wide(k)].astype(F32) * pair_columns(cols, heads, size)
        copy_g(k).start()
        return unused

    end = jnp.logical_or(first, last)
    pl.when(end)(lambda: pl.semaphore_wait(barrier, min(nz, 2)))
    pl.when(jnp.logical_not(end))(lambda: pl.semaphore_wait(barrier, 3))
    copy_span().start()
    lax.fori_loop(0, EARLY, scale, 0)
    bc = dot(t_ref[...], w_ref[...], 1, 0).astype(BF16)
    b_ref[...] = bc[:, :state]
    c_ref[...] = bc[:, state:]
    cf[...] = bc[:, state:].astype(F32)
    copy_c().start()
    lax.fori_loop(EARLY, chunks, scale, 0)

    @pl.when(first)
    def _():
        e_in[...] = jnp.zeros_like(e_in)

    @pl.when(last)
    def _():
        f_in[...] = jnp.zeros_like(f_in)

    scores[...] = dot(b_ref[...], c_ref[...], 1, 1)
    for ref in (d_scores, d_b, d_c, sums1, sums2, row_sums, back):
        ref[...] = jnp.zeros_like(ref)
    copy_span().wait_recv()
    copy_c().wait_recv()
    c_in[...] = cf_in[...].astype(BF16)

    def spans(ref, k):
        return pair_columns(turn(ref[...], k)[:1, :], heads, size)

    def forward(k):
        value = e_in[k]
        weight = pair_columns(cols1[k], heads, size) * pair_columns(cols2[k], 0, size)
        near = dot(b_ref[...], (x_ref[:, wide(k)].astype(F32) * weight).astype(BF16), 0, 0)
        mine, theirs = spans(span, k), spans(span_in, k)

        @pl.when(odd == 0)
        def _():
            e_own[k] = value.astype(BF16)
            middle = mine * value + near
            e_other[k] = middle.astype(BF16)
            e_snd[k] = theirs * middle

        @pl.when(odd == 1)
        def _():
            e_other[k] = value.astype(BF16)
            middle = theirs * value
            e_own[k] = middle.astype(BF16)
            e_snd[k] = mine * middle + near

    def backward(k):
        value = f_in[k]
        near = dot(c_ref[...], gs_snd[k].astype(BF16), 0, 0)
        far = dot(c_in[...], gs_in[k].astype(BF16), 0, 0)
        mine, theirs = spans(span, k), spans(span_in, k)

        @pl.when(odd == 0)
        def _():
            f_other[k] = value.astype(BF16)
            middle = theirs * value + far
            f_own[k] = middle.astype(BF16)
            f_snd[k] = mine * middle + near

        @pl.when(odd == 1)
        def _():
            f_own[k] = value.astype(BF16)
            middle = mine * value + near
            f_other[k] = middle.astype(BF16)
            f_snd[k] = theirs * middle + far

    def gradients(k):
        cols, rows = cols1[k], rows_ref[k]
        k_st = scores[...]
        causal = col_at >= row_at
        low = lax.broadcasted_iota(jnp.int32, (length, width), 1) < size
        place = lax.broadcasted_iota(jnp.int32, sums1.shape, 1) - k * HEADS
        row_place = lax.broadcasted_iota(jnp.int32, row_sums.shape, 0) - k * HEADS
        res1, res2, res3, res_rows = sums1[...], sums2[...], back[1], row_sums[...]
        q_sum = d_scores[...]
        x2, g2 = x_ref[:, wide(k)], g_ref[:, wide(k)]
        x2f = x2.astype(F32)
        e2, f2, e3, f3 = e_own[k], f_own[k], e_other[k], f_other[k]
        gs, gs3 = gs_snd[k], gs_in[k]
        dt2 = pair_columns(cols, heads, size)
        end2 = pair_columns(cols2[k], 0, size)
        g_low = jnp.where(low, g2, jnp.zeros_like(g2))
        g_high = jnp.where(low, jnp.zeros_like(g2), g2)
        g_both = jnp.concatenate([g_low, g_high], axis=0)
        gram = dot(x2, g_both, 1, 1)
        weights = []
        for h in range(HEADS):
            gap = rows[h : h + 1, :] - cols[:, h : h + 1]
            decay = jnp.exp(jnp.where(causal, gap, -jnp.inf))
            mg = decay * gram[:, h * length : (h + 1) * length]
            dt = cols[:, heads + h : heads + h + 1]
            q_sum = q_sum + mg * dt
            raw = mg * k_st
            res_rows = jnp.where(row_place == h, jnp.sum(raw * dt, axis=0, keepdims=True), res_rows)
            res1 = jnp.where(place == h, jnp.sum(raw, axis=1, keepdims=True), res1)
            weights.append((decay * k_st).astype(BF16))
        z2 = dot(jnp.concatenate(weights, axis=1), g_both, 1, 0)
        z_in = dot(b_ref[...], f2, 1, 0) * end2
        dx_ref[:, wide(k)] = (dt2 * (z2 + z_in)).astype(dx_ref.dtype)
        xz = x2f * z_in
        gy = gs * dot(c_ref[...], e2, 1, 0)
        gy3 = gs3 * dot(c_in[...], e3, 1, 0)
        ef = jnp.sum(e2.astype(F32) * f2.astype(F32), axis=0, keepdims=True)
        ef3 = jnp.sum(e3.astype(F32) * f3.astype(F32), axis=0, keepdims=True)
        low_row = low[:1, :]

        def half(value, h, mask):
            keep = mask if h == 0 else jnp.logical_not(mask)
            return jnp.sum(jnp.where(keep, value, jnp.zeros_like(value)), axis=1, keepdims=True)

        for h in range(HEADS):
            res1 = jnp.where(place == h + heads, half(xz, h, low), res1)
            res2 = jnp.where(place == h, half(gy, h, low), res2)
            res2 = jnp.where(place == h + heads, half(ef, h, low_row), res2)
            res3 = jnp.where(place == h, half(gy3, h, low), res3)
            res3 = jnp.where(place == h + heads, half(ef3, h, low_row), res3)
        sums1[...] = res1
        sums2[...] = res2
        back[1] = res3
        row_sums[...] = res_rows
        d_scores[...] = q_sum
        d_b[...] += dot((x2f * (end2 * dt2)).astype(BF16), f2, 1, 1)
        d_c[...] += dot(gs.astype(BF16), e2, 1, 1)
        back[0] += dot(gs3.astype(BF16), e3, 1, 1)

    delay = LAG * lax.max(z, nz - 1 - z)

    def step(t, unused):
        kf = t - LAG * z

        @pl.when(jnp.logical_and(kf >= 0, kf < chunks))
        def _():
            pl.when(jnp.logical_not(first))(lambda: copy_e(kf).wait_recv())
            forward(kf)
            pl.when(jnp.logical_not(last))(lambda: copy_e(kf).start())

        kb = t - LAG * (nz - 1 - z)

        @pl.when(jnp.logical_and(kb >= 0, kb < chunks))
        def _():
            copy_g(kb).wait_recv()
            pl.when(jnp.logical_not(last))(lambda: copy_f(kb).wait_recv())
            backward(kb)
            pl.when(jnp.logical_not(first))(lambda: copy_f(kb).start())

        kg = t - delay
        pl.when(jnp.logical_and(kg >= 0, kg < chunks))(lambda: gradients(kg))
        return unused

    lax.fori_loop(0, chunks + delay, step, 0)
    copy_back(0).start()
    copy_back(1).start()
    dk = d_scores[...].astype(BF16)
    gbc_ref[:, :state] = (d_b[...] + dot(dk, c_ref[...], 1, 0)).astype(gbc_ref.dtype)
    c_total = d_c[...] + dot(dk, b_ref[...], 0, 0)
    copy_back(0).wait_recv()
    gbc_ref[:, state:] = (c_total + back_in[0]).astype(gbc_ref.dtype)
    copy_back(1).wait_recv()
    total = sums2[...] + back_in[1]
    inside, x_in = sums1[:, :heads], sums1[:, heads:]
    g_in, both = total[:, :heads], span[:1, heads:] * total[:, heads:]
    dt_all = cols1[0, :, heads:]
    after = (row_at <= col_at).astype(F32)
    before = (row_at > col_at).astype(F32)
    d_log = (
        both
        + exact_dot(before, dt_all * x_in, 1, 0)
        + exact_dot(after, g_in - dt_all * inside, 1, 0)
        + exact_dot(after, row_sums[...], 1, 1)
    )
    dlogit_ref[...] = (inside + x_in - rate * d_log) * jax.nn.sigmoid(logit_ref[...])
    d_rate = -jnp.sum(dt_all * d_log, axis=0, keepdims=True)
    drate_ref[...] = jnp.broadcast_to(
        jnp.concatenate([d_rate, jnp.zeros_like(d_rate)], axis=1), drate_ref.shape
    )
    copy_span().wait_send()
    copy_c().wait_send()
    copy_back(0).wait_send()
    copy_back(1).wait_send()

    def settle(k, unused):
        copy_g(k).wait_send()
        pl.when(jnp.logical_not(last))(lambda: copy_e(k).wait_send())
        pl.when(jnp.logical_not(first))(lambda: copy_f(k).wait_send())
        return unused

    lax.fori_loop(0, chunks, settle, 0)


def weight_kernel(
    n, m, t_ref, g_ref, rate_ref, out_ref, rate_out,
    acc, got, ring, r_acc, r_got, sem, out_sem, r_sem,
):
    chunks, blocks, rows = acc.shape[0], acc.shape[1], acc.shape[2]
    piece = chunks * rows
    seq, dp = lax.axis_index("seq"), lax.axis_index("dp")
    dp_steps, seq_steps, bit = [], [], 1
    while bit < m:
        dp_steps.append(("dp", bit, lax.rem(lax.div(dp, bit), 2)))
        bit *= 2
    bit = 1
    while bit < n:
        seq_steps.append(("seq", bit, lax.rem(lax.div(seq, bit), 2)))
        bit *= 2
    count = len(dp_steps) + len(seq_steps)
    orders = (dp_steps + seq_steps, dp_steps[:1] + seq_steps + dp_steps[1:])

    def peer(c, s):
        axis, bit, mine = orders[c % 2][s]
        return {axis: lax.axis_index(axis) + bit - 2 * bit * mine}

    def dp_peer(k):
        other, bit = dp, 1
        while bit < m:
            if k & bit:
                other = other + bit - 2 * bit * lax.rem(lax.div(dp, bit), 2)
            bit *= 2
        return {"dp": other}

    barrier = pltpu.get_barrier_semaphore()
    friends = [dp_peer(k) for k in range(1, m)] + [
        peer(0, s) for s in range(len(dp_steps), count)
    ]
    for friend in friends:
        pl.semaphore_signal(
            barrier, inc=1, device_id=friend, device_id_type=pl.DeviceIdType.MESH
        )

    starts, offsets = [], []
    for order in orders:
        base, width, total = 0, blocks, 0
        starts.append([])
        for unused, unused, mine in order:
            width //= 2
            starts[-1].append((base + width * mine, base + width * (1 - mine), width))
            base = base + width * mine
            if len(starts) == 1:
                offsets.append(total)
                total += width

    def copy(c, s):
        keep, give, size = starts[c % 2][s]
        return pltpu.make_async_remote_copy(
            src_ref=acc.at[c, pl.ds(give, size)],
            dst_ref=got.at[c, pl.ds(offsets[s], size)],
            send_sem=sem.at[0, c, s], recv_sem=sem.at[1, c, s],
            device_id=peer(c, s), device_id_type=pl.DeviceIdType.MESH,
        )

    def rate_copy(s):
        return pltpu.make_async_remote_copy(
            src_ref=r_acc.at[s], dst_ref=r_got.at[s],
            send_sem=r_sem.at[0, s], recv_sem=r_sem.at[1, s],
            device_id=peer(0, s), device_id_type=pl.DeviceIdType.MESH,
        )

    def out_copy(c, k):
        return pltpu.make_async_remote_copy(
            src_ref=ring.at[0, c], dst_ref=ring.at[k, c],
            send_sem=out_sem.at[0, c, k], recv_sem=out_sem.at[1, c, k],
            device_id=dp_peer(k), device_id_type=pl.DeviceIdType.MESH,
        )

    g = g_ref[...]
    r_acc[0] = rate_ref[...]
    block = 128
    for first in range(0, t_ref.shape[1], block):
        product = dot(t_ref[:, first : first + block], g, 0, 0)
        for part in range(0, block, rows):
            row = first + part
            owner, inner = row // (m * piece), row % (m * piece)
            chunk, place = inner % piece // rows, 0
            for axis, bit, unused in orders[chunk % 2]:
                index = inner // piece if axis == "dp" else owner
                place = 2 * place + index // bit % 2
            acc[chunk, place] = product[part : part + rows]
    pl.semaphore_wait(barrier, len(friends))
    for c in range(chunks):
        copy(c, 0).start()
    rate_copy(0).start()
    for s in range(count):
        for c in range(chunks):
            copy(c, s).wait_recv()
            keep, give, size = starts[c % 2][s]
            value = acc[c, pl.ds(keep, size)] + got[c, pl.ds(offsets[s], size)]
            if s + 1 < count:
                acc[c, pl.ds(keep, size)] = value
                copy(c, s + 1).start()
            else:
                ring[0, c] = value[0]
                for k in range(1, m):
                    out_copy(c, k).start()
        rate_copy(s).wait_recv()
        r_acc[s + 1] = r_acc[s] + r_got[s]
        if s + 1 < count:
            rate_copy(s + 1).start()
    rate_out[...] = r_acc[count]
    for c in range(chunks):
        for k in range(m):
            if k > 0:
                out_copy(c, k).wait_recv()
            where = dp_peer(k)["dp"] if k > 0 else dp
            out_ref[pl.ds(where * piece + c * rows, rows)] = ring[k, c]
    for c in range(chunks):
        for s in range(count):
            copy(c, s).wait_send()
        for k in range(1, m):
            out_copy(c, k).wait_send()
    for s in range(count):
        rate_copy(s).wait_send()


def shards(layer_input, projection, ssm_input, step_logit, decay_rate, output_grad):
    tokens, x_rows, logit, grad_rows = layer_input[0], ssm_input[0], step_logit[0], output_grad[0]
    length, full = x_rows.shape
    heads = logit.shape[1]
    size = full // heads
    state = projection.shape[1] // 2
    groups = heads // HEADS
    width = HEADS * size
    count = lax.axis_size("seq")
    limit = 60 * 2**20
    vmem = pl.BlockSpec(memory_space=pltpu.VMEM)
    slots = pltpu.VMEM((groups, state, width), F32)
    rows_in = pltpu.VMEM((groups, length, width), F32)
    half = pltpu.VMEM((groups, state, width), BF16)
    square = pltpu.VMEM((length, length), F32)
    sums = pltpu.VMEM((length, state), F32)
    short = pltpu.VMEM((length, state), BF16)
    by_lane = pltpu.VMEM((length, 2 * heads), F32)
    cols = pltpu.VMEM((groups, length, 2 * heads), F32)
    strip = pltpu.VMEM((8, 2 * heads), F32)
    two = pltpu.VMEM((2, length, state), F32)
    grad_x, grad_logit, rate_rows, grad_bc = pl.pallas_call(
        functools.partial(layer_kernel, count, size),
        in_specs=[vmem] * 6,
        out_specs=[vmem] * 4,
        out_shape=[
            jax.ShapeDtypeStruct((length, full), BF16),
            jax.ShapeDtypeStruct((length, heads), F32),
            jax.ShapeDtypeStruct((8, 2 * heads), F32),
            jax.ShapeDtypeStruct((length, 2 * state), BF16),
        ],
        scratch_shapes=[short] * 3
        + [cols] * 2
        + [pltpu.VMEM((groups, HEADS, length), F32), strip, strip, sums, sums]
        + [half] * 4
        + [square, square, sums, sums]
        + [by_lane, by_lane, pltpu.VMEM((heads, length), F32), two, two]
        + [rows_in] * 2
        + [slots] * 4
        + [pltpu.SemaphoreType.DMA((2, 4))]
        + [pltpu.SemaphoreType.DMA((2, groups))] * 3,
        compiler_params=pltpu.CompilerParams(
            collective_id=0, has_side_effects=True, vmem_limit_bytes=limit
        ),
        name="layer_gradients",
    )(tokens, projection, x_rows, grad_rows, logit, decay_rate[None, :])
    members = lax.axis_size("dp")
    blocks = count * members
    piece = tokens.shape[1] // blocks
    chunks = max(1, min(8, piece // 8))
    rows = piece // chunks
    levels = blocks.bit_length() - 1
    weight_rows, rate_sum = pl.pallas_call(
        functools.partial(weight_kernel, count, members),
        in_specs=[vmem] * 3,
        out_specs=[vmem] * 2,
        out_shape=[
            jax.ShapeDtypeStruct((members * piece, 2 * state), F32),
            jax.ShapeDtypeStruct((8, 128), F32),
        ],
        scratch_shapes=[
            pltpu.VMEM((chunks, blocks, rows, 2 * state), F32),
            pltpu.VMEM((chunks, blocks, rows, 2 * state), F32),
            pltpu.VMEM((members, chunks, rows, 2 * state), F32),
            pltpu.VMEM((levels + 1, 8, 128), F32),
            pltpu.VMEM((levels, 8, 128), F32),
            pltpu.SemaphoreType.DMA((2, chunks, levels)),
            pltpu.SemaphoreType.DMA((2, chunks, members)),
            pltpu.SemaphoreType.DMA((2, levels)),
        ],
        compiler_params=pltpu.CompilerParams(
            collective_id=1, has_side_effects=True, vmem_limit_bytes=limit
        ),
        name="weight_gradient",
    )(tokens, grad_bc, rate_rows)
    rate_sum = rate_sum[0, :heads]
    return (grad_x[None], grad_logit[None], rate_sum, weight_rows)


def solution(mesh):
    placed = (
        P("dp", "seq", None),
        P(),
        P("dp", "seq", None),
        P("dp", "seq", None),
        P(),
        P("dp", "seq", None),
    )
    return jax.shard_map(
        shards,
        mesh=mesh,
        in_specs=placed,
        out_specs=(P("dp", "seq", None), P("dp", "seq", None), P(), P("seq", None)),
        check_vma=False,
    )
```

```python
import functools

import jax
import jax.numpy as jnp
from jax import lax
from jax.experimental import pallas as pl
from jax.experimental.pallas import tpu as pltpu
from jax.sharding import PartitionSpec as P

F32 = jnp.float32
BF16 = jnp.bfloat16
HEADS = 2
LAG = 3
EARLY = 3


def dot(a, b, ca, cb):
    return lax.dot_general(a, b, (((ca,), (cb,)), ((), ())), preferred_element_type=F32)


def exact_dot(a, b, ca, cb):
    return lax.dot_general(
        a, b, (((ca,), (cb,)), ((), ())),
        preferred_element_type=F32, precision=lax.Precision.HIGHEST,
    )


def pair_columns(cols, j, size):
    lane = lax.broadcasted_iota(jnp.int32, (cols.shape[0], 2 * size), 1)
    return jnp.where(lane < size, cols[:, j : j + 1], cols[:, j + 1 : j + 2])


def flip(index, bits, limit):
    other, bit = index, 1
    while bit < limit:
        if bits & bit:
            other = other + bit - 2 * bit * lax.rem(lax.div(index, bit), 2)
        bit *= 2
    return other


def ordered(n):
    def key(r):
        return (r & -r) or n, -r

    return sorted(range(0, n, 2), key=key)


def layer_kernel(
    n, m, size, fused, t_ref, w_ref, x_ref, g_ref, logit_ref, rate_ref,
    dx_ref, dlogit_ref, drate_ref, weight_ref,
    b_ref, c_ref, c_in, cols1, cols2, rows_ref, span, span_in, cf, cf_in,
    e_own, e_other, f_own, f_other, scores, d_scores, d_b, d_c,
    sums1, sums2, row_sums, back, back_in,
    gs_snd, gs_in, e_in, f_in, e_snd, f_snd,
    small_sem, gs_sem, e_sem, f_sem, *more,
):
    if fused:
        (
            tok_snd, tok_in, tok, gbc_snd, gbc_in, gbc, acc, got, out, rate_dp, rate_got, rate_acc,
            tok_sem, gbc_sem, acc_sem, out_sem, rate_sem,
        ) = more
    chunks = gs_snd.shape[0]
    length, state = b_ref.shape
    heads = logit_ref.shape[0]
    width = HEADS * size
    nz = n // 2
    me = lax.axis_index("seq")
    odd = lax.rem(me, 2)
    z = lax.div(me, 2)
    partner = me + 1 - 2 * odd
    first, last = z == 0, z == nz - 1
    barrier = pltpu.get_barrier_semaphore()

    def greet(who, axis="seq"):
        pl.semaphore_signal(
            barrier, inc=1, device_id={axis: who}, device_id_type=pl.DeviceIdType.MESH
        )

    greet(partner)
    pl.when(jnp.logical_not(first))(lambda: greet(me - 2))
    pl.when(jnp.logical_not(last))(lambda: greet(me + 2))
    greeters = 1
    if fused:
        bit = 4
        while bit < n:
            greet(flip(me, bit, n))
            greeters += 1
            bit *= 2
        for k in range(1, m):
            greet(flip(lax.axis_index("dp"), k, m), "dp")
            greeters += 1

    def send(src, dst, sems, k, who, axis="seq"):
        return pltpu.make_async_remote_copy(
            src_ref=src, dst_ref=dst, send_sem=sems.at[0, k], recv_sem=sems.at[1, k],
            device_id={axis: who}, device_id_type=pl.DeviceIdType.MESH,
        )

    def copy_span():
        return send(span, span_in, small_sem, 0, partner)

    def copy_c():
        return send(cf, cf_in, small_sem, 1, partner)

    def copy_back(i):
        return send(back.at[i], back_in.at[i], small_sem, 2 + i, partner)

    def copy_g(k):
        return send(gs_snd.at[k], gs_in.at[k], gs_sem, k, partner)

    def copy_e(k):
        return send(e_snd.at[k], e_in.at[k], e_sem, k, me + 2)

    def copy_f(k):
        return send(f_snd.at[k], f_in.at[k], f_sem, k, me - 2)

    def turn(value, k):
        lanes = value.shape[1]
        return pltpu.roll(value, lax.rem(lanes - HEADS * k, lanes), 1)

    def wide(k):
        return pl.ds(pl.multiple_of(k * width, width), width)

    logit, rate = logit_ref[...], rate_ref[...]
    dt_all = (jnp.maximum(logit, 0.0) + jnp.log1p(jnp.exp(-jnp.abs(logit)))).T
    row_at = lax.broadcasted_iota(jnp.int32, (length, length), 0)
    col_at = lax.broadcasted_iota(jnp.int32, (length, length), 1)
    until = (row_at >= col_at).astype(F32)
    log_decay = exact_dot(until, -rate * dt_all, 1, 0)
    to_end = jnp.exp(log_decay[length - 1 : length, :] - log_decay)
    grow_all = jnp.exp(log_decay)
    q1 = jnp.concatenate([log_decay, dt_all], axis=1)
    q2 = jnp.concatenate([to_end, grow_all], axis=1)
    span[...] = jnp.broadcast_to(q2[length - 1 : length, :], span.shape)
    by_head = q1.T
    for k in range(chunks):
        rows_ref[k] = by_head[HEADS * k : HEADS * (k + 1), :]

    def scale(k, unused):
        cols1[k] = turn(q1, k)
        cols = turn(q2, k)
        cols2[k] = cols
        gs_snd[k] = g_ref[:, wide(k)].astype(F32) * pair_columns(cols, heads, size)
        copy_g(k).start()
        return unused

    end = jnp.logical_or(first, last)
    pl.when(end)(lambda: pl.semaphore_wait(barrier, min(nz - 1, 1) + greeters))
    pl.when(jnp.logical_not(end))(lambda: pl.semaphore_wait(barrier, 2 + greeters))
    copy_span().start()
    lax.fori_loop(0, EARLY, scale, 0)
    bc = dot(t_ref[...], w_ref[...], 1, 0).astype(BF16)
    b_ref[...] = bc[:, :state]
    c_ref[...] = bc[:, state:]
    cf[...] = bc[:, state:].astype(F32)
    copy_c().start()
    scores[...] = dot(b_ref[...], c_ref[...], 1, 1)
    for ref in (d_scores, d_b, d_c, sums1, sums2, row_sums, back):
        ref[...] = jnp.zeros_like(ref)
    copy_span().wait_recv()
    copy_c().wait_recv()
    c_in[...] = cf_in[...].astype(BF16)

    def spans(ref, k):
        return pair_columns(turn(ref[...], k)[:1, :], heads, size)

    def forward(k):
        value = e_in[k]
        weight = pair_columns(cols1[k], heads, size) * pair_columns(cols2[k], 0, size)
        near = dot(b_ref[...], (x_ref[:, wide(k)].astype(F32) * weight).astype(BF16), 0, 0)
        mine, theirs = spans(span, k), spans(span_in, k)

        @pl.when(odd == 0)
        def _():
            e_own[k] = value.astype(BF16)
            middle = mine * value + near
            e_other[k] = middle.astype(BF16)
            e_snd[k] = theirs * middle

        @pl.when(odd == 1)
        def _():
            e_other[k] = value.astype(BF16)
            middle = theirs * value
            e_own[k] = middle.astype(BF16)
            e_snd[k] = mine * middle + near

    def backward(k):
        value = f_in[k]
        near = dot(c_ref[...], gs_snd[k].astype(BF16), 0, 0)
        far = dot(c_in[...], gs_in[k].astype(BF16), 0, 0)
        mine, theirs = spans(span, k), spans(span_in, k)

        @pl.when(odd == 0)
        def _():
            f_other[k] = value.astype(BF16)
            middle = theirs * value + far
            f_own[k] = middle.astype(BF16)
            f_snd[k] = mine * middle + near

        @pl.when(odd == 1)
        def _():
            f_own[k] = value.astype(BF16)
            middle = mine * value + near
            f_other[k] = middle.astype(BF16)
            f_snd[k] = theirs * middle + far

    def gradients(k):
        cols, rows = cols1[k], rows_ref[k]
        k_st = scores[...]
        causal = col_at >= row_at
        low = lax.broadcasted_iota(jnp.int32, (length, width), 1) < size
        place = lax.broadcasted_iota(jnp.int32, sums1.shape, 1) - k * HEADS
        row_place = lax.broadcasted_iota(jnp.int32, row_sums.shape, 0) - k * HEADS
        res1, res2, res3, res_rows = sums1[...], sums2[...], back[1], row_sums[...]
        q_sum = d_scores[...]
        x2, g2 = x_ref[:, wide(k)], g_ref[:, wide(k)]
        x2f = x2.astype(F32)
        e2, f2, e3, f3 = e_own[k], f_own[k], e_other[k], f_other[k]
        gs, gs3 = gs_snd[k], gs_in[k]
        dt2 = pair_columns(cols, heads, size)
        end2 = pair_columns(cols2[k], 0, size)
        g_low = jnp.where(low, g2, jnp.zeros_like(g2))
        g_high = jnp.where(low, jnp.zeros_like(g2), g2)
        g_both = jnp.concatenate([g_low, g_high], axis=0)
        gram = dot(x2, g_both, 1, 1)
        weights = []
        for h in range(HEADS):
            gap = rows[h : h + 1, :] - cols[:, h : h + 1]
            decay = jnp.exp(jnp.where(causal, gap, -jnp.inf))
            mg = decay * gram[:, h * length : (h + 1) * length]
            dt = cols[:, heads + h : heads + h + 1]
            q_sum = q_sum + mg * dt
            raw = mg * k_st
            res_rows = jnp.where(row_place == h, jnp.sum(raw * dt, axis=0, keepdims=True), res_rows)
            res1 = jnp.where(place == h, jnp.sum(raw, axis=1, keepdims=True), res1)
            weights.append((decay * k_st).astype(BF16))
        z2 = dot(jnp.concatenate(weights, axis=1), g_both, 1, 0)
        z_in = dot(b_ref[...], f2, 1, 0) * end2
        dx_ref[:, wide(k)] = (dt2 * (z2 + z_in)).astype(dx_ref.dtype)
        xz = x2f * z_in
        gy = gs * dot(c_ref[...], e2, 1, 0)
        gy3 = gs3 * dot(c_in[...], e3, 1, 0)
        ef = jnp.sum(e2.astype(F32) * f2.astype(F32), axis=0, keepdims=True)
        ef3 = jnp.sum(e3.astype(F32) * f3.astype(F32), axis=0, keepdims=True)
        low_row = low[:1, :]

        def half(value, h, mask):
            keep = mask if h == 0 else jnp.logical_not(mask)
            return jnp.sum(jnp.where(keep, value, jnp.zeros_like(value)), axis=1, keepdims=True)

        for h in range(HEADS):
            res1 = jnp.where(place == h + heads, half(xz, h, low), res1)
            res2 = jnp.where(place == h, half(gy, h, low), res2)
            res2 = jnp.where(place == h + heads, half(ef, h, low_row), res2)
            res3 = jnp.where(place == h, half(gy3, h, low), res3)
            res3 = jnp.where(place == h + heads, half(ef3, h, low_row), res3)
        sums1[...] = res1
        sums2[...] = res2
        back[1] = res3
        row_sums[...] = res_rows
        d_scores[...] = q_sum
        d_b[...] += dot((x2f * (end2 * dt2)).astype(BF16), f2, 1, 1)
        d_c[...] += dot(gs.astype(BF16), e2, 1, 1)
        back[0] += dot(gs3.astype(BF16), e3, 1, 1)

    delay = LAG * lax.max(z, nz - 1 - z)

    def step(t, unused):
        @pl.when(t + EARLY < chunks)
        def _():
            scale(t + EARLY, 0)

        kf = t - LAG * z

        @pl.when(jnp.logical_and(kf >= 0, kf < chunks))
        def _():
            pl.when(jnp.logical_not(first))(lambda: copy_e(kf).wait_recv())

            @pl.when(first)
            def _():
                e_in[kf] = jnp.zeros_like(e_in[kf])

            forward(kf)
            pl.when(jnp.logical_not(last))(lambda: copy_e(kf).start())

        kb = t - LAG * (nz - 1 - z)

        @pl.when(jnp.logical_and(kb >= 0, kb < chunks))
        def _():
            copy_g(kb).wait_recv()
            pl.when(jnp.logical_not(last))(lambda: copy_f(kb).wait_recv())

            @pl.when(last)
            def _():
                f_in[kb] = jnp.zeros_like(f_in[kb])

            backward(kb)
            pl.when(jnp.logical_not(first))(lambda: copy_f(kb).start())

        kg = t - delay
        pl.when(jnp.logical_and(kg >= 0, kg < chunks))(lambda: gradients(kg))
        return unused

    if fused:
        dp = lax.axis_index("dp")
        piece = tok.shape[1]

        def columns(s, k):
            first_column = (s * m + flip(dp, k, m)) * piece
            return t_ref[:, pl.ds(pl.multiple_of(first_column, piece), piece)].astype(F32)

        def copy_tokens(k):
            return send(
                tok_snd.at[k - 1], tok_in.at[k - 1], tok_sem, k - 1, flip(dp, k, m), "dp"
            )

        def copy_gbc(i, k):
            return send(
                gbc_snd.at[i], gbc_in.at[k - 1, i], gbc_sem, (m - 1) * i + k - 1,
                flip(dp, k, m), "dp",
            )

        def copy_acc(i, r):
            bit = r & -r
            return send(
                acc.at[i, r], got.at[i, r - 1], acc_sem, (n - 1) * i + r - 1, flip(me, bit, n)
            )

        def copy_out(i, k):
            return send(
                out.at[i, 0], out.at[i, k], out_sem, m * i + k, flip(dp, k, m), "dp"
            )

        def copy_rate_dp(k):
            return send(
                rate_dp.at[0], rate_dp.at[k], rate_sem, k - 1, flip(dp, k, m), "dp"
            )

        def copy_rate(i):
            return send(
                rate_acc.at[i], rate_got.at[i], rate_sem, m - 1 + i, flip(me, 1 << i, n)
            )

        def spread(s, unused):
            for k in range(1, m):
                tok_snd[k - 1, s] = columns(s, k)
            return unused

        lax.fori_loop(0, n, spread, 0)
        for k in range(1, m):
            copy_tokens(k).start()

    lax.fori_loop(0, chunks + delay, step, 0)
    copy_back(0).start()
    copy_back(1).start()
    dk = d_scores[...].astype(BF16)
    grad_b = (d_b[...] + dot(dk, c_ref[...], 1, 0)).astype(BF16)
    if fused:
        gbc_snd[0] = grad_b.astype(F32)
        for k in range(1, m):
            copy_gbc(0, k).start()
        gbc[0, :length] = grad_b
    else:
        weight_ref[:, :state] = grad_b
    c_total = d_c[...] + dot(dk, b_ref[...], 0, 0)
    copy_back(0).wait_recv()
    grad_c = (c_total + back_in[0]).astype(BF16)
    if fused:
        gbc_snd[1] = grad_c.astype(F32)
        for k in range(1, m):
            copy_gbc(1, k).start()
        gbc[1, :length] = grad_c
        for k in range(1, m):
            copy_tokens(k).wait_recv()

        def place_tokens(r, unused):
            s = r
            for k in range(m):
                block = columns(s, k) if k == 0 else tok_in[k - 1, s]
                tok[s, :, k * length : (k + 1) * length] = block.T.astype(BF16)
            return unused

        lax.fori_loop(0, n, place_tokens, 0)
        order = ordered(n)
        for i in range(2):
            for k in range(1, m):
                copy_gbc(i, k).wait_recv()
                gbc[i, k * length : (k + 1) * length] = gbc_in[k - 1, i].astype(BF16)
            for r in [r + 1 for r in order] + order:
                acc[i, r] = dot(tok[flip(me, r, n)], gbc[i], 1, 0)
                if r % 2:
                    copy_acc(i, r).start()
    else:
        weight_ref[:, state:] = grad_c
    copy_back(1).wait_recv()
    total = sums2[...] + back_in[1]
    inside, x_in = sums1[:, :heads], sums1[:, heads:]
    g_in, both = total[:, :heads], span[:1, heads:] * total[:, heads:]
    dt_all = cols1[0, :, heads:]
    after = (row_at <= col_at).astype(F32)
    before = (row_at > col_at).astype(F32)
    d_log = (
        both
        + exact_dot(before, dt_all * x_in, 1, 0)
        + exact_dot(after, g_in - dt_all * inside, 1, 0)
        + exact_dot(after, row_sums[...], 1, 1)
    )
    d_rate = -jnp.sum(dt_all * d_log, axis=0, keepdims=True)
    d_rate = jnp.broadcast_to(
        jnp.concatenate([d_rate, jnp.zeros_like(d_rate)], axis=1), (8, 2 * heads)
    )
    if fused:
        rate_dp[0] = d_rate
        for k in range(1, m):
            copy_rate_dp(k).start()
    else:
        drate_ref[...] = d_rate
    d_step = inside + x_in - rate_ref[...] * d_log
    dlogit_ref[...] = d_step.T * jax.nn.sigmoid(logit_ref[...])
    if fused:
        for i in range(2):
            for r in order:
                bit = 1
                while bit < ((r & -r) or n):
                    copy_acc(i, r + bit).wait_recv()
                    acc[i, r] += got[i, r + bit - 1]
                    bit *= 2
                if r:
                    copy_acc(i, r).start()
            out[i, 0] = acc[i, 0]
            for k in range(1, m):
                copy_out(i, k).start()
            if i == 0:
                parts = [rate_dp[0]]
                for k in range(1, m):
                    copy_rate_dp(k).wait_recv()
                    parts.append(rate_dp[k])
                while len(parts) > 1:
                    parts = [p + q for p, q in zip(parts[::2], parts[1::2])]
                rate_acc[0] = parts[0]
                copy_rate(0).start()
        stages = n.bit_length() - 1
        for i in range(stages):
            copy_rate(i).wait_recv()
            rate_acc[i + 1] = rate_acc[i] + rate_got[i]
            if i + 1 < stages:
                copy_rate(i + 1).start()
        drate_ref[...] = rate_acc[stages, :1, :heads]
        for i in range(2):
            for k in range(m):
                if k:
                    copy_out(i, k).wait_recv()
                first_row = pl.multiple_of(flip(dp, k, m) * piece, piece)
                weight_ref[pl.ds(first_row, piece), i * state : (i + 1) * state] = out[i, k]
        for k in range(1, m):
            copy_tokens(k).wait_send()
            copy_rate_dp(k).wait_send()
            for i in range(2):
                copy_gbc(i, k).wait_send()
                copy_out(i, k).wait_send()
        for i in range(2):
            for r in range(1, n):
                copy_acc(i, r).wait_send()
        for i in range(stages):
            copy_rate(i).wait_send()
    copy_span().wait_send()
    copy_c().wait_send()
    copy_back(0).wait_send()
    copy_back(1).wait_send()

    def settle(k, unused):
        copy_g(k).wait_send()
        pl.when(jnp.logical_not(last))(lambda: copy_e(k).wait_send())
        pl.when(jnp.logical_not(first))(lambda: copy_f(k).wait_send())
        return unused

    lax.fori_loop(0, chunks, settle, 0)


def weight_kernel(
    n, m, t_ref, g_ref, rate_ref, out_ref, rate_out,
    acc, got, ring, r_acc, r_got, sem, out_sem, r_sem,
):
    chunks, blocks, rows = acc.shape[0], acc.shape[1], acc.shape[2]
    piece = chunks * rows
    seq, dp = lax.axis_index("seq"), lax.axis_index("dp")
    dp_steps, seq_steps, bit = [], [], 1
    while bit < m:
        dp_steps.append(("dp", bit, lax.rem(lax.div(dp, bit), 2)))
        bit *= 2
    bit = 1
    while bit < n:
        seq_steps.append(("seq", bit, lax.rem(lax.div(seq, bit), 2)))
        bit *= 2
    count = len(dp_steps) + len(seq_steps)
    orders = (dp_steps + seq_steps, dp_steps[:1] + seq_steps + dp_steps[1:])

    def peer(c, s):
        axis, bit, mine = orders[c % 2][s]
        return {axis: lax.axis_index(axis) + bit - 2 * bit * mine}

    def dp_peer(k):
        other, bit = dp, 1
        while bit < m:
            if k & bit:
                other = other + bit - 2 * bit * lax.rem(lax.div(dp, bit), 2)
            bit *= 2
        return {"dp": other}

    barrier = pltpu.get_barrier_semaphore()
    friends = [dp_peer(k) for k in range(1, m)] + [
        peer(0, s) for s in range(len(dp_steps), count)
    ]
    for friend in friends:
        pl.semaphore_signal(
            barrier, inc=1, device_id=friend, device_id_type=pl.DeviceIdType.MESH
        )

    starts, offsets = [], []
    for order in orders:
        base, width, total = 0, blocks, 0
        starts.append([])
        for unused, unused, mine in order:
            width //= 2
            starts[-1].append((base + width * mine, base + width * (1 - mine), width))
            base = base + width * mine
            if len(starts) == 1:
                offsets.append(total)
                total += width

    def copy(c, s):
        keep, give, size = starts[c % 2][s]
        return pltpu.make_async_remote_copy(
            src_ref=acc.at[c, pl.ds(give, size)],
            dst_ref=got.at[c, pl.ds(offsets[s], size)],
            send_sem=sem.at[0, c, s], recv_sem=sem.at[1, c, s],
            device_id=peer(c, s), device_id_type=pl.DeviceIdType.MESH,
        )

    def rate_copy(s):
        return pltpu.make_async_remote_copy(
            src_ref=r_acc.at[s], dst_ref=r_got.at[s],
            send_sem=r_sem.at[0, s], recv_sem=r_sem.at[1, s],
            device_id=peer(0, s), device_id_type=pl.DeviceIdType.MESH,
        )

    def out_copy(c, k):
        return pltpu.make_async_remote_copy(
            src_ref=ring.at[0, c], dst_ref=ring.at[k, c],
            send_sem=out_sem.at[0, c, k], recv_sem=out_sem.at[1, c, k],
            device_id=dp_peer(k), device_id_type=pl.DeviceIdType.MESH,
        )

    g = g_ref[...]
    r_acc[0] = rate_ref[...]
    block = 128
    for first in range(0, t_ref.shape[1], block):
        product = dot(t_ref[:, first : first + block], g, 0, 0)
        for part in range(0, block, rows):
            row = first + part
            owner, inner = row // (m * piece), row % (m * piece)
            chunk, place = inner % piece // rows, 0
            for axis, bit, unused in orders[chunk % 2]:
                index = inner // piece if axis == "dp" else owner
                place = 2 * place + index // bit % 2
            acc[chunk, place] = product[part : part + rows]
    pl.semaphore_wait(barrier, len(friends))
    for c in range(chunks):
        copy(c, 0).start()
    rate_copy(0).start()
    for s in range(count):
        for c in range(chunks):
            copy(c, s).wait_recv()
            keep, give, size = starts[c % 2][s]
            value = acc[c, pl.ds(keep, size)] + got[c, pl.ds(offsets[s], size)]
            if s + 1 < count:
                acc[c, pl.ds(keep, size)] = value
                copy(c, s + 1).start()
            else:
                ring[0, c] = value[0]
                for k in range(1, m):
                    out_copy(c, k).start()
        rate_copy(s).wait_recv()
        r_acc[s + 1] = r_acc[s] + r_got[s]
        if s + 1 < count:
            rate_copy(s + 1).start()
    rate_out[...] = r_acc[count]
    for c in range(chunks):
        for k in range(m):
            if k > 0:
                out_copy(c, k).wait_recv()
            where = dp_peer(k)["dp"] if k > 0 else dp
            out_ref[pl.ds(where * piece + c * rows, rows)] = ring[k, c]
    for c in range(chunks):
        for s in range(count):
            copy(c, s).wait_send()
        for k in range(1, m):
            out_copy(c, k).wait_send()
    for s in range(count):
        rate_copy(s).wait_send()


def shards(layer_input, projection, ssm_input, step_logit, decay_rate, output_grad):
    tokens, x_rows, logit, grad_rows = layer_input[0], ssm_input[0], step_logit[0], output_grad[0]
    length, full = x_rows.shape
    heads = logit.shape[1]
    size = full // heads
    state = projection.shape[1] // 2
    groups = heads // HEADS
    width = HEADS * size
    count = lax.axis_size("seq")
    limit = 60 * 2**20
    vmem = pl.BlockSpec(memory_space=pltpu.VMEM)
    slots = pltpu.VMEM((groups, state, width), F32)
    rows_in = pltpu.VMEM((groups, length, width), F32)
    half = pltpu.VMEM((groups, state, width), BF16)
    square = pltpu.VMEM((length, length), F32)
    sums = pltpu.VMEM((length, state), F32)
    short = pltpu.VMEM((length, state), BF16)
    by_lane = pltpu.VMEM((length, 2 * heads), F32)
    cols = pltpu.VMEM((groups, length, 2 * heads), F32)
    strip = pltpu.VMEM((8, 2 * heads), F32)
    two = pltpu.VMEM((2, length, state), F32)
    members = lax.axis_size("dp")
    blocks = count * members
    piece = tokens.shape[1] // blocks
    levels = blocks.bit_length() - 1
    fused = piece % 128 == 0
    scratch = (
        [short] * 3
        + [cols] * 2
        + [pltpu.VMEM((groups, HEADS, length), F32), strip, strip, sums, sums]
        + [half] * 4
        + [square, square, sums, sums]
        + [by_lane, by_lane, pltpu.VMEM((heads, length), F32), two, two]
        + [rows_in] * 2
        + [slots] * 4
        + [pltpu.SemaphoreType.DMA((2, 4))]
        + [pltpu.SemaphoreType.DMA((2, groups))] * 3
    )
    rate_shape = jax.ShapeDtypeStruct((8, 2 * heads), F32)
    weight_shape = jax.ShapeDtypeStruct((length, 2 * state), BF16)
    if fused:
        stages = count.bit_length() - 1
        others = members - 1
        scratch += [pltpu.VMEM((others, count, length, piece), F32)] * 2
        scratch += [
            pltpu.VMEM((count, piece, members * length), BF16),
            pltpu.VMEM((2, length, state), F32),
            pltpu.VMEM((others, 2, length, state), F32),
            pltpu.VMEM((2, members * length, state), BF16),
            pltpu.VMEM((2, count, piece, state), F32),
            pltpu.VMEM((2, count - 1, piece, state), F32),
            pltpu.VMEM((2, members, piece, state), F32),
            pltpu.VMEM((members, 8, 2 * heads), F32),
            pltpu.VMEM((stages, 8, 2 * heads), F32),
            pltpu.VMEM((stages + 1, 8, 2 * heads), F32),
            pltpu.SemaphoreType.DMA((2, others)),
            pltpu.SemaphoreType.DMA((2, 2 * others)),
            pltpu.SemaphoreType.DMA((2, 2 * (count - 1))),
            pltpu.SemaphoreType.DMA((2, 2 * members)),
            pltpu.SemaphoreType.DMA((2, others + stages)),
        ]
        rate_shape = jax.ShapeDtypeStruct((1, heads), F32)
        weight_shape = jax.ShapeDtypeStruct((members * piece, 2 * state), F32)
    grad_x, grad_logit, rate_rows, weights = pl.pallas_call(
        functools.partial(layer_kernel, count, members, size, fused),
        in_specs=[vmem] * 6,
        out_specs=[vmem] * 4,
        out_shape=[
            jax.ShapeDtypeStruct((length, full), BF16),
            jax.ShapeDtypeStruct((heads, length), F32),
            rate_shape,
            weight_shape,
        ],
        scratch_shapes=scratch,
        compiler_params=pltpu.CompilerParams(
            collective_id=0, has_side_effects=True, vmem_limit_bytes=limit
        ),
        name="layer_gradients",
    )(tokens, projection, x_rows, grad_rows, logit.T, decay_rate[None, :])
    if fused:
        return (grad_x[None], grad_logit.T[None], rate_rows[0], weights)
    chunks = max(1, min(8, piece // 8))
    rows = piece // chunks
    weight_rows, rate_sum = pl.pallas_call(
        functools.partial(weight_kernel, count, members),
        in_specs=[vmem] * 3,
        out_specs=[vmem] * 2,
        out_shape=[
            jax.ShapeDtypeStruct((members * piece, 2 * state), F32),
            jax.ShapeDtypeStruct((8, 128), F32),
        ],
        scratch_shapes=[
            pltpu.VMEM((chunks, blocks, rows, 2 * state), F32),
            pltpu.VMEM((chunks, blocks, rows, 2 * state), F32),
            pltpu.VMEM((members, chunks, rows, 2 * state), F32),
            pltpu.VMEM((levels + 1, 8, 128), F32),
            pltpu.VMEM((levels, 8, 128), F32),
            pltpu.SemaphoreType.DMA((2, chunks, levels)),
            pltpu.SemaphoreType.DMA((2, chunks, members)),
            pltpu.SemaphoreType.DMA((2, levels)),
        ],
        compiler_params=pltpu.CompilerParams(
            collective_id=1, has_side_effects=True, vmem_limit_bytes=limit
        ),
        name="weight_gradient",
    )(tokens, weights, rate_rows)
    rate_sum = rate_sum[0, :heads]
    return (grad_x[None], grad_logit.T[None], rate_sum, weight_rows)


def solution(mesh):
    placed = (
        P("dp", "seq", None),
        P(),
        P("dp", "seq", None),
        P("dp", "seq", None),
        P(),
        P("dp", "seq", None),
    )
    return jax.shard_map(
        shards,
        mesh=mesh,
        in_specs=placed,
        out_specs=(P("dp", "seq", None), P("dp", "seq", None), P(), P("seq", None)),
        check_vma=False,
    )
```

```python
import functools

import jax
import jax.numpy as jnp
from jax import lax
from jax.experimental import pallas as pl
from jax.experimental.pallas import tpu as pltpu
from jax.sharding import PartitionSpec as P

F32 = jnp.float32
BF16 = jnp.bfloat16
HEADS = 2
LAG = 3
EARLY = 3


def dot(a, b, ca, cb):
    return lax.dot_general(a, b, (((ca,), (cb,)), ((), ())), preferred_element_type=F32)


def exact_dot(a, b, ca, cb):
    return lax.dot_general(
        a, b, (((ca,), (cb,)), ((), ())),
        preferred_element_type=F32, precision=lax.Precision.HIGHEST,
    )


def pair_columns(cols, j, size):
    lane = lax.broadcasted_iota(jnp.int32, (cols.shape[0], 2 * size), 1)
    return jnp.where(lane < size, cols[:, j : j + 1], cols[:, j + 1 : j + 2])


def flip(index, bits, limit):
    other, bit = index, 1
    while bit < limit:
        if bits & bit:
            other = other + bit - 2 * bit * lax.rem(lax.div(index, bit), 2)
        bit *= 2
    return other


def ordered(n):
    def key(r):
        return (r & -r) or n, -r

    return sorted(range(0, n, 2), key=key)


def layer_kernel(
    n, m, size, fused, t_hbm, w_hbm, x_hbm, g_hbm, logit_ref, rate_ref,
    dx_ref, dlogit_ref, drate_ref, weight_ref, t_ref, w_ref, x_ref, g_ref,
    b_ref, c_ref, c_in, cols1, cols2, rows_ref, span, span_in, cf, cf_in,
    e_own, e_other, f_own, f_other, scores, d_scores, d_b, d_c,
    sums1, sums2, row_sums, back, back_in,
    gs_snd, gs_in, e_in, f_in, e_snd, f_snd,
    load_sem, small_sem, gs_sem, e_sem, f_sem, *more,
):
    if fused:
        (
            tok_snd, tok_in, tok, gbc_snd, gbc_in, gbc, acc, got, out, rate_dp, rate_got, rate_acc,
            tok_sem, gbc_sem, acc_sem, out_sem, rate_sem,
        ) = more
    chunks = gs_snd.shape[0]
    length, state = b_ref.shape
    heads = logit_ref.shape[0]
    width = HEADS * size
    nz = n // 2
    me = lax.axis_index("seq")
    odd = lax.rem(me, 2)
    z = lax.div(me, 2)
    partner = me + 1 - 2 * odd
    first, last = z == 0, z == nz - 1
    barrier = pltpu.get_barrier_semaphore()
    operands = ((g_hbm, g_ref), (t_hbm, t_ref), (w_hbm, w_ref), (x_hbm, x_ref))
    load_g, load_t, load_w, load_x = (
        pltpu.make_async_copy(source, target, load_sem.at[i])
        for i, (source, target) in enumerate(operands)
    )

    def greet(who, axis="seq"):
        pl.semaphore_signal(
            barrier, inc=1, device_id={axis: who}, device_id_type=pl.DeviceIdType.MESH
        )

    load_g.start()
    load_t.start()
    load_w.start()
    load_x.start()
    greet(partner)
    pl.when(jnp.logical_not(first))(lambda: greet(me - 2))
    pl.when(jnp.logical_not(last))(lambda: greet(me + 2))
    greeters = 1
    if fused:
        bit = 4
        while bit < n:
            greet(flip(me, bit, n))
            greeters += 1
            bit *= 2
        for k in range(1, m):
            greet(flip(lax.axis_index("dp"), k, m), "dp")
            greeters += 1

    def send(src, dst, sems, k, who, axis="seq"):
        return pltpu.make_async_remote_copy(
            src_ref=src, dst_ref=dst, send_sem=sems.at[0, k], recv_sem=sems.at[1, k],
            device_id={axis: who}, device_id_type=pl.DeviceIdType.MESH,
        )

    def copy_span():
        return send(span, span_in, small_sem, 0, partner)

    def copy_c():
        return send(cf, cf_in, small_sem, 1, partner)

    def copy_back(i):
        return send(back.at[i], back_in.at[i], small_sem, 2 + i, partner)

    def copy_g(k):
        return send(gs_snd.at[k], gs_in.at[k], gs_sem, k, partner)

    def copy_e(k):
        return send(e_snd.at[k], e_in.at[k], e_sem, k, me + 2)

    def copy_f(k):
        return send(f_snd.at[k], f_in.at[k], f_sem, k, me - 2)

    def turn(value, k):
        lanes = value.shape[1]
        return pltpu.roll(value, lax.rem(lanes - HEADS * k, lanes), 1)

    def wide(k):
        return pl.ds(pl.multiple_of(k * width, width), width)

    logit, rate = logit_ref[...], rate_ref[...]
    dt_all = (jnp.maximum(logit, 0.0) + jnp.log1p(jnp.exp(-jnp.abs(logit)))).T
    row_at = lax.broadcasted_iota(jnp.int32, (length, length), 0)
    col_at = lax.broadcasted_iota(jnp.int32, (length, length), 1)
    until = (row_at >= col_at).astype(F32)
    log_decay = exact_dot(until, -rate * dt_all, 1, 0)
    to_end = jnp.exp(log_decay[length - 1 : length, :] - log_decay)
    grow_all = jnp.exp(log_decay)
    q1 = jnp.concatenate([log_decay, dt_all], axis=1)
    q2 = jnp.concatenate([to_end, grow_all], axis=1)
    span[...] = jnp.broadcast_to(q2[length - 1 : length, :], span.shape)
    def scale(k, unused):
        cols1[k] = turn(q1, k)
        cols = turn(q2, k)
        cols2[k] = cols
        gs_snd[k] = g_ref[:, wide(k)].astype(F32) * pair_columns(cols, heads, size)
        copy_g(k).start()
        return unused

    load_g.wait()
    end = jnp.logical_or(first, last)
    pl.when(end)(lambda: pl.semaphore_wait(barrier, min(nz - 1, 1) + greeters))
    pl.when(jnp.logical_not(end))(lambda: pl.semaphore_wait(barrier, 2 + greeters))
    copy_span().start()
    lax.fori_loop(0, EARLY, scale, 0)
    load_t.wait()
    load_w.wait()
    bc = dot(t_ref[...], w_ref[...], 1, 0).astype(BF16)
    b_ref[...] = bc[:, :state]
    c_ref[...] = bc[:, state:]
    cf[...] = bc[:, state:].astype(F32)
    copy_c().start()
    by_head = q1.T
    for k in range(chunks):
        rows_ref[k] = by_head[HEADS * k : HEADS * (k + 1), :]
    load_x.wait()
    scores[...] = dot(b_ref[...], c_ref[...], 1, 1)
    for ref in (d_scores, d_b, d_c, sums1, sums2, row_sums, back):
        ref[...] = jnp.zeros_like(ref)
    copy_span().wait_recv()
    copy_c().wait_recv()
    c_in[...] = cf_in[...].astype(BF16)

    def spans(ref, k):
        return pair_columns(turn(ref[...], k)[:1, :], heads, size)

    def forward(k):
        value = e_in[k]
        weight = pair_columns(cols1[k], heads, size) * pair_columns(cols2[k], 0, size)
        near = dot(b_ref[...], (x_ref[:, wide(k)].astype(F32) * weight).astype(BF16), 0, 0)
        mine, theirs = spans(span, k), spans(span_in, k)

        @pl.when(odd == 0)
        def _():
            e_own[k] = value.astype(BF16)
            middle = mine * value + near
            e_other[k] = middle.astype(BF16)
            e_snd[k] = theirs * middle

        @pl.when(odd == 1)
        def _():
            e_other[k] = value.astype(BF16)
            middle = theirs * value
            e_own[k] = middle.astype(BF16)
            e_snd[k] = mine * middle + near

    def backward(k):
        value = f_in[k]
        near = dot(c_ref[...], gs_snd[k].astype(BF16), 0, 0)
        far = dot(c_in[...], gs_in[k].astype(BF16), 0, 0)
        mine, theirs = spans(span, k), spans(span_in, k)

        @pl.when(odd == 0)
        def _():
            f_other[k] = value.astype(BF16)
            middle = theirs * value + far
            f_own[k] = middle.astype(BF16)
            f_snd[k] = mine * middle + near

        @pl.when(odd == 1)
        def _():
            f_own[k] = value.astype(BF16)
            middle = mine * value + near
            f_other[k] = middle.astype(BF16)
            f_snd[k] = theirs * middle + far

    def gradients(k):
        cols, rows = cols1[k], rows_ref[k]
        k_st = scores[...]
        causal = col_at >= row_at
        low = lax.broadcasted_iota(jnp.int32, (length, width), 1) < size
        place = lax.broadcasted_iota(jnp.int32, sums1.shape, 1) - k * HEADS
        row_place = lax.broadcasted_iota(jnp.int32, row_sums.shape, 0) - k * HEADS
        res1, res2, res3, res_rows = sums1[...], sums2[...], back[1], row_sums[...]
        q_sum = d_scores[...]
        x2, g2 = x_ref[:, wide(k)], g_ref[:, wide(k)]
        x2f = x2.astype(F32)
        e2, f2, e3, f3 = e_own[k], f_own[k], e_other[k], f_other[k]
        gs, gs3 = gs_snd[k], gs_in[k]
        dt2 = pair_columns(cols, heads, size)
        end2 = pair_columns(cols2[k], 0, size)
        g_low = jnp.where(low, g2, jnp.zeros_like(g2))
        g_high = jnp.where(low, jnp.zeros_like(g2), g2)
        g_both = jnp.concatenate([g_low, g_high], axis=0)
        gram = dot(x2, g_both, 1, 1)
        weights = []
        for h in range(HEADS):
            gap = rows[h : h + 1, :] - cols[:, h : h + 1]
            decay = jnp.exp(jnp.where(causal, gap, -jnp.inf))
            mg = decay * gram[:, h * length : (h + 1) * length]
            dt = cols[:, heads + h : heads + h + 1]
            q_sum = q_sum + mg * dt
            raw = mg * k_st
            res_rows = jnp.where(row_place == h, jnp.sum(raw * dt, axis=0, keepdims=True), res_rows)
            res1 = jnp.where(place == h, jnp.sum(raw, axis=1, keepdims=True), res1)
            weights.append((decay * k_st).astype(BF16))
        z2 = dot(jnp.concatenate(weights, axis=1), g_both, 1, 0)
        z_in = dot(b_ref[...], f2, 1, 0) * end2
        dx_ref[:, wide(k)] = (dt2 * (z2 + z_in)).astype(dx_ref.dtype)
        xz = x2f * z_in
        gy = gs * dot(c_ref[...], e2, 1, 0)
        gy3 = gs3 * dot(c_in[...], e3, 1, 0)
        ef = jnp.sum(e2.astype(F32) * f2.astype(F32), axis=0, keepdims=True)
        ef3 = jnp.sum(e3.astype(F32) * f3.astype(F32), axis=0, keepdims=True)
        low_row = low[:1, :]

        def half(value, h, mask):
            keep = mask if h == 0 else jnp.logical_not(mask)
            return jnp.sum(jnp.where(keep, value, jnp.zeros_like(value)), axis=1, keepdims=True)

        for h in range(HEADS):
            res1 = jnp.where(place == h + heads, half(xz, h, low), res1)
            res2 = jnp.where(place == h, half(gy, h, low), res2)
            res2 = jnp.where(place == h + heads, half(ef, h, low_row), res2)
            res3 = jnp.where(place == h, half(gy3, h, low), res3)
            res3 = jnp.where(place == h + heads, half(ef3, h, low_row), res3)
        sums1[...] = res1
        sums2[...] = res2
        back[1] = res3
        row_sums[...] = res_rows
        d_scores[...] = q_sum
        d_b[...] += dot((x2f * (end2 * dt2)).astype(BF16), f2, 1, 1)
        d_c[...] += dot(gs.astype(BF16), e2, 1, 1)
        back[0] += dot(gs3.astype(BF16), e3, 1, 1)

    delay = LAG * lax.max(z, nz - 1 - z)

    def step(t, unused):
        @pl.when(t + EARLY < chunks)
        def _():
            scale(t + EARLY, 0)

        kf = t - LAG * z

        @pl.when(jnp.logical_and(kf >= 0, kf < chunks))
        def _():
            pl.when(jnp.logical_not(first))(lambda: copy_e(kf).wait_recv())

            @pl.when(first)
            def _():
                e_in[kf] = jnp.zeros_like(e_in[kf])

            forward(kf)
            pl.when(jnp.logical_not(last))(lambda: copy_e(kf).start())

        kb = t - LAG * (nz - 1 - z)

        @pl.when(jnp.logical_and(kb >= 0, kb < chunks))
        def _():
            copy_g(kb).wait_recv()
            pl.when(jnp.logical_not(last))(lambda: copy_f(kb).wait_recv())

            @pl.when(last)
            def _():
                f_in[kb] = jnp.zeros_like(f_in[kb])

            backward(kb)
            pl.when(jnp.logical_not(first))(lambda: copy_f(kb).start())

        kg = t - delay
        pl.when(jnp.logical_and(kg >= 0, kg < chunks))(lambda: gradients(kg))
        return unused

    if fused:
        dp = lax.axis_index("dp")
        piece = tok.shape[1]

        def columns(s, k):
            first_column = (s * m + flip(dp, k, m)) * piece
            return t_ref[:, pl.ds(pl.multiple_of(first_column, piece), piece)].astype(F32)

        def copy_tokens(k):
            return send(
                tok_snd.at[k - 1], tok_in.at[k - 1], tok_sem, k - 1, flip(dp, k, m), "dp"
            )

        def copy_gbc(i, k):
            return send(
                gbc_snd.at[i], gbc_in.at[k - 1, i], gbc_sem, (m - 1) * i + k - 1,
                flip(dp, k, m), "dp",
            )

        def copy_acc(i, r):
            bit = r & -r
            return send(
                acc.at[i, r], got.at[i, r - 1], acc_sem, (n - 1) * i + r - 1, flip(me, bit, n)
            )

        def copy_out(i, k):
            return send(
                out.at[i, 0], out.at[i, k], out_sem, m * i + k, flip(dp, k, m), "dp"
            )

        def copy_rate_dp(k):
            return send(
                rate_dp.at[0], rate_dp.at[k], rate_sem, k - 1, flip(dp, k, m), "dp"
            )

        def copy_rate(i):
            return send(
                rate_acc.at[i], rate_got.at[i], rate_sem, m - 1 + i, flip(me, 1 << i, n)
            )

        def spread(s, unused):
            for k in range(1, m):
                tok_snd[k - 1, s] = columns(s, k)
            return unused

        lax.fori_loop(0, n, spread, 0)
        for k in range(1, m):
            copy_tokens(k).start()

    lax.fori_loop(0, chunks + delay, step, 0)
    copy_back(0).start()
    copy_back(1).start()
    dk = d_scores[...].astype(BF16)
    grad_b = (d_b[...] + dot(dk, c_ref[...], 1, 0)).astype(BF16)
    if fused:
        gbc_snd[0] = grad_b.astype(F32)
        for k in range(1, m):
            copy_gbc(0, k).start()
        gbc[0, :length] = grad_b
    else:
        weight_ref[:, :state] = grad_b
    c_total = d_c[...] + dot(dk, b_ref[...], 0, 0)
    copy_back(0).wait_recv()
    grad_c = (c_total + back_in[0]).astype(BF16)
    if fused:
        gbc_snd[1] = grad_c.astype(F32)
        for k in range(1, m):
            copy_gbc(1, k).start()
        gbc[1, :length] = grad_c
        for k in range(1, m):
            copy_tokens(k).wait_recv()

        def place_tokens(r, unused):
            s = r
            for k in range(m):
                block = columns(s, k) if k == 0 else tok_in[k - 1, s]
                tok[s, :, k * length : (k + 1) * length] = block.T.astype(BF16)
            return unused

        lax.fori_loop(0, n, place_tokens, 0)
        order = ordered(n)
        for i in range(2):
            for k in range(1, m):
                copy_gbc(i, k).wait_recv()
                gbc[i, k * length : (k + 1) * length] = gbc_in[k - 1, i].astype(BF16)
            for r in [r + 1 for r in order] + order:
                acc[i, r] = dot(tok[flip(me, r, n)], gbc[i], 1, 0)
                if r % 2:
                    copy_acc(i, r).start()
    else:
        weight_ref[:, state:] = grad_c
    copy_back(1).wait_recv()
    total = sums2[...] + back_in[1]
    inside, x_in = sums1[:, :heads], sums1[:, heads:]
    g_in, both = total[:, :heads], span[:1, heads:] * total[:, heads:]
    dt_all = cols1[0, :, heads:]
    after = (row_at <= col_at).astype(F32)
    before = (row_at > col_at).astype(F32)
    d_log = (
        both
        + exact_dot(before, dt_all * x_in, 1, 0)
        + exact_dot(after, g_in - dt_all * inside, 1, 0)
        + exact_dot(after, row_sums[...], 1, 1)
    )
    d_rate = -jnp.sum(dt_all * d_log, axis=0, keepdims=True)
    d_rate = jnp.broadcast_to(
        jnp.concatenate([d_rate, jnp.zeros_like(d_rate)], axis=1), (8, 2 * heads)
    )
    if fused:
        rate_dp[0] = d_rate
        for k in range(1, m):
            copy_rate_dp(k).start()
    else:
        drate_ref[...] = d_rate
    d_step = inside + x_in - rate_ref[...] * d_log
    dlogit_ref[...] = d_step.T * jax.nn.sigmoid(logit_ref[...])
    if fused:
        for i in range(2):
            for r in order:
                bit = 1
                while bit < ((r & -r) or n):
                    copy_acc(i, r + bit).wait_recv()
                    acc[i, r] += got[i, r + bit - 1]
                    bit *= 2
                if r:
                    copy_acc(i, r).start()
            out[i, 0] = acc[i, 0]
            for k in range(1, m):
                copy_out(i, k).start()
            if i == 0:
                parts = [rate_dp[0]]
                for k in range(1, m):
                    copy_rate_dp(k).wait_recv()
                    parts.append(rate_dp[k])
                while len(parts) > 1:
                    parts = [p + q for p, q in zip(parts[::2], parts[1::2])]
                rate_acc[0] = parts[0]
                copy_rate(0).start()
        stages = n.bit_length() - 1
        for i in range(stages):
            copy_rate(i).wait_recv()
            rate_acc[i + 1] = rate_acc[i] + rate_got[i]
            if i + 1 < stages:
                copy_rate(i + 1).start()
        drate_ref[...] = rate_acc[stages, :1, :heads]
        for i in range(2):
            for k in range(m):
                if k:
                    copy_out(i, k).wait_recv()
                first_row = pl.multiple_of(flip(dp, k, m) * piece, piece)
                weight_ref[pl.ds(first_row, piece), i * state : (i + 1) * state] = out[i, k]
        for k in range(1, m):
            copy_tokens(k).wait_send()
            copy_rate_dp(k).wait_send()
            for i in range(2):
                copy_gbc(i, k).wait_send()
                copy_out(i, k).wait_send()
        for i in range(2):
            for r in range(1, n):
                copy_acc(i, r).wait_send()
        for i in range(stages):
            copy_rate(i).wait_send()
    copy_span().wait_send()
    copy_c().wait_send()
    copy_back(0).wait_send()
    copy_back(1).wait_send()

    def settle(k, unused):
        copy_g(k).wait_send()
        pl.when(jnp.logical_not(last))(lambda: copy_e(k).wait_send())
        pl.when(jnp.logical_not(first))(lambda: copy_f(k).wait_send())
        return unused

    lax.fori_loop(0, chunks, settle, 0)


def weight_kernel(
    n, m, t_ref, g_ref, rate_ref, out_ref, rate_out,
    acc, got, ring, r_acc, r_got, sem, out_sem, r_sem,
):
    chunks, blocks, rows = acc.shape[0], acc.shape[1], acc.shape[2]
    piece = chunks * rows
    seq, dp = lax.axis_index("seq"), lax.axis_index("dp")
    dp_steps, seq_steps, bit = [], [], 1
    while bit < m:
        dp_steps.append(("dp", bit, lax.rem(lax.div(dp, bit), 2)))
        bit *= 2
    bit = 1
    while bit < n:
        seq_steps.append(("seq", bit, lax.rem(lax.div(seq, bit), 2)))
        bit *= 2
    count = len(dp_steps) + len(seq_steps)
    orders = (dp_steps + seq_steps, dp_steps[:1] + seq_steps + dp_steps[1:])

    def peer(c, s):
        axis, bit, mine = orders[c % 2][s]
        return {axis: lax.axis_index(axis) + bit - 2 * bit * mine}

    def dp_peer(k):
        other, bit = dp, 1
        while bit < m:
            if k & bit:
                other = other + bit - 2 * bit * lax.rem(lax.div(dp, bit), 2)
            bit *= 2
        return {"dp": other}

    barrier = pltpu.get_barrier_semaphore()
    friends = [dp_peer(k) for k in range(1, m)] + [
        peer(0, s) for s in range(len(dp_steps), count)
    ]
    for friend in friends:
        pl.semaphore_signal(
            barrier, inc=1, device_id=friend, device_id_type=pl.DeviceIdType.MESH
        )

    starts, offsets = [], []
    for order in orders:
        base, width, total = 0, blocks, 0
        starts.append([])
        for unused, unused, mine in order:
            width //= 2
            starts[-1].append((base + width * mine, base + width * (1 - mine), width))
            base = base + width * mine
            if len(starts) == 1:
                offsets.append(total)
                total += width

    def copy(c, s):
        keep, give, size = starts[c % 2][s]
        return pltpu.make_async_remote_copy(
            src_ref=acc.at[c, pl.ds(give, size)],
            dst_ref=got.at[c, pl.ds(offsets[s], size)],
            send_sem=sem.at[0, c, s], recv_sem=sem.at[1, c, s],
            device_id=peer(c, s), device_id_type=pl.DeviceIdType.MESH,
        )

    def rate_copy(s):
        return pltpu.make_async_remote_copy(
            src_ref=r_acc.at[s], dst_ref=r_got.at[s],
            send_sem=r_sem.at[0, s], recv_sem=r_sem.at[1, s],
            device_id=peer(0, s), device_id_type=pl.DeviceIdType.MESH,
        )

    def out_copy(c, k):
        return pltpu.make_async_remote_copy(
            src_ref=ring.at[0, c], dst_ref=ring.at[k, c],
            send_sem=out_sem.at[0, c, k], recv_sem=out_sem.at[1, c, k],
            device_id=dp_peer(k), device_id_type=pl.DeviceIdType.MESH,
        )

    g = g_ref[...]
    r_acc[0] = rate_ref[...]
    block = 128
    for first in range(0, t_ref.shape[1], block):
        product = dot(t_ref[:, first : first + block], g, 0, 0)
        for part in range(0, block, rows):
            row = first + part
            owner, inner = row // (m * piece), row % (m * piece)
            chunk, place = inner % piece // rows, 0
            for axis, bit, unused in orders[chunk % 2]:
                index = inner // piece if axis == "dp" else owner
                place = 2 * place + index // bit % 2
            acc[chunk, place] = product[part : part + rows]
    pl.semaphore_wait(barrier, len(friends))
    for c in range(chunks):
        copy(c, 0).start()
    rate_copy(0).start()
    for s in range(count):
        for c in range(chunks):
            copy(c, s).wait_recv()
            keep, give, size = starts[c % 2][s]
            value = acc[c, pl.ds(keep, size)] + got[c, pl.ds(offsets[s], size)]
            if s + 1 < count:
                acc[c, pl.ds(keep, size)] = value
                copy(c, s + 1).start()
            else:
                ring[0, c] = value[0]
                for k in range(1, m):
                    out_copy(c, k).start()
        rate_copy(s).wait_recv()
        r_acc[s + 1] = r_acc[s] + r_got[s]
        if s + 1 < count:
            rate_copy(s + 1).start()
    rate_out[...] = r_acc[count]
    for c in range(chunks):
        for k in range(m):
            if k > 0:
                out_copy(c, k).wait_recv()
            where = dp_peer(k)["dp"] if k > 0 else dp
            out_ref[pl.ds(where * piece + c * rows, rows)] = ring[k, c]
    for c in range(chunks):
        for s in range(count):
            copy(c, s).wait_send()
        for k in range(1, m):
            out_copy(c, k).wait_send()
    for s in range(count):
        rate_copy(s).wait_send()


def shards(layer_input, projection, ssm_input, step_logit, decay_rate, output_grad):
    tokens, x_rows, logit, grad_rows = layer_input[0], ssm_input[0], step_logit[0], output_grad[0]
    length, full = x_rows.shape
    heads = logit.shape[1]
    size = full // heads
    state = projection.shape[1] // 2
    groups = heads // HEADS
    width = HEADS * size
    count = lax.axis_size("seq")
    limit = 46 * 2**20
    away = pl.BlockSpec(memory_space=pltpu.HBM)
    vmem = pl.BlockSpec(memory_space=pltpu.VMEM)
    slots = pltpu.VMEM((groups, state, width), F32)
    rows_in = pltpu.VMEM((groups, length, width), F32)
    half = pltpu.VMEM((groups, state, width), BF16)
    square = pltpu.VMEM((length, length), F32)
    sums = pltpu.VMEM((length, state), F32)
    short = pltpu.VMEM((length, state), BF16)
    by_lane = pltpu.VMEM((length, 2 * heads), F32)
    cols = pltpu.VMEM((groups, length, 2 * heads), F32)
    strip = pltpu.VMEM((8, 2 * heads), F32)
    two = pltpu.VMEM((2, length, state), F32)
    members = lax.axis_size("dp")
    blocks = count * members
    piece = tokens.shape[1] // blocks
    levels = blocks.bit_length() - 1
    fused = piece % 128 == 0
    rows = pltpu.VMEM((length, full), BF16)
    scratch = (
        [rows, pltpu.VMEM(projection.shape, BF16), rows, rows]
        + [short] * 3
        + [cols] * 2
        + [pltpu.VMEM((groups, HEADS, length), F32), strip, strip, sums, sums]
        + [half] * 4
        + [square, square, sums, sums]
        + [by_lane, by_lane, pltpu.VMEM((heads, length), F32), two, two]
        + [rows_in] * 2
        + [slots] * 4
        + [pltpu.SemaphoreType.DMA((4,)), pltpu.SemaphoreType.DMA((2, 4))]
        + [pltpu.SemaphoreType.DMA((2, groups))] * 3
    )
    rate_shape = jax.ShapeDtypeStruct((8, 2 * heads), F32)
    weight_shape = jax.ShapeDtypeStruct((length, 2 * state), BF16)
    if fused:
        stages = count.bit_length() - 1
        others = members - 1
        scratch += [pltpu.VMEM((others, count, length, piece), F32)] * 2
        scratch += [
            pltpu.VMEM((count, piece, members * length), BF16),
            pltpu.VMEM((2, length, state), F32),
            pltpu.VMEM((others, 2, length, state), F32),
            pltpu.VMEM((2, members * length, state), BF16),
            pltpu.VMEM((2, count, piece, state), F32),
            pltpu.VMEM((2, count - 1, piece, state), F32),
            pltpu.VMEM((2, members, piece, state), F32),
            pltpu.VMEM((members, 8, 2 * heads), F32),
            pltpu.VMEM((stages, 8, 2 * heads), F32),
            pltpu.VMEM((stages + 1, 8, 2 * heads), F32),
            pltpu.SemaphoreType.DMA((2, others)),
            pltpu.SemaphoreType.DMA((2, 2 * others)),
            pltpu.SemaphoreType.DMA((2, 2 * (count - 1))),
            pltpu.SemaphoreType.DMA((2, 2 * members)),
            pltpu.SemaphoreType.DMA((2, others + stages)),
        ]
        rate_shape = jax.ShapeDtypeStruct((1, heads), F32)
        weight_shape = pltpu.VMEM((members * piece, 2 * state), F32)
    grad_x, grad_logit, rate_rows, weights = pl.pallas_call(
        functools.partial(layer_kernel, count, members, size, fused),
        in_specs=[away] * 4 + [vmem] * 2,
        out_specs=[vmem] * 4,
        out_shape=[
            rows,
            pltpu.VMEM((heads, length), F32),
            rate_shape,
            weight_shape,
        ],
        scratch_shapes=scratch,
        compiler_params=pltpu.CompilerParams(
            collective_id=0, has_side_effects=True, vmem_limit_bytes=limit
        ),
        name="layer_gradients",
    )(
        *(pltpu.with_memory_space_constraint(v, pltpu.HBM) for v in (tokens, projection, x_rows, grad_rows)),
        logit.T, decay_rate[None, :],
    )
    if fused:
        return (grad_x[None], grad_logit.T[None], rate_rows[0], weights)
    chunks = max(1, min(8, piece // 8))
    rows = piece // chunks
    weight_rows, rate_sum = pl.pallas_call(
        functools.partial(weight_kernel, count, members),
        in_specs=[vmem] * 3,
        out_specs=[vmem] * 2,
        out_shape=[
            jax.ShapeDtypeStruct((members * piece, 2 * state), F32),
            jax.ShapeDtypeStruct((8, 128), F32),
        ],
        scratch_shapes=[
            pltpu.VMEM((chunks, blocks, rows, 2 * state), F32),
            pltpu.VMEM((chunks, blocks, rows, 2 * state), F32),
            pltpu.VMEM((members, chunks, rows, 2 * state), F32),
            pltpu.VMEM((levels + 1, 8, 128), F32),
            pltpu.VMEM((levels, 8, 128), F32),
            pltpu.SemaphoreType.DMA((2, chunks, levels)),
            pltpu.SemaphoreType.DMA((2, chunks, members)),
            pltpu.SemaphoreType.DMA((2, levels)),
        ],
        compiler_params=pltpu.CompilerParams(
            collective_id=1, has_side_effects=True, vmem_limit_bytes=limit
        ),
        name="weight_gradient",
    )(tokens, weights, rate_rows)
    rate_sum = rate_sum[0, :heads]
    return (grad_x[None], grad_logit.T[None], rate_sum, weight_rows)


def solution(mesh):
    placed = (
        P("dp", "seq", None),
        P(),
        P("dp", "seq", None),
        P("dp", "seq", None),
        P(),
        P("dp", "seq", None),
    )
    return jax.shard_map(
        shards,
        mesh=mesh,
        in_specs=placed,
        out_specs=(P("dp", "seq", None), P("dp", "seq", None), P(), P("seq", None)),
        check_vma=False,
    )
```

```python
import functools

import jax
import jax.numpy as jnp
from jax import lax
from jax.experimental import pallas as pl
from jax.experimental.pallas import tpu as pltpu
from jax.sharding import PartitionSpec as P

F32 = jnp.float32
BF16 = jnp.bfloat16
HEADS = 2
LAG = 3
EARLY = 3
PARTS = 1


def dot(a, b, ca, cb):
    return lax.dot_general(a, b, (((ca,), (cb,)), ((), ())), preferred_element_type=F32)


def exact_dot(a, b, ca, cb):
    return lax.dot_general(
        a, b, (((ca,), (cb,)), ((), ())),
        preferred_element_type=F32, precision=lax.Precision.HIGHEST,
    )


def pair_columns(cols, j, size):
    lane = lax.broadcasted_iota(jnp.int32, (cols.shape[0], 2 * size), 1)
    return jnp.where(lane < size, cols[:, j : j + 1], cols[:, j + 1 : j + 2])


def flip(index, bits, limit):
    other, bit = index, 1
    while bit < limit:
        if bits & bit:
            other = other + bit - 2 * bit * lax.rem(lax.div(index, bit), 2)
        bit *= 2
    return other


def layer_kernel(
    n, m, size, fused, t_hbm, w_hbm, x_hbm, g_hbm, logit_hbm, rate_hbm,
    dx_ref, dlogit_ref, drate_ref, weight_ref, t_ref, w_ref, x_ref, g_ref, logit_ref, rate_ref,
    b_ref, c_ref, c_in, cols1, cols2, rows_ref, span, span_in, cf, cf_in,
    e_own, e_other, f_own, f_other, scores, d_scores, d_b, d_c,
    sums1, sums2, row_sums, back, back_in,
    gs_snd, gs_in, e_in, f_in, e_snd, f_snd,
    load_sem, small_sem, gs_sem, e_sem, f_sem, *more,
):
    if fused:
        (
            tok_snd, tok_in, tok, gbc_snd, gbc_in, gbc, acc, got, out, rate_dp, rate_got, rate_acc,
            tok_sem, gbc_sem, acc_sem, out_sem, rate_sem,
        ) = more
    chunks = gs_snd.shape[0]
    length, state = b_ref.shape
    heads = logit_ref.shape[0]
    width = HEADS * size
    nz = n // 2
    me = lax.axis_index("seq")
    odd = lax.rem(me, 2)
    z = lax.div(me, 2)
    partner = me + 1 - 2 * odd
    first, last = z == 0, z == nz - 1
    barrier = pltpu.get_barrier_semaphore()
    operands = (
        (logit_hbm, logit_ref), (rate_hbm, rate_ref),
        (g_hbm, g_ref), (t_hbm, t_ref), (w_hbm, w_ref), (x_hbm, x_ref),
    )
    load_logit, load_rate, load_g, load_t, load_w, load_x = (
        pltpu.make_async_copy(source, target, load_sem.at[i])
        for i, (source, target) in enumerate(operands)
    )

    def greet(who, axis="seq"):
        pl.semaphore_signal(
            barrier, inc=1, device_id={axis: who}, device_id_type=pl.DeviceIdType.MESH
        )

    load_logit.start()
    load_rate.start()
    load_g.start()
    load_t.start()
    load_w.start()
    load_x.start()
    greet(partner)
    pl.when(jnp.logical_not(first))(lambda: greet(me - 2))
    pl.when(jnp.logical_not(last))(lambda: greet(me + 2))
    greeters = 1
    if fused:
        for r in range(4, n, 2):
            greet(flip(me, r, n))
            greeters += 1
        for k in range(1, m):
            greet(flip(lax.axis_index("dp"), k, m), "dp")
            greeters += 1

    def send(src, dst, sems, k, who, axis="seq"):
        return pltpu.make_async_remote_copy(
            src_ref=src, dst_ref=dst, send_sem=sems.at[0, k], recv_sem=sems.at[1, k],
            device_id={axis: who}, device_id_type=pl.DeviceIdType.MESH,
        )

    def copy_span():
        return send(span, span_in, small_sem, 0, partner)

    def copy_c():
        return send(cf, cf_in, small_sem, 1, partner)

    def copy_back(i):
        return send(back.at[i], back_in.at[i], small_sem, 2 + i, partner)

    def copy_g(k):
        return send(gs_snd.at[k], gs_in.at[k], gs_sem, k, partner)

    part = state // PARTS

    def copy_e(k, i):
        rows = pl.ds(i * part, part)
        return send(e_snd.at[k, rows], e_in.at[k, rows], e_sem, PARTS * k + i, me + 2)

    def copy_f(k, i):
        rows = pl.ds(i * part, part)
        return send(f_snd.at[k, rows], f_in.at[k, rows], f_sem, PARTS * k + i, me - 2)

    def turn(value, k):
        lanes = value.shape[1]
        return pltpu.roll(value, lax.rem(lanes - HEADS * k, lanes), 1)

    def wide(k):
        return pl.ds(pl.multiple_of(k * width, width), width)

    load_logit.wait()
    load_rate.wait()
    logit, rate = logit_ref[...], rate_ref[...]
    dt_all = (jnp.maximum(logit, 0.0) + jnp.log1p(jnp.exp(-jnp.abs(logit)))).T
    row_at = lax.broadcasted_iota(jnp.int32, (length, length), 0)
    col_at = lax.broadcasted_iota(jnp.int32, (length, length), 1)
    until = (row_at >= col_at).astype(F32)
    log_decay = exact_dot(until, -rate * dt_all, 1, 0)
    to_end = jnp.exp(log_decay[length - 1 : length, :] - log_decay)
    grow_all = jnp.exp(log_decay)
    q1 = jnp.concatenate([log_decay, dt_all], axis=1)
    q2 = jnp.concatenate([to_end, grow_all], axis=1)
    span[...] = jnp.broadcast_to(q2[length - 1 : length, :], span.shape)
    def scale(k, unused):
        cols1[k] = turn(q1, k)
        cols = turn(q2, k)
        cols2[k] = cols
        gs_snd[k] = g_ref[:, wide(k)].astype(F32) * pair_columns(cols, heads, size)
        copy_g(k).start()
        return unused

    load_g.wait()
    end = jnp.logical_or(first, last)
    pl.when(end)(lambda: pl.semaphore_wait(barrier, min(nz - 1, 1) + greeters))
    pl.when(jnp.logical_not(end))(lambda: pl.semaphore_wait(barrier, 2 + greeters))
    copy_span().start()
    lax.fori_loop(0, EARLY, scale, 0)
    load_t.wait()
    load_w.wait()
    bc = dot(t_ref[...], w_ref[...], 1, 0).astype(BF16)
    b_ref[...] = bc[:, :state]
    c_ref[...] = bc[:, state:]
    cf[...] = bc[:, state:].astype(F32)
    copy_c().start()
    by_head = q1.T
    for k in range(chunks):
        rows_ref[k] = by_head[HEADS * k : HEADS * (k + 1), :]
    load_x.wait()
    scores[...] = dot(b_ref[...], c_ref[...], 1, 1)
    for ref in (d_scores, d_b, d_c, sums1, sums2, row_sums, back):
        ref[...] = jnp.zeros_like(ref)
    copy_span().wait_recv()
    copy_c().wait_recv()
    c_in[...] = cf_in[...].astype(BF16)

    def spans(ref, k):
        return pair_columns(turn(ref[...], k)[:1, :], heads, size)

    def forward(k):
        weight = pair_columns(cols1[k], heads, size) * pair_columns(cols2[k], 0, size)
        near = dot(b_ref[...], (x_ref[:, wide(k)].astype(F32) * weight).astype(BF16), 0, 0)
        mine, theirs = spans(span, k), spans(span_in, k)

        @pl.when(first)
        def _():
            e_in[k] = jnp.zeros_like(e_in[k])

        for i in range(PARTS):
            rows = slice(i * part, (i + 1) * part)
            pl.when(jnp.logical_not(first))(lambda: copy_e(k, i).wait_recv())
            value = e_in[k, rows]

            @pl.when(odd == 0)
            def _():
                e_own[k, rows] = value.astype(BF16)
                middle = mine * value + near[rows]
                e_other[k, rows] = middle.astype(BF16)
                e_snd[k, rows] = theirs * middle

            @pl.when(odd == 1)
            def _():
                e_other[k, rows] = value.astype(BF16)
                middle = theirs * value
                e_own[k, rows] = middle.astype(BF16)
                e_snd[k, rows] = mine * middle + near[rows]

            pl.when(jnp.logical_not(last))(lambda: copy_e(k, i).start())

    def backward(k):
        copy_g(k).wait_recv()
        near = dot(c_ref[...], gs_snd[k].astype(BF16), 0, 0)
        far = dot(c_in[...], gs_in[k].astype(BF16), 0, 0)
        mine, theirs = spans(span, k), spans(span_in, k)

        @pl.when(last)
        def _():
            f_in[k] = jnp.zeros_like(f_in[k])

        for i in range(PARTS):
            rows = slice(i * part, (i + 1) * part)
            pl.when(jnp.logical_not(last))(lambda: copy_f(k, i).wait_recv())
            value = f_in[k, rows]

            @pl.when(odd == 0)
            def _():
                f_other[k, rows] = value.astype(BF16)
                middle = theirs * value + far[rows]
                f_own[k, rows] = middle.astype(BF16)
                f_snd[k, rows] = mine * middle + near[rows]

            @pl.when(odd == 1)
            def _():
                f_own[k, rows] = value.astype(BF16)
                middle = mine * value + near[rows]
                f_other[k, rows] = middle.astype(BF16)
                f_snd[k, rows] = theirs * middle + far[rows]

            pl.when(jnp.logical_not(first))(lambda: copy_f(k, i).start())

    def gradients(k):
        cols, rows = cols1[k], rows_ref[k]
        k_st = scores[...]
        causal = col_at >= row_at
        low = lax.broadcasted_iota(jnp.int32, (length, width), 1) < size
        place = lax.broadcasted_iota(jnp.int32, sums1.shape, 1) - k * HEADS
        row_place = lax.broadcasted_iota(jnp.int32, row_sums.shape, 0) - k * HEADS
        res1, res2, res3, res_rows = sums1[...], sums2[...], back[1], row_sums[...]
        q_sum = d_scores[...]
        x2, g2 = x_ref[:, wide(k)], g_ref[:, wide(k)]
        x2f = x2.astype(F32)
        e2, f2, e3, f3 = e_own[k], f_own[k], e_other[k], f_other[k]
        gs, gs3 = gs_snd[k], gs_in[k]
        dt2 = pair_columns(cols, heads, size)
        end2 = pair_columns(cols2[k], 0, size)
        g_low = jnp.where(low, g2, jnp.zeros_like(g2))
        g_high = jnp.where(low, jnp.zeros_like(g2), g2)
        g_both = jnp.concatenate([g_low, g_high], axis=0)
        gram = dot(x2, g_both, 1, 1)
        weights = []
        for h in range(HEADS):
            gap = rows[h : h + 1, :] - cols[:, h : h + 1]
            decay = jnp.exp(jnp.where(causal, gap, -jnp.inf))
            mg = decay * gram[:, h * length : (h + 1) * length]
            dt = cols[:, heads + h : heads + h + 1]
            q_sum = q_sum + mg * dt
            raw = mg * k_st
            res_rows = jnp.where(row_place == h, jnp.sum(raw * dt, axis=0, keepdims=True), res_rows)
            res1 = jnp.where(place == h, jnp.sum(raw, axis=1, keepdims=True), res1)
            weights.append((decay * k_st).astype(BF16))
        z2 = dot(jnp.concatenate(weights, axis=1), g_both, 1, 0)
        z_in = dot(b_ref[...], f2, 1, 0) * end2
        dx_ref[:, wide(k)] = (dt2 * (z2 + z_in)).astype(dx_ref.dtype)
        xz = x2f * z_in
        gy = gs * dot(c_ref[...], e2, 1, 0)
        gy3 = gs3 * dot(c_in[...], e3, 1, 0)
        ef = jnp.sum(e2.astype(F32) * f2.astype(F32), axis=0, keepdims=True)
        ef3 = jnp.sum(e3.astype(F32) * f3.astype(F32), axis=0, keepdims=True)
        low_row = low[:1, :]

        def half(value, h, mask):
            keep = mask if h == 0 else jnp.logical_not(mask)
            return jnp.sum(jnp.where(keep, value, jnp.zeros_like(value)), axis=1, keepdims=True)

        for h in range(HEADS):
            res1 = jnp.where(place == h + heads, half(xz, h, low), res1)
            res2 = jnp.where(place == h, half(gy, h, low), res2)
            res2 = jnp.where(place == h + heads, half(ef, h, low_row), res2)
            res3 = jnp.where(place == h, half(gy3, h, low), res3)
            res3 = jnp.where(place == h + heads, half(ef3, h, low_row), res3)
        sums1[...] = res1
        sums2[...] = res2
        back[1] = res3
        row_sums[...] = res_rows
        d_scores[...] = q_sum
        d_b[...] += dot((x2f * (end2 * dt2)).astype(BF16), f2, 1, 1)
        d_c[...] += dot(gs.astype(BF16), e2, 1, 1)
        back[0] += dot(gs3.astype(BF16), e3, 1, 1)

    delay = LAG * lax.max(z, nz - 1 - z)

    def step(t, unused):
        @pl.when(t + EARLY < chunks)
        def _():
            scale(t + EARLY, 0)

        kf = t - LAG * z

        pl.when(jnp.logical_and(kf >= 0, kf < chunks))(lambda: forward(kf))
        kb = t - LAG * (nz - 1 - z)
        pl.when(jnp.logical_and(kb >= 0, kb < chunks))(lambda: backward(kb))
        kg = t - delay
        pl.when(jnp.logical_and(kg >= 0, kg < chunks))(lambda: gradients(kg))
        return unused

    if fused:
        dp = lax.axis_index("dp")
        piece = tok.shape[1]

        def columns(s, k):
            first_column = (s * m + flip(dp, k, m)) * piece
            return t_ref[:, pl.ds(pl.multiple_of(first_column, piece), piece)].astype(F32)

        def copy_tokens(k):
            return send(
                tok_snd.at[k - 1], tok_in.at[k - 1], tok_sem, k - 1, flip(dp, k, m), "dp"
            )

        def copy_gbc(i, k):
            return send(
                gbc_snd.at[i], gbc_in.at[k - 1, i], gbc_sem, (m - 1) * i + k - 1,
                flip(dp, k, m), "dp",
            )

        def copy_acc(i, r):
            who = partner if r % 2 else flip(me, r, n)
            return send(acc.at[i, r], got.at[i, r - 1], acc_sem, (n - 1) * i + r - 1, who)

        def copy_out(i, k):
            return send(
                out.at[i, 0], out.at[i, k], out_sem, m * i + k, flip(dp, k, m), "dp"
            )

        def copy_rate_dp(k):
            return send(
                rate_dp.at[0], rate_dp.at[k], rate_sem, k - 1, flip(dp, k, m), "dp"
            )

        def copy_rate_x():
            return send(rate_acc.at[0], rate_got.at[0], rate_sem, m - 1, partner)

        def copy_rate_z(j):
            return send(rate_acc.at[1], rate_got.at[j], rate_sem, m - 1 + j, flip(me, 2 * j, n))

        def tree(parts):
            while len(parts) > 1:
                parts = [p + q for p, q in zip(parts[::2], parts[1::2])]
            return parts[0]

        def spread(s, unused):
            for k in range(1, m):
                tok_snd[k - 1, s] = columns(s, k)
            return unused

        lax.fori_loop(0, n, spread, 0)
        for k in range(1, m):
            copy_tokens(k).start()

    lax.fori_loop(0, chunks + delay, step, 0)
    copy_back(0).start()
    copy_back(1).start()
    dk = d_scores[...].astype(BF16)
    grad_b = (d_b[...] + dot(dk, c_ref[...], 1, 0)).astype(BF16)
    if fused:
        gbc_snd[0] = grad_b.astype(F32)
        for k in range(1, m):
            copy_gbc(0, k).start()
        gbc[0, :length] = grad_b
    else:
        weight_ref[:, :state] = grad_b
    c_total = d_c[...] + dot(dk, b_ref[...], 0, 0)
    copy_back(0).wait_recv()
    grad_c = (c_total + back_in[0]).astype(BF16)
    if fused:
        gbc_snd[1] = grad_c.astype(F32)
        for k in range(1, m):
            copy_gbc(1, k).start()
        gbc[1, :length] = grad_c
        for k in range(1, m):
            copy_tokens(k).wait_recv()

        def place_tokens(r, unused):
            s = r
            for k in range(m):
                block = columns(s, k) if k == 0 else tok_in[k - 1, s]
                tok[s, :, k * length : (k + 1) * length] = block.T.astype(BF16)
            return unused

        lax.fori_loop(0, n, place_tokens, 0)
        order = list(range(n - 2, -1, -2))
        for i in range(2):
            for k in range(1, m):
                copy_gbc(i, k).wait_recv()
                gbc[i, k * length : (k + 1) * length] = gbc_in[k - 1, i].astype(BF16)
            for r in [r + 1 for r in order] + order:
                acc[i, r] = dot(tok[flip(me, r, n)], gbc[i], 1, 0)
                if r % 2:
                    copy_acc(i, r).start()
    else:
        weight_ref[:, state:] = grad_c
    copy_back(1).wait_recv()
    total = sums2[...] + back_in[1]
    inside, x_in = sums1[:, :heads], sums1[:, heads:]
    g_in, both = total[:, :heads], span[:1, heads:] * total[:, heads:]
    dt_all = cols1[0, :, heads:]
    after = (row_at <= col_at).astype(F32)
    before = (row_at > col_at).astype(F32)
    d_log = (
        both
        + exact_dot(before, dt_all * x_in, 1, 0)
        + exact_dot(after, g_in - dt_all * inside, 1, 0)
        + exact_dot(after, row_sums[...], 1, 1)
    )
    d_rate = -jnp.sum(dt_all * d_log, axis=0, keepdims=True)
    d_rate = jnp.broadcast_to(
        jnp.concatenate([d_rate, jnp.zeros_like(d_rate)], axis=1), (8, 2 * heads)
    )
    if fused:
        rate_dp[0] = d_rate
        for k in range(1, m):
            copy_rate_dp(k).start()
    else:
        drate_ref[...] = d_rate
    d_step = inside + x_in - rate_ref[...] * d_log
    dlogit_ref[...] = d_step.T * jax.nn.sigmoid(logit_ref[...])
    if fused:

        def join(i, r):
            copy_acc(i, r + 1).wait_recv()
            acc[i, r] += got[i, r]
            if r:
                copy_acc(i, r).start()

        def finish(i):
            value = acc[i, 0]
            for r in order[:-1]:
                copy_acc(i, r).wait_recv()
                value += got[i, r - 1]
            out[i, 0] = value
            for k in range(1, m):
                copy_out(i, k).start()

        for r in order:
            join(0, r)
        for k in range(1, m):
            copy_rate_dp(k).wait_recv()
        rate_acc[0] = tree([rate_dp[k] for k in range(m)])
        copy_rate_x().start()
        for r in order[: len(order) // 2]:
            join(1, r)
        finish(0)
        copy_rate_x().wait_recv()
        rate_acc[1] = rate_acc[0] + rate_got[0]
        for j in range(1, nz):
            copy_rate_z(j).start()
        for r in order[len(order) // 2 :]:
            join(1, r)
        finish(1)
        for j in range(1, nz):
            copy_rate_z(j).wait_recv()
        drate_ref[...] = tree([rate_acc[1]] + [rate_got[j] for j in range(1, nz)])[:1, :heads]
        for i in range(2):
            for k in range(m):
                if k:
                    copy_out(i, k).wait_recv()
                first_row = pl.multiple_of(flip(dp, k, m) * piece, piece)
                weight_ref[pl.ds(first_row, piece), i * state : (i + 1) * state] = out[i, k]
        for k in range(1, m):
            copy_tokens(k).wait_send()
            copy_rate_dp(k).wait_send()
            for i in range(2):
                copy_gbc(i, k).wait_send()
                copy_out(i, k).wait_send()
        for i in range(2):
            for r in range(1, n):
                copy_acc(i, r).wait_send()
        copy_rate_x().wait_send()
        for j in range(1, nz):
            copy_rate_z(j).wait_send()
    copy_span().wait_send()
    copy_c().wait_send()
    copy_back(0).wait_send()
    copy_back(1).wait_send()

    def settle(k, unused):
        copy_g(k).wait_send()
        for i in range(PARTS):
            pl.when(jnp.logical_not(last))(lambda: copy_e(k, i).wait_send())
            pl.when(jnp.logical_not(first))(lambda: copy_f(k, i).wait_send())
        return unused

    lax.fori_loop(0, chunks, settle, 0)


def store_kernel(*refs):
    copies = [pltpu.make_async_copy(refs[i], refs[4 + i], refs[8].at[i]) for i in range(4)]
    for copy in copies:
        copy.start()
    for copy in copies:
        copy.wait()


def weight_kernel(
    n, m, t_ref, g_ref, rate_ref, out_ref, rate_out,
    acc, got, ring, r_acc, r_got, sem, out_sem, r_sem,
):
    chunks, blocks, rows = acc.shape[0], acc.shape[1], acc.shape[2]
    piece = chunks * rows
    seq, dp = lax.axis_index("seq"), lax.axis_index("dp")
    dp_steps, seq_steps, bit = [], [], 1
    while bit < m:
        dp_steps.append(("dp", bit, lax.rem(lax.div(dp, bit), 2)))
        bit *= 2
    bit = 1
    while bit < n:
        seq_steps.append(("seq", bit, lax.rem(lax.div(seq, bit), 2)))
        bit *= 2
    count = len(dp_steps) + len(seq_steps)
    orders = (dp_steps + seq_steps, dp_steps[:1] + seq_steps + dp_steps[1:])

    def peer(c, s):
        axis, bit, mine = orders[c % 2][s]
        return {axis: lax.axis_index(axis) + bit - 2 * bit * mine}

    def dp_peer(k):
        other, bit = dp, 1
        while bit < m:
            if k & bit:
                other = other + bit - 2 * bit * lax.rem(lax.div(dp, bit), 2)
            bit *= 2
        return {"dp": other}

    barrier = pltpu.get_barrier_semaphore()
    friends = [dp_peer(k) for k in range(1, m)] + [
        peer(0, s) for s in range(len(dp_steps), count)
    ]
    for friend in friends:
        pl.semaphore_signal(
            barrier, inc=1, device_id=friend, device_id_type=pl.DeviceIdType.MESH
        )

    starts, offsets = [], []
    for order in orders:
        base, width, total = 0, blocks, 0
        starts.append([])
        for unused, unused, mine in order:
            width //= 2
            starts[-1].append((base + width * mine, base + width * (1 - mine), width))
            base = base + width * mine
            if len(starts) == 1:
                offsets.append(total)
                total += width

    def copy(c, s):
        keep, give, size = starts[c % 2][s]
        return pltpu.make_async_remote_copy(
            src_ref=acc.at[c, pl.ds(give, size)],
            dst_ref=got.at[c, pl.ds(offsets[s], size)],
            send_sem=sem.at[0, c, s], recv_sem=sem.at[1, c, s],
            device_id=peer(c, s), device_id_type=pl.DeviceIdType.MESH,
        )

    def rate_copy(s):
        return pltpu.make_async_remote_copy(
            src_ref=r_acc.at[s], dst_ref=r_got.at[s],
            send_sem=r_sem.at[0, s], recv_sem=r_sem.at[1, s],
            device_id=peer(0, s), device_id_type=pl.DeviceIdType.MESH,
        )

    def out_copy(c, k):
        return pltpu.make_async_remote_copy(
            src_ref=ring.at[0, c], dst_ref=ring.at[k, c],
            send_sem=out_sem.at[0, c, k], recv_sem=out_sem.at[1, c, k],
            device_id=dp_peer(k), device_id_type=pl.DeviceIdType.MESH,
        )

    g = g_ref[...]
    r_acc[0] = rate_ref[...]
    block = 128
    for first in range(0, t_ref.shape[1], block):
        product = dot(t_ref[:, first : first + block], g, 0, 0)
        for part in range(0, block, rows):
            row = first + part
            owner, inner = row // (m * piece), row % (m * piece)
            chunk, place = inner % piece // rows, 0
            for axis, bit, unused in orders[chunk % 2]:
                index = inner // piece if axis == "dp" else owner
                place = 2 * place + index // bit % 2
            acc[chunk, place] = product[part : part + rows]
    pl.semaphore_wait(barrier, len(friends))
    for c in range(chunks):
        copy(c, 0).start()
    rate_copy(0).start()
    for s in range(count):
        for c in range(chunks):
            copy(c, s).wait_recv()
            keep, give, size = starts[c % 2][s]
            value = acc[c, pl.ds(keep, size)] + got[c, pl.ds(offsets[s], size)]
            if s + 1 < count:
                acc[c, pl.ds(keep, size)] = value
                copy(c, s + 1).start()
            else:
                ring[0, c] = value[0]
                for k in range(1, m):
                    out_copy(c, k).start()
        rate_copy(s).wait_recv()
        r_acc[s + 1] = r_acc[s] + r_got[s]
        if s + 1 < count:
            rate_copy(s + 1).start()
    rate_out[...] = r_acc[count]
    for c in range(chunks):
        for k in range(m):
            if k > 0:
                out_copy(c, k).wait_recv()
            where = dp_peer(k)["dp"] if k > 0 else dp
            out_ref[pl.ds(where * piece + c * rows, rows)] = ring[k, c]
    for c in range(chunks):
        for s in range(count):
            copy(c, s).wait_send()
        for k in range(1, m):
            out_copy(c, k).wait_send()
    for s in range(count):
        rate_copy(s).wait_send()


def shards(layer_input, projection, ssm_input, step_logit, decay_rate, output_grad):
    tokens, x_rows, logit, grad_rows = layer_input[0], ssm_input[0], step_logit[0], output_grad[0]
    length, full = x_rows.shape
    heads = logit.shape[1]
    size = full // heads
    state = projection.shape[1] // 2
    groups = heads // HEADS
    width = HEADS * size
    count = lax.axis_size("seq")
    limit = 46 * 2**20
    away = pl.BlockSpec(memory_space=pltpu.HBM)
    vmem = pl.BlockSpec(memory_space=pltpu.VMEM)
    slots = pltpu.VMEM((groups, state, width), F32)
    rows_in = pltpu.VMEM((groups, length, width), F32)
    half = pltpu.VMEM((groups, state, width), BF16)
    square = pltpu.VMEM((length, length), F32)
    sums = pltpu.VMEM((length, state), F32)
    short = pltpu.VMEM((length, state), BF16)
    by_lane = pltpu.VMEM((length, 2 * heads), F32)
    cols = pltpu.VMEM((groups, length, 2 * heads), F32)
    strip = pltpu.VMEM((8, 2 * heads), F32)
    two = pltpu.VMEM((2, length, state), F32)
    members = lax.axis_size("dp")
    blocks = count * members
    piece = tokens.shape[1] // blocks
    levels = blocks.bit_length() - 1
    fused = piece % 128 == 0
    rows = pltpu.VMEM((length, full), BF16)
    scratch = (
        [rows, pltpu.VMEM(projection.shape, BF16), rows, rows]
        + [pltpu.VMEM((heads, length), F32), pltpu.VMEM((1, heads), F32)]
        + [short] * 3
        + [cols] * 2
        + [pltpu.VMEM((groups, HEADS, length), F32), strip, strip, sums, sums]
        + [half] * 4
        + [square, square, sums, sums]
        + [by_lane, by_lane, pltpu.VMEM((heads, length), F32), two, two]
        + [rows_in] * 2
        + [slots] * 4
        + [pltpu.SemaphoreType.DMA((6,)), pltpu.SemaphoreType.DMA((2, 4))]
        + [pltpu.SemaphoreType.DMA((2, groups))]
        + [pltpu.SemaphoreType.DMA((2, PARTS * groups))] * 2
    )
    rate_shape = jax.ShapeDtypeStruct((8, 2 * heads), F32)
    weight_shape = jax.ShapeDtypeStruct((length, 2 * state), BF16)
    if fused:
        pairs = count // 2
        others = members - 1
        scratch += [pltpu.VMEM((others, count, length, piece), F32)] * 2
        scratch += [
            pltpu.VMEM((count, piece, members * length), BF16),
            pltpu.VMEM((2, length, state), F32),
            pltpu.VMEM((others, 2, length, state), F32),
            pltpu.VMEM((2, members * length, state), BF16),
            pltpu.VMEM((2, count, piece, state), F32),
            pltpu.VMEM((2, count - 1, piece, state), F32),
            pltpu.VMEM((2, members, piece, state), F32),
            pltpu.VMEM((members, 8, 2 * heads), F32),
            pltpu.VMEM((pairs, 8, 2 * heads), F32),
            pltpu.VMEM((2, 8, 2 * heads), F32),
            pltpu.SemaphoreType.DMA((2, others)),
            pltpu.SemaphoreType.DMA((2, 2 * others)),
            pltpu.SemaphoreType.DMA((2, 2 * (count - 1))),
            pltpu.SemaphoreType.DMA((2, 2 * members)),
            pltpu.SemaphoreType.DMA((2, others + pairs)),
        ]
        rate_shape = pltpu.VMEM((1, heads), F32)
        weight_shape = pltpu.VMEM((members * piece, 2 * state), F32)
    grad_x, grad_logit, rate_rows, weights = pl.pallas_call(
        functools.partial(layer_kernel, count, members, size, fused),
        in_specs=[away] * 6,
        out_specs=[vmem] * 4,
        out_shape=[
            rows,
            pltpu.VMEM((heads, length), F32),
            rate_shape,
            weight_shape,
        ],
        scratch_shapes=scratch,
        compiler_params=pltpu.CompilerParams(
            collective_id=0, has_side_effects=True, vmem_limit_bytes=limit
        ),
        name="layer_gradients",
    )(
        *(
            pltpu.with_memory_space_constraint(v, pltpu.HBM)
            for v in (tokens, projection, x_rows, grad_rows, logit.T, decay_rate[None, :])
        )
    )
    if fused:
        results = (grad_x, grad_logit, rate_rows, weights)
        grad_x, grad_logit, rate_rows, weights = pl.pallas_call(
            store_kernel,
            in_specs=[vmem] * 4,
            out_specs=[away] * 4,
            out_shape=[jax.ShapeDtypeStruct(v.shape, v.dtype) for v in results],
            scratch_shapes=[pltpu.SemaphoreType.DMA((4,))],
            name="store_results",
        )(*results)
        return (grad_x[None], grad_logit.T[None], rate_rows[0], weights)
    chunks = max(1, min(8, piece // 8))
    rows = piece // chunks
    weight_rows, rate_sum = pl.pallas_call(
        functools.partial(weight_kernel, count, members),
        in_specs=[vmem] * 3,
        out_specs=[vmem] * 2,
        out_shape=[
            jax.ShapeDtypeStruct((members * piece, 2 * state), F32),
            jax.ShapeDtypeStruct((8, 128), F32),
        ],
        scratch_shapes=[
            pltpu.VMEM((chunks, blocks, rows, 2 * state), F32),
            pltpu.VMEM((chunks, blocks, rows, 2 * state), F32),
            pltpu.VMEM((members, chunks, rows, 2 * state), F32),
            pltpu.VMEM((levels + 1, 8, 128), F32),
            pltpu.VMEM((levels, 8, 128), F32),
            pltpu.SemaphoreType.DMA((2, chunks, levels)),
            pltpu.SemaphoreType.DMA((2, chunks, members)),
            pltpu.SemaphoreType.DMA((2, levels)),
        ],
        compiler_params=pltpu.CompilerParams(
            collective_id=1, has_side_effects=True, vmem_limit_bytes=limit
        ),
        name="weight_gradient",
    )(tokens, weights, rate_rows)
    rate_sum = rate_sum[0, :heads]
    return (grad_x[None], grad_logit.T[None], rate_sum, weight_rows)


def solution(mesh):
    placed = (
        P("dp", "seq", None),
        P(),
        P("dp", "seq", None),
        P("dp", "seq", None),
        P(),
        P("dp", "seq", None),
    )
    return jax.shard_map(
        shards,
        mesh=mesh,
        in_specs=placed,
        out_specs=(P("dp", "seq", None), P("dp", "seq", None), P(), P("seq", None)),
        check_vma=False,
    )
```

```python
import functools

import jax
import jax.numpy as jnp
from jax import lax
from jax.experimental import pallas as pl
from jax.experimental.pallas import tpu as pltpu
from jax.sharding import PartitionSpec as P

F32 = jnp.float32
BF16 = jnp.bfloat16
HEADS = 2
LAG = 3
EARLY = 3
PARTS = 1


def dot(a, b, ca, cb):
    return lax.dot_general(a, b, (((ca,), (cb,)), ((), ())), preferred_element_type=F32)


def exact_dot(a, b, ca, cb):
    return lax.dot_general(
        a, b, (((ca,), (cb,)), ((), ())),
        preferred_element_type=F32, precision=lax.Precision.HIGHEST,
    )


def pair_columns(cols, j, size):
    lane = lax.broadcasted_iota(jnp.int32, (cols.shape[0], 2 * size), 1)
    return jnp.where(lane < size, cols[:, j : j + 1], cols[:, j + 1 : j + 2])


def flip(index, bits, limit):
    other, bit = index, 1
    while bit < limit:
        if bits & bit:
            other = other + bit - 2 * bit * lax.rem(lax.div(index, bit), 2)
        bit *= 2
    return other


def layer_kernel(
    n, m, size, fused, t_hbm, w_hbm, x_hbm, g_hbm, logit_hbm, rate_hbm,
    dx_ref, dlogit_ref, drate_ref, weight_ref, t_ref, w_ref, x_ref, g_ref, logit_ref, rate_ref,
    b_ref, c_ref, c_in, cols1, cols2, rows_ref, span, span_in, cf, cf_in,
    e_own, e_other, f_own, f_other, scores, d_scores, d_b, d_c,
    sums1, sums2, row_sums, back, back_in,
    gs_snd, gs_in, e_in, f_in, e_snd, f_snd,
    load_sem, small_sem, gs_sem, e_sem, f_sem, *more,
):
    if fused:
        (
            tok_snd, tok_in, tok, gbc_snd, gbc_in, gbc, acc, got, out, rate_dp, rate_got, rate_acc,
            tok_sem, gbc_sem, acc_sem, out_sem, rate_sem,
        ) = more
    chunks = gs_snd.shape[0]
    length, state = b_ref.shape
    heads = logit_ref.shape[0]
    width = HEADS * size
    nz = n // 2
    me = lax.axis_index("seq")
    odd = lax.rem(me, 2)
    z = lax.div(me, 2)
    partner = me + 1 - 2 * odd
    first, last = z == 0, z == nz - 1
    barrier = pltpu.get_barrier_semaphore()
    operands = (
        (logit_hbm, logit_ref), (rate_hbm, rate_ref),
        (g_hbm, g_ref), (t_hbm, t_ref), (w_hbm, w_ref), (x_hbm, x_ref),
    )
    load_logit, load_rate, load_g, load_t, load_w, load_x = (
        pltpu.make_async_copy(source, target, load_sem.at[i])
        for i, (source, target) in enumerate(operands)
    )

    def greet(who, axis="seq"):
        pl.semaphore_signal(
            barrier, inc=1, device_id={axis: who}, device_id_type=pl.DeviceIdType.MESH
        )

    load_logit.start()
    load_rate.start()
    load_g.start()
    load_t.start()
    load_w.start()
    load_x.start()
    greet(partner)
    pl.when(jnp.logical_not(first))(lambda: greet(me - 2))
    pl.when(jnp.logical_not(last))(lambda: greet(me + 2))
    greeters = 1
    if fused:
        for r in range(4, n, 2):
            greet(flip(me, r, n))
            greeters += 1
        for k in range(1, m):
            greet(flip(lax.axis_index("dp"), k, m), "dp")
            greeters += 1

    def send(src, dst, sems, k, who, axis="seq"):
        return pltpu.make_async_remote_copy(
            src_ref=src, dst_ref=dst, send_sem=sems.at[0, k], recv_sem=sems.at[1, k],
            device_id={axis: who}, device_id_type=pl.DeviceIdType.MESH,
        )

    def copy_span():
        return send(span, span_in, small_sem, 0, partner)

    def copy_c():
        return send(cf, cf_in, small_sem, 1, partner)

    def copy_back(i):
        return send(back.at[i], back_in.at[i], small_sem, 2 + i, partner)

    def copy_g(k):
        return send(gs_snd.at[k], gs_in.at[k], gs_sem, k, partner)

    part = state // PARTS

    def copy_e(k, i):
        rows = pl.ds(i * part, part)
        return send(e_snd.at[k, rows], e_in.at[k, rows], e_sem, PARTS * k + i, me + 2)

    def copy_f(k, i):
        rows = pl.ds(i * part, part)
        return send(f_snd.at[k, rows], f_in.at[k, rows], f_sem, PARTS * k + i, me - 2)

    def turn(value, k):
        lanes = value.shape[1]
        return pltpu.roll(value, lax.rem(lanes - HEADS * k, lanes), 1)

    def wide(k):
        return pl.ds(pl.multiple_of(k * width, width), width)

    load_logit.wait()
    load_rate.wait()
    logit, rate = logit_ref[...], rate_ref[...]
    dt_all = (jnp.maximum(logit, 0.0) + jnp.log1p(jnp.exp(-jnp.abs(logit)))).T
    row_at = lax.broadcasted_iota(jnp.int32, (length, length), 0)
    col_at = lax.broadcasted_iota(jnp.int32, (length, length), 1)
    until = (row_at >= col_at).astype(F32)
    log_decay = exact_dot(until, -rate * dt_all, 1, 0)
    to_end = jnp.exp(log_decay[length - 1 : length, :] - log_decay)
    grow_all = jnp.exp(log_decay)
    q1 = jnp.concatenate([log_decay, dt_all], axis=1)
    q2 = jnp.concatenate([to_end, grow_all], axis=1)
    span[...] = jnp.broadcast_to(q2[length - 1 : length, :], span.shape)
    def scale(k, unused):
        cols1[k] = turn(q1, k)
        cols = turn(q2, k)
        cols2[k] = cols
        gs_snd[k] = g_ref[:, wide(k)].astype(F32) * pair_columns(cols, heads, size)
        copy_g(k).start()
        return unused

    load_g.wait()
    end = jnp.logical_or(first, last)
    pl.when(end)(lambda: pl.semaphore_wait(barrier, min(nz - 1, 1) + greeters))
    pl.when(jnp.logical_not(end))(lambda: pl.semaphore_wait(barrier, 2 + greeters))
    copy_span().start()
    lax.fori_loop(0, EARLY, scale, 0)
    load_t.wait()
    load_w.wait()
    bc = dot(t_ref[...], w_ref[...], 1, 0).astype(BF16)
    b_ref[...] = bc[:, :state]
    c_ref[...] = bc[:, state:]
    cf[...] = bc[:, state:].astype(F32)
    copy_c().start()
    by_head = q1.T
    for k in range(chunks):
        rows_ref[k] = by_head[HEADS * k : HEADS * (k + 1), :]
    load_x.wait()
    scores[...] = dot(b_ref[...], c_ref[...], 1, 1)
    for ref in (d_scores, d_b, d_c, sums1, sums2, row_sums, back):
        ref[...] = jnp.zeros_like(ref)
    copy_span().wait_recv()
    copy_c().wait_recv()
    c_in[...] = cf_in[...].astype(BF16)

    def spans(ref, k):
        return pair_columns(turn(ref[...], k)[:1, :], heads, size)

    def forward(k):
        weight = pair_columns(cols1[k], heads, size) * pair_columns(cols2[k], 0, size)
        near = dot(b_ref[...], (x_ref[:, wide(k)].astype(F32) * weight).astype(BF16), 0, 0)
        mine, theirs = spans(span, k), spans(span_in, k)

        @pl.when(first)
        def _():
            e_in[k] = jnp.zeros_like(e_in[k])

        for i in range(PARTS):
            rows = slice(i * part, (i + 1) * part)
            pl.when(jnp.logical_not(first))(lambda: copy_e(k, i).wait_recv())
            value = e_in[k, rows]

            @pl.when(odd == 0)
            def _():
                e_own[k, rows] = value.astype(BF16)
                middle = mine * value + near[rows]
                e_other[k, rows] = middle.astype(BF16)
                e_snd[k, rows] = theirs * middle

            @pl.when(odd == 1)
            def _():
                e_other[k, rows] = value.astype(BF16)
                middle = theirs * value
                e_own[k, rows] = middle.astype(BF16)
                e_snd[k, rows] = mine * middle + near[rows]

            pl.when(jnp.logical_not(last))(lambda: copy_e(k, i).start())

    def backward(k):
        copy_g(k).wait_recv()
        near = dot(c_ref[...], gs_snd[k].astype(BF16), 0, 0)
        far = dot(c_in[...], gs_in[k].astype(BF16), 0, 0)
        mine, theirs = spans(span, k), spans(span_in, k)

        @pl.when(last)
        def _():
            f_in[k] = jnp.zeros_like(f_in[k])

        for i in range(PARTS):
            rows = slice(i * part, (i + 1) * part)
            pl.when(jnp.logical_not(last))(lambda: copy_f(k, i).wait_recv())
            value = f_in[k, rows]

            @pl.when(odd == 0)
            def _():
                f_other[k, rows] = value.astype(BF16)
                middle = theirs * value + far[rows]
                f_own[k, rows] = middle.astype(BF16)
                f_snd[k, rows] = mine * middle + near[rows]

            @pl.when(odd == 1)
            def _():
                f_own[k, rows] = value.astype(BF16)
                middle = mine * value + near[rows]
                f_other[k, rows] = middle.astype(BF16)
                f_snd[k, rows] = theirs * middle + far[rows]

            pl.when(jnp.logical_not(first))(lambda: copy_f(k, i).start())

    def gradients(k):
        cols, rows = cols1[k], rows_ref[k]
        k_st = scores[...]
        causal = col_at >= row_at
        low = lax.broadcasted_iota(jnp.int32, (length, width), 1) < size
        place = lax.broadcasted_iota(jnp.int32, sums1.shape, 1) - k * HEADS
        row_place = lax.broadcasted_iota(jnp.int32, row_sums.shape, 0) - k * HEADS
        res1, res2, res3, res_rows = sums1[...], sums2[...], back[1], row_sums[...]
        q_sum = d_scores[...]
        x2, g2 = x_ref[:, wide(k)], g_ref[:, wide(k)]
        x2f = x2.astype(F32)
        e2, f2, e3, f3 = e_own[k], f_own[k], e_other[k], f_other[k]
        gs, gs3 = gs_snd[k], gs_in[k]
        dt2 = pair_columns(cols, heads, size)
        end2 = pair_columns(cols2[k], 0, size)
        g_low = jnp.where(low, g2, jnp.zeros_like(g2))
        g_high = jnp.where(low, jnp.zeros_like(g2), g2)
        g_both = jnp.concatenate([g_low, g_high], axis=0)
        gram = dot(x2, g_both, 1, 1)
        weights = []
        for h in range(HEADS):
            gap = rows[h : h + 1, :] - cols[:, h : h + 1]
            decay = jnp.exp(jnp.where(causal, gap, -jnp.inf))
            mg = decay * gram[:, h * length : (h + 1) * length]
            dt = cols[:, heads + h : heads + h + 1]
            q_sum = q_sum + mg * dt
            raw = mg * k_st
            res_rows = jnp.where(row_place == h, jnp.sum(raw * dt, axis=0, keepdims=True), res_rows)
            res1 = jnp.where(place == h, jnp.sum(raw, axis=1, keepdims=True), res1)
            weights.append((decay * k_st).astype(BF16))
        z2 = dot(jnp.concatenate(weights, axis=1), g_both, 1, 0)
        z_in = dot(b_ref[...], f2, 1, 0) * end2
        dx_ref[:, wide(k)] = (dt2 * (z2 + z_in)).astype(dx_ref.dtype)
        xz = x2f * z_in
        gy = gs * dot(c_ref[...], e2, 1, 0)
        gy3 = gs3 * dot(c_in[...], e3, 1, 0)
        ef = jnp.sum(e2.astype(F32) * f2.astype(F32), axis=0, keepdims=True)
        ef3 = jnp.sum(e3.astype(F32) * f3.astype(F32), axis=0, keepdims=True)
        low_row = low[:1, :]

        def half(value, h, mask):
            keep = mask if h == 0 else jnp.logical_not(mask)
            return jnp.sum(jnp.where(keep, value, jnp.zeros_like(value)), axis=1, keepdims=True)

        for h in range(HEADS):
            res1 = jnp.where(place == h + heads, half(xz, h, low), res1)
            res2 = jnp.where(place == h, half(gy, h, low), res2)
            res2 = jnp.where(place == h + heads, half(ef, h, low_row), res2)
            res3 = jnp.where(place == h, half(gy3, h, low), res3)
            res3 = jnp.where(place == h + heads, half(ef3, h, low_row), res3)
        sums1[...] = res1
        sums2[...] = res2
        back[1] = res3
        row_sums[...] = res_rows
        d_scores[...] = q_sum
        d_b[...] += dot((x2f * (end2 * dt2)).astype(BF16), f2, 1, 1)
        d_c[...] += dot(gs.astype(BF16), e2, 1, 1)
        back[0] += dot(gs3.astype(BF16), e3, 1, 1)

    delay = LAG * lax.max(z, nz - 1 - z)

    def step(t, unused):
        @pl.when(t + EARLY < chunks)
        def _():
            scale(t + EARLY, 0)

        kf = t - LAG * z

        pl.when(jnp.logical_and(kf >= 0, kf < chunks))(lambda: forward(kf))
        kb = t - LAG * (nz - 1 - z)
        pl.when(jnp.logical_and(kb >= 0, kb < chunks))(lambda: backward(kb))
        kg = t - delay
        pl.when(jnp.logical_and(kg >= 0, kg < chunks))(lambda: gradients(kg))
        return unused

    if fused:
        dp = lax.axis_index("dp")
        piece = tok.shape[1]

        def columns(s, k):
            first_column = (s * m + flip(dp, k, m)) * piece
            return t_ref[:, pl.ds(pl.multiple_of(first_column, piece), piece)].astype(F32)

        def copy_tokens(k):
            return send(
                tok_snd.at[k - 1], tok_in.at[k - 1], tok_sem, k - 1, flip(dp, k, m), "dp"
            )

        def copy_gbc(i, k):
            return send(
                gbc_snd.at[i], gbc_in.at[k - 1, i], gbc_sem, (m - 1) * i + k - 1,
                flip(dp, k, m), "dp",
            )

        def copy_acc(i, r):
            who = partner if r % 2 else flip(me, r, n)
            return send(acc.at[i, r], got.at[i, r - 1], acc_sem, (n - 1) * i + r - 1, who)

        def copy_out(i, k):
            return send(
                out.at[i, 0], out.at[i, k], out_sem, m * i + k, flip(dp, k, m), "dp"
            )

        def copy_rate_dp(k):
            return send(
                rate_dp.at[0], rate_dp.at[k], rate_sem, k - 1, flip(dp, k, m), "dp"
            )

        def copy_rate_x():
            return send(rate_acc.at[0], rate_got.at[0], rate_sem, m - 1, partner)

        def copy_rate_z(j):
            return send(rate_acc.at[1], rate_got.at[j], rate_sem, m - 1 + j, flip(me, 2 * j, n))

        def tree(parts):
            while len(parts) > 1:
                parts = [p + q for p, q in zip(parts[::2], parts[1::2])]
            return parts[0]

        def spread(s, unused):
            for k in range(1, m):
                tok_snd[k - 1, s] = columns(s, k)
            return unused

        lax.fori_loop(0, n, spread, 0)
        for k in range(1, m):
            copy_tokens(k).start()

    lax.fori_loop(0, chunks + delay, step, 0)
    copy_back(0).start()
    copy_back(1).start()
    dk = d_scores[...].astype(BF16)
    grad_b = (d_b[...] + dot(dk, c_ref[...], 1, 0)).astype(BF16)
    if fused:
        gbc_snd[0] = grad_b.astype(F32)
        for k in range(1, m):
            copy_gbc(0, k).start()
        gbc[0, :length] = grad_b
    else:
        weight_ref[:, :state] = grad_b
    c_total = d_c[...] + dot(dk, b_ref[...], 0, 0)
    copy_back(0).wait_recv()
    grad_c = (c_total + back_in[0]).astype(BF16)
    if fused:
        gbc_snd[1] = grad_c.astype(F32)
        for k in range(1, m):
            copy_gbc(1, k).start()
        gbc[1, :length] = grad_c
        for k in range(1, m):
            copy_tokens(k).wait_recv()

        def place_tokens(r, unused):
            s = r
            for k in range(m):
                block = columns(s, k) if k == 0 else tok_in[k - 1, s]
                tok[s, :, k * length : (k + 1) * length] = block.T.astype(BF16)
            return unused

        lax.fori_loop(0, n, place_tokens, 0)
        order = list(range(n - 2, -1, -2))
        for i in range(2):
            for k in range(1, m):
                copy_gbc(i, k).wait_recv()
                gbc[i, k * length : (k + 1) * length] = gbc_in[k - 1, i].astype(BF16)
            for r in [r + 1 for r in order] + order:
                acc[i, r] = dot(tok[flip(me, r, n)], gbc[i], 1, 0)
                if r % 2:
                    copy_acc(i, r).start()
    else:
        weight_ref[:, state:] = grad_c
    copy_back(1).wait_recv()
    total = sums2[...] + back_in[1]
    inside, x_in = sums1[:, :heads], sums1[:, heads:]
    g_in, both = total[:, :heads], span[:1, heads:] * total[:, heads:]
    dt_all = cols1[0, :, heads:]
    after = (row_at <= col_at).astype(F32)
    before = (row_at > col_at).astype(F32)
    d_log = (
        both
        + exact_dot(before, dt_all * x_in, 1, 0)
        + exact_dot(after, g_in - dt_all * inside, 1, 0)
        + exact_dot(after, row_sums[...], 1, 1)
    )
    d_rate = -jnp.sum(dt_all * d_log, axis=0, keepdims=True)
    d_rate = jnp.broadcast_to(
        jnp.concatenate([d_rate, jnp.zeros_like(d_rate)], axis=1), (8, 2 * heads)
    )
    if fused:
        rate_dp[0] = d_rate
        for k in range(1, m):
            copy_rate_dp(k).start()
    else:
        drate_ref[...] = d_rate
    d_step = inside + x_in - rate_ref[...] * d_log
    dlogit_ref[...] = d_step.T * jax.nn.sigmoid(logit_ref[...])
    if fused:

        def join(i, r):
            copy_acc(i, r + 1).wait_recv()
            acc[i, r] += got[i, r]
            if r:
                copy_acc(i, r).start()

        def finish(i):
            value = acc[i, 0]
            for r in order[:-1]:
                copy_acc(i, r).wait_recv()
                value += got[i, r - 1]
            out[i, 0] = value
            for k in range(1, m):
                copy_out(i, k).start()

        for r in order:
            join(0, r)
        for k in range(1, m):
            copy_rate_dp(k).wait_recv()
        rate_acc[0] = tree([rate_dp[k] for k in range(m)])
        copy_rate_x().start()
        for r in order[: len(order) // 2]:
            join(1, r)
        finish(0)
        copy_rate_x().wait_recv()
        rate_acc[1] = rate_acc[0] + rate_got[0]
        for j in range(1, nz):
            copy_rate_z(j).start()
        for r in order[len(order) // 2 :]:
            join(1, r)
        finish(1)
        for j in range(1, nz):
            copy_rate_z(j).wait_recv()
        drate_ref[...] = tree([rate_acc[1]] + [rate_got[j] for j in range(1, nz)])[:1, :heads]
        for i in range(2):
            for k in range(m):
                if k:
                    copy_out(i, k).wait_recv()
                first_row = pl.multiple_of(flip(dp, k, m) * piece, piece)
                weight_ref[pl.ds(first_row, piece), i * state : (i + 1) * state] = out[i, k]
        for k in range(1, m):
            copy_tokens(k).wait_send()
            copy_rate_dp(k).wait_send()
            for i in range(2):
                copy_gbc(i, k).wait_send()
                copy_out(i, k).wait_send()
        for i in range(2):
            for r in range(1, n):
                copy_acc(i, r).wait_send()
        copy_rate_x().wait_send()
        for j in range(1, nz):
            copy_rate_z(j).wait_send()
    copy_span().wait_send()
    copy_c().wait_send()
    copy_back(0).wait_send()
    copy_back(1).wait_send()

    def settle(k, unused):
        copy_g(k).wait_send()
        for i in range(PARTS):
            pl.when(jnp.logical_not(last))(lambda: copy_e(k, i).wait_send())
            pl.when(jnp.logical_not(first))(lambda: copy_f(k, i).wait_send())
        return unused

    lax.fori_loop(0, chunks, settle, 0)


def store_kernel(*refs):
    copies = [pltpu.make_async_copy(refs[i], refs[4 + i], refs[8].at[i]) for i in range(4)]
    for copy in copies:
        copy.start()
    for copy in copies:
        copy.wait()


def weight_kernel(
    n, m, t_ref, g_ref, rate_ref, out_ref, rate_out,
    acc, got, ring, r_acc, r_got, sem, out_sem, r_sem,
):
    chunks, blocks, rows = acc.shape[0], acc.shape[1], acc.shape[2]
    piece = chunks * rows
    seq, dp = lax.axis_index("seq"), lax.axis_index("dp")
    dp_steps, seq_steps, bit = [], [], 1
    while bit < m:
        dp_steps.append(("dp", bit, lax.rem(lax.div(dp, bit), 2)))
        bit *= 2
    bit = 1
    while bit < n:
        seq_steps.append(("seq", bit, lax.rem(lax.div(seq, bit), 2)))
        bit *= 2
    count = len(dp_steps) + len(seq_steps)
    orders = (dp_steps + seq_steps, dp_steps[:1] + seq_steps + dp_steps[1:])

    def peer(c, s):
        axis, bit, mine = orders[c % 2][s]
        return {axis: lax.axis_index(axis) + bit - 2 * bit * mine}

    def dp_peer(k):
        other, bit = dp, 1
        while bit < m:
            if k & bit:
                other = other + bit - 2 * bit * lax.rem(lax.div(dp, bit), 2)
            bit *= 2
        return {"dp": other}

    barrier = pltpu.get_barrier_semaphore()
    friends = [dp_peer(k) for k in range(1, m)] + [
        peer(0, s) for s in range(len(dp_steps), count)
    ]
    for friend in friends:
        pl.semaphore_signal(
            barrier, inc=1, device_id=friend, device_id_type=pl.DeviceIdType.MESH
        )

    starts, offsets = [], []
    for order in orders:
        base, width, total = 0, blocks, 0
        starts.append([])
        for unused, unused, mine in order:
            width //= 2
            starts[-1].append((base + width * mine, base + width * (1 - mine), width))
            base = base + width * mine
            if len(starts) == 1:
                offsets.append(total)
                total += width

    def copy(c, s):
        keep, give, size = starts[c % 2][s]
        return pltpu.make_async_remote_copy(
            src_ref=acc.at[c, pl.ds(give, size)],
            dst_ref=got.at[c, pl.ds(offsets[s], size)],
            send_sem=sem.at[0, c, s], recv_sem=sem.at[1, c, s],
            device_id=peer(c, s), device_id_type=pl.DeviceIdType.MESH,
        )

    def rate_copy(s):
        return pltpu.make_async_remote_copy(
            src_ref=r_acc.at[s], dst_ref=r_got.at[s],
            send_sem=r_sem.at[0, s], recv_sem=r_sem.at[1, s],
            device_id=peer(0, s), device_id_type=pl.DeviceIdType.MESH,
        )

    def out_copy(c, k):
        return pltpu.make_async_remote_copy(
            src_ref=ring.at[0, c], dst_ref=ring.at[k, c],
            send_sem=out_sem.at[0, c, k], recv_sem=out_sem.at[1, c, k],
            device_id=dp_peer(k), device_id_type=pl.DeviceIdType.MESH,
        )

    g = g_ref[...]
    r_acc[0] = rate_ref[...]
    block = 128
    for first in range(0, t_ref.shape[1], block):
        product = dot(t_ref[:, first : first + block], g, 0, 0)
        for part in range(0, block, rows):
            row = first + part
            owner, inner = row // (m * piece), row % (m * piece)
            chunk, place = inner % piece // rows, 0
            for axis, bit, unused in orders[chunk % 2]:
                index = inner // piece if axis == "dp" else owner
                place = 2 * place + index // bit % 2
            acc[chunk, place] = product[part : part + rows]
    pl.semaphore_wait(barrier, len(friends))
    for c in range(chunks):
        copy(c, 0).start()
    rate_copy(0).start()
    for s in range(count):
        for c in range(chunks):
            copy(c, s).wait_recv()
            keep, give, size = starts[c % 2][s]
            value = acc[c, pl.ds(keep, size)] + got[c, pl.ds(offsets[s], size)]
            if s + 1 < count:
                acc[c, pl.ds(keep, size)] = value
                copy(c, s + 1).start()
            else:
                ring[0, c] = value[0]
                for k in range(1, m):
                    out_copy(c, k).start()
        rate_copy(s).wait_recv()
        r_acc[s + 1] = r_acc[s] + r_got[s]
        if s + 1 < count:
            rate_copy(s + 1).start()
    rate_out[...] = r_acc[count]
    for c in range(chunks):
        for k in range(m):
            if k > 0:
                out_copy(c, k).wait_recv()
            where = dp_peer(k)["dp"] if k > 0 else dp
            out_ref[pl.ds(where * piece + c * rows, rows)] = ring[k, c]
    for c in range(chunks):
        for s in range(count):
            copy(c, s).wait_send()
        for k in range(1, m):
            out_copy(c, k).wait_send()
    for s in range(count):
        rate_copy(s).wait_send()


def shards(layer_input, projection, ssm_input, step_logit, decay_rate, output_grad):
    tokens, x_rows, logit, grad_rows = layer_input[0], ssm_input[0], step_logit[0], output_grad[0]
    length, full = x_rows.shape
    heads = logit.shape[1]
    size = full // heads
    state = projection.shape[1] // 2
    groups = heads // HEADS
    width = HEADS * size
    count = lax.axis_size("seq")
    limit = 46 * 2**20
    away = pl.BlockSpec(memory_space=pltpu.HBM)
    vmem = pl.BlockSpec(memory_space=pltpu.VMEM)
    slots = pltpu.VMEM((groups, state, width), F32)
    rows_in = pltpu.VMEM((groups, length, width), F32)
    half = pltpu.VMEM((groups, state, width), BF16)
    square = pltpu.VMEM((length, length), F32)
    sums = pltpu.VMEM((length, state), F32)
    short = pltpu.VMEM((length, state), BF16)
    by_lane = pltpu.VMEM((length, 2 * heads), F32)
    cols = pltpu.VMEM((groups, length, 2 * heads), F32)
    strip = pltpu.VMEM((8, 2 * heads), F32)
    two = pltpu.VMEM((2, length, state), F32)
    members = lax.axis_size("dp")
    blocks = count * members
    piece = tokens.shape[1] // blocks
    levels = blocks.bit_length() - 1
    fused = piece % 128 == 0
    rows = pltpu.VMEM((length, full), BF16)
    scratch = (
        [rows, pltpu.VMEM(projection.shape, BF16), rows, rows]
        + [pltpu.VMEM((heads, length), F32), pltpu.VMEM((1, heads), F32)]
        + [short] * 3
        + [cols] * 2
        + [pltpu.VMEM((groups, HEADS, length), F32), strip, strip, sums, sums]
        + [half] * 4
        + [square, square, sums, sums]
        + [by_lane, by_lane, pltpu.VMEM((heads, length), F32), two, two]
        + [rows_in] * 2
        + [slots] * 4
        + [pltpu.SemaphoreType.DMA((6,)), pltpu.SemaphoreType.DMA((2, 4))]
        + [pltpu.SemaphoreType.DMA((2, groups))]
        + [pltpu.SemaphoreType.DMA((2, PARTS * groups))] * 2
    )
    rate_shape = jax.ShapeDtypeStruct((8, 2 * heads), F32)
    weight_shape = jax.ShapeDtypeStruct((length, 2 * state), BF16)
    if fused:
        pairs = count // 2
        others = members - 1
        scratch += [pltpu.VMEM((others, count, length, piece), F32)] * 2
        scratch += [
            pltpu.VMEM((count, piece, members * length), BF16),
            pltpu.VMEM((2, length, state), F32),
            pltpu.VMEM((others, 2, length, state), F32),
            pltpu.VMEM((2, members * length, state), BF16),
            pltpu.VMEM((2, count, piece, state), F32),
            pltpu.VMEM((2, count - 1, piece, state), F32),
            pltpu.VMEM((2, members, piece, state), F32),
            pltpu.VMEM((members, 8, 2 * heads), F32),
            pltpu.VMEM((pairs, 8, 2 * heads), F32),
            pltpu.VMEM((2, 8, 2 * heads), F32),
            pltpu.SemaphoreType.DMA((2, others)),
            pltpu.SemaphoreType.DMA((2, 2 * others)),
            pltpu.SemaphoreType.DMA((2, 2 * (count - 1))),
            pltpu.SemaphoreType.DMA((2, 2 * members)),
            pltpu.SemaphoreType.DMA((2, others + pairs)),
        ]
        rate_shape = pltpu.VMEM((1, heads), F32)
        weight_shape = pltpu.VMEM((members * piece, 2 * state), F32)
    grad_x, grad_logit, rate_rows, weights = pl.pallas_call(
        functools.partial(layer_kernel, count, members, size, fused),
        in_specs=[away] * 6,
        out_specs=[vmem] * 4,
        out_shape=[
            rows,
            pltpu.VMEM((heads, length), F32),
            rate_shape,
            weight_shape,
        ],
        scratch_shapes=scratch,
        compiler_params=pltpu.CompilerParams(
            collective_id=0, has_side_effects=True, vmem_limit_bytes=limit
        ),
        name="layer_gradients",
    )(
        *(
            pltpu.with_memory_space_constraint(v, pltpu.HBM)
            for v in (tokens, projection, x_rows, grad_rows, logit.T, decay_rate[None, :])
        )
    )
    if fused:
        results = (grad_x, grad_logit, rate_rows, weights)
        grad_x, grad_logit, rate_rows, weights = pl.pallas_call(
            store_kernel,
            in_specs=[vmem] * 4,
            out_specs=[away] * 4,
            out_shape=[jax.ShapeDtypeStruct(v.shape, v.dtype) for v in results],
            scratch_shapes=[pltpu.SemaphoreType.DMA((4,))],
            name="store_results",
        )(*(pltpu.with_memory_space_constraint(v, pltpu.VMEM) for v in results))
        return (grad_x[None], grad_logit.T[None], rate_rows[0], weights)
    chunks = max(1, min(8, piece // 8))
    rows = piece // chunks
    weight_rows, rate_sum = pl.pallas_call(
        functools.partial(weight_kernel, count, members),
        in_specs=[vmem] * 3,
        out_specs=[vmem] * 2,
        out_shape=[
            jax.ShapeDtypeStruct((members * piece, 2 * state), F32),
            jax.ShapeDtypeStruct((8, 128), F32),
        ],
        scratch_shapes=[
            pltpu.VMEM((chunks, blocks, rows, 2 * state), F32),
            pltpu.VMEM((chunks, blocks, rows, 2 * state), F32),
            pltpu.VMEM((members, chunks, rows, 2 * state), F32),
            pltpu.VMEM((levels + 1, 8, 128), F32),
            pltpu.VMEM((levels, 8, 128), F32),
            pltpu.SemaphoreType.DMA((2, chunks, levels)),
            pltpu.SemaphoreType.DMA((2, chunks, members)),
            pltpu.SemaphoreType.DMA((2, levels)),
        ],
        compiler_params=pltpu.CompilerParams(
            collective_id=1, has_side_effects=True, vmem_limit_bytes=limit
        ),
        name="weight_gradient",
    )(tokens, weights, rate_rows)
    rate_sum = rate_sum[0, :heads]
    return (grad_x[None], grad_logit.T[None], rate_sum, weight_rows)


def solution(mesh):
    placed = (
        P("dp", "seq", None),
        P(),
        P("dp", "seq", None),
        P("dp", "seq", None),
        P(),
        P("dp", "seq", None),
    )
    return jax.shard_map(
        shards,
        mesh=mesh,
        in_specs=placed,
        out_specs=(P("dp", "seq", None), P("dp", "seq", None), P(), P("seq", None)),
        check_vma=False,
    )
```

```python
import functools

import jax
import jax.numpy as jnp
from jax import lax
from jax.experimental import pallas as pl
from jax.experimental.pallas import tpu as pltpu
from jax.sharding import PartitionSpec as P

F32 = jnp.float32
BF16 = jnp.bfloat16
HEADS = 2
LAG = 3
FIRST = 1
EARLY = 3
PARTS = 1


def dot(a, b, ca, cb):
    return lax.dot_general(a, b, (((ca,), (cb,)), ((), ())), preferred_element_type=F32)


def exact_dot(a, b, ca, cb):
    return lax.dot_general(
        a, b, (((ca,), (cb,)), ((), ())),
        preferred_element_type=F32, precision=lax.Precision.HIGHEST,
    )


def pair_columns(cols, j, size):
    lane = lax.broadcasted_iota(jnp.int32, (cols.shape[0], 2 * size), 1)
    return jnp.where(lane < size, cols[:, j : j + 1], cols[:, j + 1 : j + 2])


def flip(index, bits, limit):
    other, bit = index, 1
    while bit < limit:
        if bits & bit:
            other = other + bit - 2 * bit * lax.rem(lax.div(index, bit), 2)
        bit *= 2
    return other


def layer_kernel(
    n, m, size, fused, t_hbm, w_hbm, x_hbm, g_hbm, logit_hbm, rate_hbm,
    dx_ref, dlogit_ref, drate_ref, weight_ref, t_ref, w_ref, x_ref, g_ref, logit_ref, rate_ref,
    b_ref, c_ref, c_in, cols1, cols2, rows_ref, span, span_in, cf, cf_in,
    e_own, e_other, f_own, f_other, scores, d_scores, d_b, d_c,
    sums1, sums2, row_sums, back, back_in,
    gs_snd, gs_in, e_in, f_in, e_snd, f_snd,
    load_sem, small_sem, gs_sem, e_sem, f_sem, *more,
):
    if fused:
        (
            tok_snd, tok_in, tok, gbc_snd, gbc_in, gbc, acc, got, out,
            tok_sem, gbc_sem, acc_sem, out_sem,
        ) = more
    chunks = gs_snd.shape[0]
    length, state = b_ref.shape
    heads = logit_ref.shape[0]
    width = HEADS * size
    nz = n // 2
    me = lax.axis_index("seq")
    odd = lax.rem(me, 2)
    z = lax.div(me, 2)
    partner = me + 1 - 2 * odd
    first, last = z == 0, z == nz - 1
    barrier = pltpu.get_barrier_semaphore()
    operands = (
        (logit_hbm, logit_ref), (rate_hbm, rate_ref),
        (g_hbm, g_ref), (t_hbm, t_ref), (w_hbm, w_ref), (x_hbm, x_ref),
    )
    load_logit, load_rate, load_g, load_t, load_w, load_x = (
        pltpu.make_async_copy(source, target, load_sem.at[i])
        for i, (source, target) in enumerate(operands)
    )

    def greet(who, axis="seq"):
        pl.semaphore_signal(
            barrier, inc=1, device_id={axis: who}, device_id_type=pl.DeviceIdType.MESH
        )

    load_logit.start()
    load_rate.start()
    load_g.start()
    load_t.start()
    load_w.start()
    load_x.start()
    greet(partner)
    pl.when(jnp.logical_not(first))(lambda: greet(me - 2))
    pl.when(jnp.logical_not(last))(lambda: greet(me + 2))
    greeters = 1
    if fused:
        for r in range(4, n, 2):
            greet(flip(me, r, n))
            greeters += 1
        for k in range(1, m):
            greet(flip(lax.axis_index("dp"), k, m), "dp")
            greeters += 1

    def send(src, dst, sems, k, who, axis="seq"):
        return pltpu.make_async_remote_copy(
            src_ref=src, dst_ref=dst, send_sem=sems.at[0, k], recv_sem=sems.at[1, k],
            device_id={axis: who}, device_id_type=pl.DeviceIdType.MESH,
        )

    def copy_span():
        return send(span, span_in, small_sem, 0, partner)

    def copy_c():
        return send(cf, cf_in, small_sem, 1, partner)

    def copy_back(i):
        return send(back.at[i], back_in.at[i], small_sem, 2 + i, partner)

    def copy_g(k):
        return send(gs_snd.at[k], gs_in.at[k], gs_sem, k, partner)

    part = state // PARTS

    def copy_e(k, i):
        rows = pl.ds(i * part, part)
        return send(e_snd.at[k, rows], e_in.at[k, rows], e_sem, PARTS * k + i, me + 2)

    def copy_f(k, i):
        rows = pl.ds(i * part, part)
        return send(f_snd.at[k, rows], f_in.at[k, rows], f_sem, PARTS * k + i, me - 2)

    def turn(value, k):
        lanes = value.shape[1]
        return pltpu.roll(value, lax.rem(lanes - HEADS * k, lanes), 1)

    def wide(k):
        return pl.ds(pl.multiple_of(k * width, width), width)

    load_logit.wait()
    load_rate.wait()
    logit, rate = logit_ref[...], rate_ref[...]
    dt_all = (jnp.maximum(logit, 0.0) + jnp.log1p(jnp.exp(-jnp.abs(logit)))).T
    row_at = lax.broadcasted_iota(jnp.int32, (length, length), 0)
    col_at = lax.broadcasted_iota(jnp.int32, (length, length), 1)
    until = (row_at >= col_at).astype(F32)
    log_decay = exact_dot(until, -rate * dt_all, 1, 0)
    to_end = jnp.exp(log_decay[length - 1 : length, :] - log_decay)
    grow_all = jnp.exp(log_decay)
    q1 = jnp.concatenate([log_decay, dt_all], axis=1)
    q2 = jnp.concatenate([to_end, grow_all], axis=1)
    span[...] = jnp.broadcast_to(q2[length - 1 : length, :], span.shape)
    def scale(k, unused):
        cols1[k] = turn(q1, k)
        cols = turn(q2, k)
        cols2[k] = cols
        gs_snd[k] = g_ref[:, wide(k)].astype(F32) * pair_columns(cols, heads, size)
        copy_g(k).start()
        return unused

    load_g.wait()
    end = jnp.logical_or(first, last)
    pl.when(end)(lambda: pl.semaphore_wait(barrier, min(nz - 1, 1) + greeters))
    pl.when(jnp.logical_not(end))(lambda: pl.semaphore_wait(barrier, 2 + greeters))
    copy_span().start()
    lax.fori_loop(0, FIRST, scale, 0)
    load_t.wait()
    load_w.wait()
    bc = dot(t_ref[...], w_ref[...], 1, 0).astype(BF16)
    b_ref[...] = bc[:, :state]
    c_ref[...] = bc[:, state:]
    cf[...] = bc[:, state:].astype(F32)
    copy_c().start()
    lax.fori_loop(FIRST, EARLY, scale, 0)
    by_head = q1.T
    for k in range(chunks):
        rows_ref[k] = by_head[HEADS * k : HEADS * (k + 1), :]
    load_x.wait()
    scores[...] = dot(b_ref[...], c_ref[...], 1, 1)
    for ref in (d_scores, d_b, d_c, sums1, sums2, row_sums, back):
        ref[...] = jnp.zeros_like(ref)
    copy_span().wait_recv()

    def receive_c():
        copy_c().wait_recv()
        c_in[...] = cf_in[...].astype(BF16)

    def spans(ref, k):
        return pair_columns(turn(ref[...], k)[:1, :], heads, size)

    def forward(k):
        weight = pair_columns(cols1[k], heads, size) * pair_columns(cols2[k], 0, size)
        near = dot(b_ref[...], (x_ref[:, wide(k)].astype(F32) * weight).astype(BF16), 0, 0)
        mine, theirs = spans(span, k), spans(span_in, k)

        @pl.when(first)
        def _():
            e_in[k] = jnp.zeros_like(e_in[k])

        for i in range(PARTS):
            rows = slice(i * part, (i + 1) * part)
            pl.when(jnp.logical_not(first))(lambda: copy_e(k, i).wait_recv())
            value = e_in[k, rows]

            @pl.when(odd == 0)
            def _():
                e_own[k, rows] = value.astype(BF16)
                middle = mine * value + near[rows]
                e_other[k, rows] = middle.astype(BF16)
                e_snd[k, rows] = theirs * middle

            @pl.when(odd == 1)
            def _():
                e_other[k, rows] = value.astype(BF16)
                middle = theirs * value
                e_own[k, rows] = middle.astype(BF16)
                e_snd[k, rows] = mine * middle + near[rows]

            pl.when(jnp.logical_not(last))(lambda: copy_e(k, i).start())

    def backward(k):
        copy_g(k).wait_recv()
        near = dot(c_ref[...], gs_snd[k].astype(BF16), 0, 0)
        far = dot(c_in[...], gs_in[k].astype(BF16), 0, 0)
        mine, theirs = spans(span, k), spans(span_in, k)

        @pl.when(last)
        def _():
            f_in[k] = jnp.zeros_like(f_in[k])

        for i in range(PARTS):
            rows = slice(i * part, (i + 1) * part)
            pl.when(jnp.logical_not(last))(lambda: copy_f(k, i).wait_recv())
            value = f_in[k, rows]

            @pl.when(odd == 0)
            def _():
                f_other[k, rows] = value.astype(BF16)
                middle = theirs * value + far[rows]
                f_own[k, rows] = middle.astype(BF16)
                f_snd[k, rows] = mine * middle + near[rows]

            @pl.when(odd == 1)
            def _():
                f_own[k, rows] = value.astype(BF16)
                middle = mine * value + near[rows]
                f_other[k, rows] = middle.astype(BF16)
                f_snd[k, rows] = theirs * middle + far[rows]

            pl.when(jnp.logical_not(first))(lambda: copy_f(k, i).start())

    def gradients(k):
        cols, rows = cols1[k], rows_ref[k]
        k_st = scores[...]
        causal = col_at >= row_at
        low = lax.broadcasted_iota(jnp.int32, (length, width), 1) < size
        place = lax.broadcasted_iota(jnp.int32, sums1.shape, 1) - k * HEADS
        row_place = lax.broadcasted_iota(jnp.int32, row_sums.shape, 0) - k * HEADS
        res1, res2, res3, res_rows = sums1[...], sums2[...], back[1], row_sums[...]
        q_sum = d_scores[...]
        x2, g2 = x_ref[:, wide(k)], g_ref[:, wide(k)]
        x2f = x2.astype(F32)
        e2, f2, e3, f3 = e_own[k], f_own[k], e_other[k], f_other[k]
        gs, gs3 = gs_snd[k], gs_in[k]
        dt2 = pair_columns(cols, heads, size)
        end2 = pair_columns(cols2[k], 0, size)
        g_low = jnp.where(low, g2, jnp.zeros_like(g2))
        g_high = jnp.where(low, jnp.zeros_like(g2), g2)
        g_both = jnp.concatenate([g_low, g_high], axis=0)
        gram = dot(x2, g_both, 1, 1)
        weights = []
        for h in range(HEADS):
            gap = rows[h : h + 1, :] - cols[:, h : h + 1]
            decay = jnp.exp(jnp.where(causal, gap, -jnp.inf))
            mg = decay * gram[:, h * length : (h + 1) * length]
            dt = cols[:, heads + h : heads + h + 1]
            q_sum = q_sum + mg * dt
            raw = mg * k_st
            res_rows = jnp.where(row_place == h, jnp.sum(raw * dt, axis=0, keepdims=True), res_rows)
            res1 = jnp.where(place == h, jnp.sum(raw, axis=1, keepdims=True), res1)
            weights.append((decay * k_st).astype(BF16))
        z2 = dot(jnp.concatenate(weights, axis=1), g_both, 1, 0)
        z_in = dot(b_ref[...], f2, 1, 0) * end2
        dx_ref[:, wide(k)] = (dt2 * (z2 + z_in)).astype(dx_ref.dtype)
        xz = x2f * z_in
        gy = gs * dot(c_ref[...], e2, 1, 0)
        gy3 = gs3 * dot(c_in[...], e3, 1, 0)
        ef = jnp.sum(e2.astype(F32) * f2.astype(F32), axis=0, keepdims=True)
        ef3 = jnp.sum(e3.astype(F32) * f3.astype(F32), axis=0, keepdims=True)
        low_row = low[:1, :]

        def half(value, h, mask):
            keep = mask if h == 0 else jnp.logical_not(mask)
            return jnp.sum(jnp.where(keep, value, jnp.zeros_like(value)), axis=1, keepdims=True)

        for h in range(HEADS):
            res1 = jnp.where(place == h + heads, half(xz, h, low), res1)
            res2 = jnp.where(place == h, half(gy, h, low), res2)
            res2 = jnp.where(place == h + heads, half(ef, h, low_row), res2)
            res3 = jnp.where(place == h, half(gy3, h, low), res3)
            res3 = jnp.where(place == h + heads, half(ef3, h, low_row), res3)
        sums1[...] = res1
        sums2[...] = res2
        back[1] = res3
        row_sums[...] = res_rows
        d_scores[...] = q_sum
        d_b[...] += dot((x2f * (end2 * dt2)).astype(BF16), f2, 1, 1)
        d_c[...] += dot(gs.astype(BF16), e2, 1, 1)
        back[0] += dot(gs3.astype(BF16), e3, 1, 1)

    delay = LAG * lax.max(z, nz - 1 - z)

    def await_tokens():
        for k in range(1, m):
            copy_tokens(k).wait_recv()

    def place_tokens(s):
        for k in range(m):
            block = columns(s, k) if k == 0 else tok_in[k - 1, s]
            tok[s, :, k * length : (k + 1) * length] = block.T.astype(BF16)

    def step(t, unused):
        @pl.when(t + EARLY < chunks)
        def _():
            scale(t + EARLY, 0)

        kf = t - LAG * z

        pl.when(jnp.logical_and(kf >= 0, kf < chunks))(lambda: forward(kf))
        kb = t - LAG * (nz - 1 - z)
        pl.when(kb == 0)(receive_c)
        pl.when(jnp.logical_and(kb >= 0, kb < chunks))(lambda: backward(kb))
        kg = t - delay
        pl.when(jnp.logical_and(kg >= 0, kg < chunks))(lambda: gradients(kg))
        if fused:
            @pl.when(t < n)
            def _():
                spread(t, 0)

            @pl.when(t == n)
            def _():
                for k in range(1, m):
                    copy_tokens(k).start()

            block = t - (chunks + delay - n)
            pl.when(block == 0)(await_tokens)
            pl.when(block >= 0)(lambda: place_tokens(block))
        return unused

    if fused:
        dp = lax.axis_index("dp")
        piece = tok.shape[1]

        def columns(s, k):
            first_column = (s * m + flip(dp, k, m)) * piece
            return t_ref[:, pl.ds(pl.multiple_of(first_column, piece), piece)].astype(F32)

        def copy_tokens(k):
            return send(
                tok_snd.at[k - 1], tok_in.at[k - 1], tok_sem, k - 1, flip(dp, k, m), "dp"
            )

        def copy_gbc(i, k):
            return send(
                gbc_snd.at[i], gbc_in.at[k - 1, i], gbc_sem, (m - 1) * i + k - 1,
                flip(dp, k, m), "dp",
            )

        def copy_acc(i, r):
            who = partner if r % 2 else flip(me, r, n)
            rows = pl.ds(0, piece + 8 * i)
            return send(
                acc.at[i, r, rows], got.at[i, r - 1, rows], acc_sem, (n - 1) * i + r - 1, who
            )

        def copy_out(i, k):
            rows = pl.ds(0, piece + 8 * i)
            return send(
                out.at[i, 0, rows], out.at[i, k, rows], out_sem, m * i + k, flip(dp, k, m), "dp"
            )

        def tree(parts):
            while len(parts) > 1:
                parts = [p + q for p, q in zip(parts[::2], parts[1::2])]
            return parts[0]

        def spread(s, unused):
            for k in range(1, m):
                tok_snd[k - 1, s] = columns(s, k)
            return unused

    lax.fori_loop(0, chunks + delay, step, 0)
    copy_back(0).start()
    copy_back(1).start()
    dk = d_scores[...].astype(BF16)
    grad_b = (d_b[...] + dot(dk, c_ref[...], 1, 0)).astype(BF16)
    if fused:
        gbc_snd[0] = grad_b.astype(F32)
        for k in range(1, m):
            copy_gbc(0, k).start()
        gbc[0, :length] = grad_b
    else:
        weight_ref[:, :state] = grad_b
    c_total = d_c[...] + dot(dk, b_ref[...], 0, 0)
    copy_back(0).wait_recv()
    grad_c = (c_total + back_in[0]).astype(BF16)
    if fused:
        gbc_snd[1] = grad_c.astype(F32)
        for k in range(1, m):
            copy_gbc(1, k).start()
        gbc[1, :length] = grad_c
    else:
        weight_ref[:, state:] = grad_c
    copy_span().wait_send()
    copy_c().wait_send()

    def settle(k, unused):
        copy_g(k).wait_send()
        for i in range(PARTS):
            pl.when(jnp.logical_not(last))(lambda: copy_e(k, i).wait_send())
            pl.when(jnp.logical_not(first))(lambda: copy_f(k, i).wait_send())
        return unused

    lax.fori_loop(0, chunks, settle, 0)
    copy_back(1).wait_recv()
    total = sums2[...] + back_in[1]
    inside, x_in = sums1[:, :heads], sums1[:, heads:]
    g_in, both = total[:, :heads], span[:1, heads:] * total[:, heads:]
    dt_all = cols1[0, :, heads:]
    after = (row_at <= col_at).astype(F32)
    before = (row_at > col_at).astype(F32)
    d_log = (
        both
        + exact_dot(before, dt_all * x_in, 1, 0)
        + exact_dot(after, g_in - dt_all * inside, 1, 0)
        + exact_dot(after, row_sums[...], 1, 1)
    )
    d_rate = -jnp.sum(dt_all * d_log, axis=0, keepdims=True)
    d_rate = jnp.broadcast_to(
        jnp.concatenate([d_rate, jnp.zeros_like(d_rate)], axis=1), (8, 2 * heads)
    )
    if not fused:
        drate_ref[...] = d_rate
    d_step = inside + x_in - rate_ref[...] * d_log
    dlogit_ref[...] = d_step.T * jax.nn.sigmoid(logit_ref[...])
    copy_back(0).wait_send()
    copy_back(1).wait_send()
    if fused:
        for k in range(1, m):
            copy_tokens(k).wait_send()
        order = list(range(n - 2, -1, -2))
        for i in range(2):
            for k in range(1, m):
                copy_gbc(i, k).wait_recv()
                gbc[i, k * length : (k + 1) * length] = gbc_in[k - 1, i].astype(BF16)
            for r in [r + 1 for r in order] + order:
                acc[i, r, :piece] = dot(tok[flip(me, r, n)], gbc[i], 1, 0)
                if i == 1:
                    acc[i, r, piece:] = d_rate
                if r % 2:
                    copy_acc(i, r).start()

        def join(i, r):
            rows = slice(0, piece + 8 * i)
            copy_acc(i, r + 1).wait_recv()
            acc[i, r, rows] += got[i, r, rows]
            if r:
                copy_acc(i, r).start()

        def finish(i):
            rows = slice(0, piece + 8 * i)
            parts = [acc[i, 0, rows]]
            for r in range(2, n, 2):
                copy_acc(i, r).wait_recv()
                parts.append(got[i, r - 1, rows])
            out[i, 0, rows] = tree(parts)
            for k in range(1, m):
                copy_out(i, k).start()

        for i in range(2):
            for k in range(1, m):
                copy_gbc(i, k).wait_send()
        for r in order:
            join(0, r)
        for r in order[: len(order) // 2]:
            join(1, r)
        finish(0)
        for r in order[len(order) // 2 :]:
            join(1, r)
        for r in range(1, n):
            copy_acc(0, r).wait_send()
        finish(1)
        for i in range(2):
            for k in range(m):
                if k:
                    copy_out(i, k).wait_recv()
                first_row = pl.multiple_of(flip(dp, k, m) * piece, piece)
                weight_ref[pl.ds(first_row, piece), i * state : (i + 1) * state] = out[i, k, :piece]
        drate_ref[...] = tree([out[1, k, piece:] for k in range(m)])[:1, :heads]
        for k in range(1, m):
            for i in range(2):
                copy_out(i, k).wait_send()
        for r in range(1, n):
            copy_acc(1, r).wait_send()


def store_kernel(*refs):
    copies = [pltpu.make_async_copy(refs[i], refs[4 + i], refs[8].at[i]) for i in range(4)]
    for copy in copies:
        copy.start()
    for copy in copies:
        copy.wait()


def weight_kernel(
    n, m, t_ref, g_ref, rate_ref, out_ref, rate_out,
    acc, got, ring, r_acc, r_got, sem, out_sem, r_sem,
):
    chunks, blocks, rows = acc.shape[0], acc.shape[1], acc.shape[2]
    piece = chunks * rows
    seq, dp = lax.axis_index("seq"), lax.axis_index("dp")
    dp_steps, seq_steps, bit = [], [], 1
    while bit < m:
        dp_steps.append(("dp", bit, lax.rem(lax.div(dp, bit), 2)))
        bit *= 2
    bit = 1
    while bit < n:
        seq_steps.append(("seq", bit, lax.rem(lax.div(seq, bit), 2)))
        bit *= 2
    count = len(dp_steps) + len(seq_steps)
    orders = (dp_steps + seq_steps, dp_steps[:1] + seq_steps + dp_steps[1:])

    def peer(c, s):
        axis, bit, mine = orders[c % 2][s]
        return {axis: lax.axis_index(axis) + bit - 2 * bit * mine}

    def dp_peer(k):
        other, bit = dp, 1
        while bit < m:
            if k & bit:
                other = other + bit - 2 * bit * lax.rem(lax.div(dp, bit), 2)
            bit *= 2
        return {"dp": other}

    barrier = pltpu.get_barrier_semaphore()
    friends = [dp_peer(k) for k in range(1, m)] + [
        peer(0, s) for s in range(len(dp_steps), count)
    ]
    for friend in friends:
        pl.semaphore_signal(
            barrier, inc=1, device_id=friend, device_id_type=pl.DeviceIdType.MESH
        )

    starts, offsets = [], []
    for order in orders:
        base, width, total = 0, blocks, 0
        starts.append([])
        for unused, unused, mine in order:
            width //= 2
            starts[-1].append((base + width * mine, base + width * (1 - mine), width))
            base = base + width * mine
            if len(starts) == 1:
                offsets.append(total)
                total += width

    def copy(c, s):
        keep, give, size = starts[c % 2][s]
        return pltpu.make_async_remote_copy(
            src_ref=acc.at[c, pl.ds(give, size)],
            dst_ref=got.at[c, pl.ds(offsets[s], size)],
            send_sem=sem.at[0, c, s], recv_sem=sem.at[1, c, s],
            device_id=peer(c, s), device_id_type=pl.DeviceIdType.MESH,
        )

    def rate_copy(s):
        return pltpu.make_async_remote_copy(
            src_ref=r_acc.at[s], dst_ref=r_got.at[s],
            send_sem=r_sem.at[0, s], recv_sem=r_sem.at[1, s],
            device_id=peer(0, s), device_id_type=pl.DeviceIdType.MESH,
        )

    def out_copy(c, k):
        return pltpu.make_async_remote_copy(
            src_ref=ring.at[0, c], dst_ref=ring.at[k, c],
            send_sem=out_sem.at[0, c, k], recv_sem=out_sem.at[1, c, k],
            device_id=dp_peer(k), device_id_type=pl.DeviceIdType.MESH,
        )

    g = g_ref[...]
    r_acc[0] = rate_ref[...]
    block = 128
    for first in range(0, t_ref.shape[1], block):
        product = dot(t_ref[:, first : first + block], g, 0, 0)
        for part in range(0, block, rows):
            row = first + part
            owner, inner = row // (m * piece), row % (m * piece)
            chunk, place = inner % piece // rows, 0
            for axis, bit, unused in orders[chunk % 2]:
                index = inner // piece if axis == "dp" else owner
                place = 2 * place + index // bit % 2
            acc[chunk, place] = product[part : part + rows]
    pl.semaphore_wait(barrier, len(friends))
    for c in range(chunks):
        copy(c, 0).start()
    rate_copy(0).start()
    for s in range(count):
        for c in range(chunks):
            copy(c, s).wait_recv()
            keep, give, size = starts[c % 2][s]
            value = acc[c, pl.ds(keep, size)] + got[c, pl.ds(offsets[s], size)]
            if s + 1 < count:
                acc[c, pl.ds(keep, size)] = value
                copy(c, s + 1).start()
            else:
                ring[0, c] = value[0]
                for k in range(1, m):
                    out_copy(c, k).start()
        rate_copy(s).wait_recv()
        r_acc[s + 1] = r_acc[s] + r_got[s]
        if s + 1 < count:
            rate_copy(s + 1).start()
    rate_out[...] = r_acc[count]
    for c in range(chunks):
        for k in range(m):
            if k > 0:
                out_copy(c, k).wait_recv()
            where = dp_peer(k)["dp"] if k > 0 else dp
            out_ref[pl.ds(where * piece + c * rows, rows)] = ring[k, c]
    for c in range(chunks):
        for s in range(count):
            copy(c, s).wait_send()
        for k in range(1, m):
            out_copy(c, k).wait_send()
    for s in range(count):
        rate_copy(s).wait_send()


def shards(layer_input, projection, ssm_input, step_logit, decay_rate, output_grad):
    tokens, x_rows, logit, grad_rows = layer_input[0], ssm_input[0], step_logit[0], output_grad[0]
    length, full = x_rows.shape
    heads = logit.shape[1]
    size = full // heads
    state = projection.shape[1] // 2
    groups = heads // HEADS
    width = HEADS * size
    count = lax.axis_size("seq")
    limit = 46 * 2**20
    away = pl.BlockSpec(memory_space=pltpu.HBM)
    vmem = pl.BlockSpec(memory_space=pltpu.VMEM)
    slots = pltpu.VMEM((groups, state, width), F32)
    rows_in = pltpu.VMEM((groups, length, width), F32)
    half = pltpu.VMEM((groups, state, width), BF16)
    square = pltpu.VMEM((length, length), F32)
    sums = pltpu.VMEM((length, state), F32)
    short = pltpu.VMEM((length, state), BF16)
    by_lane = pltpu.VMEM((length, 2 * heads), F32)
    cols = pltpu.VMEM((groups, length, 2 * heads), F32)
    strip = pltpu.VMEM((8, 2 * heads), F32)
    two = pltpu.VMEM((2, length, state), F32)
    members = lax.axis_size("dp")
    blocks = count * members
    piece = tokens.shape[1] // blocks
    levels = blocks.bit_length() - 1
    fused = piece % 128 == 0 and 2 * count <= groups
    rows = pltpu.VMEM((length, full), BF16)
    scratch = (
        [rows, pltpu.VMEM(projection.shape, BF16), rows, rows]
        + [pltpu.VMEM((heads, length), F32), pltpu.VMEM((1, heads), F32)]
        + [short] * 3
        + [cols] * 2
        + [pltpu.VMEM((groups, HEADS, length), F32), strip, strip, sums, sums]
        + [half] * 4
        + [square, square, sums, sums]
        + [by_lane, by_lane, pltpu.VMEM((heads, length), F32), two, two]
        + [rows_in] * 2
        + [slots] * 4
        + [pltpu.SemaphoreType.DMA((6,)), pltpu.SemaphoreType.DMA((2, 4))]
        + [pltpu.SemaphoreType.DMA((2, groups))]
        + [pltpu.SemaphoreType.DMA((2, PARTS * groups))] * 2
    )
    rate_shape = jax.ShapeDtypeStruct((8, 2 * heads), F32)
    weight_shape = jax.ShapeDtypeStruct((length, 2 * state), BF16)
    if fused:
        others = members - 1
        scratch += [pltpu.VMEM((others, count, length, piece), F32)] * 2
        scratch += [
            pltpu.VMEM((count, piece, members * length), BF16),
            pltpu.VMEM((2, length, state), F32),
            pltpu.VMEM((others, 2, length, state), F32),
            pltpu.VMEM((2, members * length, state), BF16),
            pltpu.VMEM((2, count, piece + 8, state), F32),
            pltpu.VMEM((2, count - 1, piece + 8, state), F32),
            pltpu.VMEM((2, members, piece + 8, state), F32),
            pltpu.SemaphoreType.DMA((2, others)),
            pltpu.SemaphoreType.DMA((2, 2 * others)),
            pltpu.SemaphoreType.DMA((2, 2 * (count - 1))),
            pltpu.SemaphoreType.DMA((2, 2 * members)),
        ]
        rate_shape = pltpu.VMEM((1, heads), F32)
        weight_shape = pltpu.VMEM((members * piece, 2 * state), F32)
    grad_x, grad_logit, rate_rows, weights = pl.pallas_call(
        functools.partial(layer_kernel, count, members, size, fused),
        in_specs=[away] * 6,
        out_specs=[vmem] * 4,
        out_shape=[
            rows,
            pltpu.VMEM((heads, length), F32),
            rate_shape,
            weight_shape,
        ],
        scratch_shapes=scratch,
        compiler_params=pltpu.CompilerParams(
            collective_id=0, has_side_effects=True, vmem_limit_bytes=limit
        ),
        name="layer_gradients",
    )(
        *(
            pltpu.with_memory_space_constraint(v, pltpu.HBM)
            for v in (tokens, projection, x_rows, grad_rows, logit.T, decay_rate[None, :])
        )
    )
    if fused:
        results = (grad_x, grad_logit, rate_rows, weights)
        grad_x, grad_logit, rate_rows, weights = pl.pallas_call(
            store_kernel,
            in_specs=[vmem] * 4,
            out_specs=[away] * 4,
            out_shape=[jax.ShapeDtypeStruct(v.shape, v.dtype) for v in results],
            scratch_shapes=[pltpu.SemaphoreType.DMA((4,))],
            name="store_results",
        )(*(pltpu.with_memory_space_constraint(v, pltpu.VMEM) for v in results))
        return (grad_x[None], grad_logit.T[None], rate_rows[0], weights)
    chunks = max(1, min(8, piece // 8))
    rows = piece // chunks
    weight_rows, rate_sum = pl.pallas_call(
        functools.partial(weight_kernel, count, members),
        in_specs=[vmem] * 3,
        out_specs=[vmem] * 2,
        out_shape=[
            jax.ShapeDtypeStruct((members * piece, 2 * state), F32),
            jax.ShapeDtypeStruct((8, 128), F32),
        ],
        scratch_shapes=[
            pltpu.VMEM((chunks, blocks, rows, 2 * state), F32),
            pltpu.VMEM((chunks, blocks, rows, 2 * state), F32),
            pltpu.VMEM((members, chunks, rows, 2 * state), F32),
            pltpu.VMEM((levels + 1, 8, 128), F32),
            pltpu.VMEM((levels, 8, 128), F32),
            pltpu.SemaphoreType.DMA((2, chunks, levels)),
            pltpu.SemaphoreType.DMA((2, chunks, members)),
            pltpu.SemaphoreType.DMA((2, levels)),
        ],
        compiler_params=pltpu.CompilerParams(
            collective_id=1, has_side_effects=True, vmem_limit_bytes=limit
        ),
        name="weight_gradient",
    )(tokens, weights, rate_rows)
    rate_sum = rate_sum[0, :heads]
    return (grad_x[None], grad_logit.T[None], rate_sum, weight_rows)


def solution(mesh):
    placed = (
        P("dp", "seq", None),
        P(),
        P("dp", "seq", None),
        P("dp", "seq", None),
        P(),
        P("dp", "seq", None),
    )
    return jax.shard_map(
        shards,
        mesh=mesh,
        in_specs=placed,
        out_specs=(P("dp", "seq", None), P("dp", "seq", None), P(), P("seq", None)),
        check_vma=False,
    )
```

```python
import functools

import jax
import jax.numpy as jnp
from jax import lax
from jax.experimental import pallas as pl
from jax.experimental.pallas import tpu as pltpu
from jax.sharding import PartitionSpec as P

F32 = jnp.float32
BF16 = jnp.bfloat16
HEADS = 2
LAG = 3
FIRST = 1
EARLY = 3
PARTS = 1


def dot(a, b, ca, cb):
    return lax.dot_general(a, b, (((ca,), (cb,)), ((), ())), preferred_element_type=F32)


def exact_dot(a, b, ca, cb):
    return lax.dot_general(
        a, b, (((ca,), (cb,)), ((), ())),
        preferred_element_type=F32, precision=lax.Precision.HIGHEST,
    )


def pair_columns(cols, j, size):
    lane = lax.broadcasted_iota(jnp.int32, (cols.shape[0], 2 * size), 1)
    return jnp.where(lane < size, cols[:, j : j + 1], cols[:, j + 1 : j + 2])


def flip(index, bits, limit):
    other, bit = index, 1
    while bit < limit:
        if bits & bit:
            other = other + bit - 2 * bit * lax.rem(lax.div(index, bit), 2)
        bit *= 2
    return other


def layer_kernel(
    n, m, size, fused, t_hbm, w_hbm, x_hbm, g_hbm, logit_hbm, rate_hbm,
    dx_ref, dlogit_ref, drate_ref, weight_ref, t_ref, w_ref, x_ref, g_ref, logit_ref, rate_ref,
    b_ref, c_ref, c_in, b_turned, c_turned, c_in_turned, cols1, cols2, rows_ref, span, span_in, cf, cf_in,
    e_own, e_other, f_own, f_other, scores, d_scores, d_b, d_c,
    sums1, sums2, row_sums, back, back_in,
    gs_snd, gs_in, e_in, f_in, e_snd, f_snd,
    load_sem, small_sem, gs_sem, e_sem, f_sem, *more,
):
    if fused:
        (
            tok_snd, tok_in, tok, gbc_snd, gbc_in, gbc, acc, got, out,
            tok_sem, gbc_sem, acc_sem, out_sem,
        ) = more
    chunks = gs_snd.shape[0]
    length, state = b_ref.shape
    heads = logit_ref.shape[0]
    width = HEADS * size
    nz = n // 2
    me = lax.axis_index("seq")
    odd = lax.rem(me, 2)
    z = lax.div(me, 2)
    partner = me + 1 - 2 * odd
    first, last = z == 0, z == nz - 1
    barrier = pltpu.get_barrier_semaphore()
    operands = (
        (logit_hbm, logit_ref), (rate_hbm, rate_ref),
        (g_hbm, g_ref), (t_hbm, t_ref), (w_hbm, w_ref), (x_hbm, x_ref),
    )
    load_logit, load_rate, load_g, load_t, load_w, load_x = (
        pltpu.make_async_copy(source, target, load_sem.at[i])
        for i, (source, target) in enumerate(operands)
    )

    def greet(who, axis="seq"):
        pl.semaphore_signal(
            barrier, inc=1, device_id={axis: who}, device_id_type=pl.DeviceIdType.MESH
        )

    load_logit.start()
    load_rate.start()
    load_g.start()
    load_t.start()
    load_w.start()
    load_x.start()
    greet(partner)
    pl.when(jnp.logical_not(first))(lambda: greet(me - 2))
    pl.when(jnp.logical_not(last))(lambda: greet(me + 2))
    greeters = 1
    if fused:
        for r in range(4, n, 2):
            greet(flip(me, r, n))
            greeters += 1
        for k in range(1, m):
            greet(flip(lax.axis_index("dp"), k, m), "dp")
            greeters += 1

    def send(src, dst, sems, k, who, axis="seq"):
        return pltpu.make_async_remote_copy(
            src_ref=src, dst_ref=dst, send_sem=sems.at[0, k], recv_sem=sems.at[1, k],
            device_id={axis: who}, device_id_type=pl.DeviceIdType.MESH,
        )

    def copy_span():
        return send(span, span_in, small_sem, 0, partner)

    def copy_c():
        return send(cf, cf_in, small_sem, 1, partner)

    def copy_back(i):
        return send(back.at[i], back_in.at[i], small_sem, 2 + i, partner)

    def copy_g(k):
        return send(gs_snd.at[k], gs_in.at[k], gs_sem, k, partner)

    part = state // PARTS

    def copy_e(k, i):
        rows = pl.ds(i * part, part)
        return send(e_snd.at[k, rows], e_in.at[k, rows], e_sem, PARTS * k + i, me + 2)

    def copy_f(k, i):
        rows = pl.ds(i * part, part)
        return send(f_snd.at[k, rows], f_in.at[k, rows], f_sem, PARTS * k + i, me - 2)

    def turn(value, k):
        lanes = value.shape[1]
        return pltpu.roll(value, lax.rem(lanes - HEADS * k, lanes), 1)

    def wide(k):
        return pl.ds(pl.multiple_of(k * width, width), width)

    load_logit.wait()
    load_rate.wait()
    logit, rate = logit_ref[...], rate_ref[...]
    dt_all = (jnp.maximum(logit, 0.0) + jnp.log1p(jnp.exp(-jnp.abs(logit)))).T
    row_at = lax.broadcasted_iota(jnp.int32, (length, length), 0)
    col_at = lax.broadcasted_iota(jnp.int32, (length, length), 1)
    until = (row_at >= col_at).astype(F32)
    log_decay = exact_dot(until, -rate * dt_all, 1, 0)
    to_end = jnp.exp(log_decay[length - 1 : length, :] - log_decay)
    grow_all = jnp.exp(log_decay)
    q1 = jnp.concatenate([log_decay, dt_all], axis=1)
    q2 = jnp.concatenate([to_end, grow_all], axis=1)
    span[...] = jnp.broadcast_to(q2[length - 1 : length, :], span.shape)
    def scale(k, unused):
        cols1[k] = turn(q1, k)
        cols = turn(q2, k)
        cols2[k] = cols
        gs_snd[k] = g_ref[:, wide(k)].astype(F32) * pair_columns(cols, heads, size)
        copy_g(k).start()
        return unused

    load_g.wait()
    end = jnp.logical_or(first, last)
    pl.when(end)(lambda: pl.semaphore_wait(barrier, min(nz - 1, 1) + greeters))
    pl.when(jnp.logical_not(end))(lambda: pl.semaphore_wait(barrier, 2 + greeters))
    copy_span().start()
    lax.fori_loop(0, FIRST, scale, 0)
    load_t.wait()
    load_w.wait()
    bc = dot(t_ref[...], w_ref[...], 1, 0).astype(BF16)
    b_ref[...] = bc[:, :state]
    c_ref[...] = bc[:, state:]
    cf[...] = bc[:, state:].astype(F32)
    copy_c().start()
    lax.fori_loop(FIRST, EARLY, scale, 0)
    b_turned[...] = b_ref[...].astype(F32).T.astype(BF16)
    c_turned[...] = cf[...].T.astype(BF16)
    by_head = q1.T
    for k in range(chunks):
        rows_ref[k] = by_head[HEADS * k : HEADS * (k + 1), :]
    load_x.wait()
    scores[...] = dot(b_ref[...], c_ref[...], 1, 1)
    for ref in (d_scores, d_b, d_c, sums1, sums2, row_sums, back):
        ref[...] = jnp.zeros_like(ref)
    copy_span().wait_recv()

    def receive_c():
        copy_c().wait_recv()
        c_in[...] = cf_in[...].astype(BF16)
        c_in_turned[...] = cf_in[...].T.astype(BF16)

    def spans(ref, k):
        return pair_columns(turn(ref[...], k)[:1, :], heads, size)

    def forward(k):
        weight = pair_columns(cols1[k], heads, size) * pair_columns(cols2[k], 0, size)
        near = dot(b_turned[...], (x_ref[:, wide(k)].astype(F32) * weight).astype(BF16), 1, 0)
        mine, theirs = spans(span, k), spans(span_in, k)

        @pl.when(first)
        def _():
            e_in[k] = jnp.zeros_like(e_in[k])

        for i in range(PARTS):
            rows = slice(i * part, (i + 1) * part)
            pl.when(jnp.logical_not(first))(lambda: copy_e(k, i).wait_recv())
            value = e_in[k, rows]

            @pl.when(odd == 0)
            def _():
                e_own[k, rows] = value.astype(BF16)
                middle = mine * value + near[rows]
                e_other[k, rows] = middle.astype(BF16)
                e_snd[k, rows] = theirs * middle

            @pl.when(odd == 1)
            def _():
                e_other[k, rows] = value.astype(BF16)
                middle = theirs * value
                e_own[k, rows] = middle.astype(BF16)
                e_snd[k, rows] = mine * middle + near[rows]

            pl.when(jnp.logical_not(last))(lambda: copy_e(k, i).start())

    def backward(k):
        copy_g(k).wait_recv()
        near = dot(c_turned[...], gs_snd[k].astype(BF16), 1, 0)
        far = dot(c_in_turned[...], gs_in[k].astype(BF16), 1, 0)
        mine, theirs = spans(span, k), spans(span_in, k)

        @pl.when(last)
        def _():
            f_in[k] = jnp.zeros_like(f_in[k])

        for i in range(PARTS):
            rows = slice(i * part, (i + 1) * part)
            pl.when(jnp.logical_not(last))(lambda: copy_f(k, i).wait_recv())
            value = f_in[k, rows]

            @pl.when(odd == 0)
            def _():
                f_other[k, rows] = value.astype(BF16)
                middle = theirs * value + far[rows]
                f_own[k, rows] = middle.astype(BF16)
                f_snd[k, rows] = mine * middle + near[rows]

            @pl.when(odd == 1)
            def _():
                f_own[k, rows] = value.astype(BF16)
                middle = mine * value + near[rows]
                f_other[k, rows] = middle.astype(BF16)
                f_snd[k, rows] = theirs * middle + far[rows]

            pl.when(jnp.logical_not(first))(lambda: copy_f(k, i).start())

    def gradients(k):
        cols, rows = cols1[k], rows_ref[k]
        k_st = scores[...]
        causal = col_at >= row_at
        low = lax.broadcasted_iota(jnp.int32, (length, width), 1) < size
        place = lax.broadcasted_iota(jnp.int32, sums1.shape, 1) - k * HEADS
        row_place = lax.broadcasted_iota(jnp.int32, row_sums.shape, 0) - k * HEADS
        res1, res2, res3, res_rows = sums1[...], sums2[...], back[1], row_sums[...]
        q_sum = d_scores[...]
        x2, g2 = x_ref[:, wide(k)], g_ref[:, wide(k)]
        x2f = x2.astype(F32)
        e2, f2, e3, f3 = e_own[k], f_own[k], e_other[k], f_other[k]
        gs, gs3 = gs_snd[k], gs_in[k]
        dt2 = pair_columns(cols, heads, size)
        end2 = pair_columns(cols2[k], 0, size)
        g_low = jnp.where(low, g2, jnp.zeros_like(g2))
        g_high = jnp.where(low, jnp.zeros_like(g2), g2)
        g_both = jnp.concatenate([g_low, g_high], axis=0)
        gram = dot(x2, g_both, 1, 1)
        weights = []
        for h in range(HEADS):
            gap = rows[h : h + 1, :] - cols[:, h : h + 1]
            decay = jnp.exp(jnp.where(causal, gap, -jnp.inf))
            mg = decay * gram[:, h * length : (h + 1) * length]
            dt = cols[:, heads + h : heads + h + 1]
            q_sum = q_sum + mg * dt
            raw = mg * k_st
            res_rows = jnp.where(row_place == h, jnp.sum(raw * dt, axis=0, keepdims=True), res_rows)
            res1 = jnp.where(place == h, jnp.sum(raw, axis=1, keepdims=True), res1)
            weights.append((decay * k_st).astype(BF16))
        z2 = dot(jnp.concatenate(weights, axis=1), g_both, 1, 0)
        z_in = dot(b_ref[...], f2, 1, 0) * end2
        dx_ref[:, wide(k)] = (dt2 * (z2 + z_in)).astype(dx_ref.dtype)
        xz = x2f * z_in
        gy = gs * dot(c_ref[...], e2, 1, 0)
        gy3 = gs3 * dot(c_in[...], e3, 1, 0)
        ef = jnp.sum(e2.astype(F32) * f2.astype(F32), axis=0, keepdims=True)
        ef3 = jnp.sum(e3.astype(F32) * f3.astype(F32), axis=0, keepdims=True)
        low_row = low[:1, :]

        def half(value, h, mask):
            keep = mask if h == 0 else jnp.logical_not(mask)
            return jnp.sum(jnp.where(keep, value, jnp.zeros_like(value)), axis=1, keepdims=True)

        for h in range(HEADS):
            res1 = jnp.where(place == h + heads, half(xz, h, low), res1)
            res2 = jnp.where(place == h, half(gy, h, low), res2)
            res2 = jnp.where(place == h + heads, half(ef, h, low_row), res2)
            res3 = jnp.where(place == h, half(gy3, h, low), res3)
            res3 = jnp.where(place == h + heads, half(ef3, h, low_row), res3)
        sums1[...] = res1
        sums2[...] = res2
        back[1] = res3
        row_sums[...] = res_rows
        d_scores[...] = q_sum
        d_b[...] += dot((x2f * (end2 * dt2)).astype(BF16), f2, 1, 1)
        d_c[...] += dot(gs.astype(BF16), e2, 1, 1)
        back[0] += dot(gs3.astype(BF16), e3, 1, 1)

    delay = LAG * lax.max(z, nz - 1 - z)

    def await_tokens():
        for k in range(1, m):
            copy_tokens(k).wait_recv()

    def place_tokens(s):
        for k in range(m):
            block = columns(s, k) if k == 0 else tok_in[k - 1, s]
            tok[s, :, k * length : (k + 1) * length] = block.T.astype(BF16)

    def step(t, unused):
        @pl.when(t + EARLY < chunks)
        def _():
            scale(t + EARLY, 0)

        kf = t - LAG * z

        pl.when(jnp.logical_and(kf >= 0, kf < chunks))(lambda: forward(kf))
        kb = t - LAG * (nz - 1 - z)
        pl.when(kb == 0)(receive_c)
        pl.when(jnp.logical_and(kb >= 0, kb < chunks))(lambda: backward(kb))
        kg = t - delay
        pl.when(jnp.logical_and(kg >= 0, kg < chunks))(lambda: gradients(kg))
        if fused:
            @pl.when(t < n)
            def _():
                spread(t, 0)

            @pl.when(t == n)
            def _():
                for k in range(1, m):
                    copy_tokens(k).start()

            block = t - (chunks + delay - n)
            pl.when(block == 0)(await_tokens)
            pl.when(block >= 0)(lambda: place_tokens(block))
        return unused

    if fused:
        dp = lax.axis_index("dp")
        piece = tok.shape[1]

        def columns(s, k):
            first_column = (s * m + flip(dp, k, m)) * piece
            return t_ref[:, pl.ds(pl.multiple_of(first_column, piece), piece)].astype(F32)

        def copy_tokens(k):
            return send(
                tok_snd.at[k - 1], tok_in.at[k - 1], tok_sem, k - 1, flip(dp, k, m), "dp"
            )

        def copy_gbc(i, k):
            return send(
                gbc_snd.at[i], gbc_in.at[k - 1, i], gbc_sem, (m - 1) * i + k - 1,
                flip(dp, k, m), "dp",
            )

        def copy_acc(i, r):
            who = partner if r % 2 else flip(me, r, n)
            rows = pl.ds(0, piece + 8 * i)
            return send(
                acc.at[i, r, rows], got.at[i, r - 1, rows], acc_sem, (n - 1) * i + r - 1, who
            )

        def copy_out(i, k):
            rows = pl.ds(0, piece + 8 * i)
            return send(
                out.at[i, 0, rows], out.at[i, k, rows], out_sem, m * i + k, flip(dp, k, m), "dp"
            )

        def tree(parts):
            while len(parts) > 1:
                parts = [p + q for p, q in zip(parts[::2], parts[1::2])]
            return parts[0]

        def spread(s, unused):
            for k in range(1, m):
                tok_snd[k - 1, s] = columns(s, k)
            return unused

    lax.fori_loop(0, chunks + delay, step, 0)
    copy_back(0).start()
    copy_back(1).start()
    dk = d_scores[...].astype(BF16)
    grad_b = (d_b[...] + dot(dk, c_ref[...], 1, 0)).astype(BF16)
    if fused:
        gbc_snd[0] = grad_b.astype(F32)
        for k in range(m - 1, 0, -1):
            copy_gbc(0, k).start()
        gbc[0, :length] = grad_b
    else:
        weight_ref[:, :state] = grad_b
    c_total = d_c[...] + dot(dk, b_ref[...], 0, 0)
    copy_back(0).wait_recv()
    grad_c = (c_total + back_in[0]).astype(BF16)
    if fused:
        gbc_snd[1] = grad_c.astype(F32)
        for k in range(m - 1, 0, -1):
            copy_gbc(1, k).start()
        gbc[1, :length] = grad_c
    else:
        weight_ref[:, state:] = grad_c
    copy_span().wait_send()
    copy_c().wait_send()

    def settle(k, unused):
        copy_g(k).wait_send()
        for i in range(PARTS):
            pl.when(jnp.logical_not(last))(lambda: copy_e(k, i).wait_send())
            pl.when(jnp.logical_not(first))(lambda: copy_f(k, i).wait_send())
        return unused

    lax.fori_loop(0, chunks, settle, 0)
    copy_back(1).wait_recv()
    total = sums2[...] + back_in[1]
    inside, x_in = sums1[:, :heads], sums1[:, heads:]
    g_in, both = total[:, :heads], span[:1, heads:] * total[:, heads:]
    dt_all = cols1[0, :, heads:]
    after = (row_at <= col_at).astype(F32)
    before = (row_at > col_at).astype(F32)
    d_log = (
        both
        + exact_dot(before, dt_all * x_in, 1, 0)
        + exact_dot(after, g_in - dt_all * inside, 1, 0)
        + exact_dot(after, row_sums[...], 1, 1)
    )
    d_rate = -jnp.sum(dt_all * d_log, axis=0, keepdims=True)
    d_rate = jnp.broadcast_to(
        jnp.concatenate([d_rate, jnp.zeros_like(d_rate)], axis=1), (8, 2 * heads)
    )
    if not fused:
        drate_ref[...] = d_rate
    d_step = inside + x_in - rate_ref[...] * d_log
    dlogit_ref[...] = d_step.T * jax.nn.sigmoid(logit_ref[...])
    copy_back(0).wait_send()
    copy_back(1).wait_send()
    if fused:
        for k in range(1, m):
            copy_tokens(k).wait_send()
        order = list(range(n - 2, -1, -2))
        for i in range(2):
            for k in range(1, m):
                copy_gbc(i, k).wait_recv()
                gbc[i, k * length : (k + 1) * length] = gbc_in[k - 1, i].astype(BF16)
            for r in [r + 1 for r in order] + order:
                acc[i, r, :piece] = dot(tok[flip(me, r, n)], gbc[i], 1, 0)
                if i == 1:
                    acc[i, r, piece:] = d_rate
                if r % 2:
                    copy_acc(i, r).start()

        def join(i, r):
            rows = slice(0, piece + 8 * i)
            copy_acc(i, r + 1).wait_recv()
            acc[i, r, rows] += got[i, r, rows]
            if r:
                copy_acc(i, r).start()

        def finish(i):
            rows = slice(0, piece + 8 * i)
            parts = [acc[i, 0, rows]]
            for r in range(2, n, 2):
                copy_acc(i, r).wait_recv()
                parts.append(got[i, r - 1, rows])
            out[i, 0, rows] = tree(parts)
            for k in range(m - 1, 0, -1):
                copy_out(i, k).start()

        for i in range(2):
            for k in range(1, m):
                copy_gbc(i, k).wait_send()
        for r in order:
            join(0, r)
        for r in order[: len(order) // 2]:
            join(1, r)
        finish(0)
        for r in order[len(order) // 2 :]:
            join(1, r)
        for r in range(1, n):
            copy_acc(0, r).wait_send()
        finish(1)
        for i in range(2):
            for k in range(m):
                if k:
                    copy_out(i, k).wait_recv()
                first_row = pl.multiple_of(flip(dp, k, m) * piece, piece)
                weight_ref[pl.ds(first_row, piece), i * state : (i + 1) * state] = out[i, k, :piece]
        drate_ref[...] = tree([out[1, k, piece:] for k in range(m)])[:1, :heads]
        for k in range(1, m):
            for i in range(2):
                copy_out(i, k).wait_send()
        for r in range(1, n):
            copy_acc(1, r).wait_send()


def store_kernel(*refs):
    copies = [pltpu.make_async_copy(refs[i], refs[4 + i], refs[8].at[i]) for i in range(4)]
    for copy in copies:
        copy.start()
    for copy in copies:
        copy.wait()


def weight_kernel(
    n, m, t_ref, g_ref, rate_ref, out_ref, rate_out,
    acc, got, ring, r_acc, r_got, sem, out_sem, r_sem,
):
    chunks, blocks, rows = acc.shape[0], acc.shape[1], acc.shape[2]
    piece = chunks * rows
    seq, dp = lax.axis_index("seq"), lax.axis_index("dp")
    dp_steps, seq_steps, bit = [], [], 1
    while bit < m:
        dp_steps.append(("dp", bit, lax.rem(lax.div(dp, bit), 2)))
        bit *= 2
    bit = 1
    while bit < n:
        seq_steps.append(("seq", bit, lax.rem(lax.div(seq, bit), 2)))
        bit *= 2
    count = len(dp_steps) + len(seq_steps)
    orders = (dp_steps + seq_steps, dp_steps[:1] + seq_steps + dp_steps[1:])

    def peer(c, s):
        axis, bit, mine = orders[c % 2][s]
        return {axis: lax.axis_index(axis) + bit - 2 * bit * mine}

    def dp_peer(k):
        other, bit = dp, 1
        while bit < m:
            if k & bit:
                other = other + bit - 2 * bit * lax.rem(lax.div(dp, bit), 2)
            bit *= 2
        return {"dp": other}

    barrier = pltpu.get_barrier_semaphore()
    friends = [dp_peer(k) for k in range(1, m)] + [
        peer(0, s) for s in range(len(dp_steps), count)
    ]
    for friend in friends:
        pl.semaphore_signal(
            barrier, inc=1, device_id=friend, device_id_type=pl.DeviceIdType.MESH
        )

    starts, offsets = [], []
    for order in orders:
        base, width, total = 0, blocks, 0
        starts.append([])
        for unused, unused, mine in order:
            width //= 2
            starts[-1].append((base + width * mine, base + width * (1 - mine), width))
            base = base + width * mine
            if len(starts) == 1:
                offsets.append(total)
                total += width

    def copy(c, s):
        keep, give, size = starts[c % 2][s]
        return pltpu.make_async_remote_copy(
            src_ref=acc.at[c, pl.ds(give, size)],
            dst_ref=got.at[c, pl.ds(offsets[s], size)],
            send_sem=sem.at[0, c, s], recv_sem=sem.at[1, c, s],
            device_id=peer(c, s), device_id_type=pl.DeviceIdType.MESH,
        )

    def rate_copy(s):
        return pltpu.make_async_remote_copy(
            src_ref=r_acc.at[s], dst_ref=r_got.at[s],
            send_sem=r_sem.at[0, s], recv_sem=r_sem.at[1, s],
            device_id=peer(0, s), device_id_type=pl.DeviceIdType.MESH,
        )

    def out_copy(c, k):
        return pltpu.make_async_remote_copy(
            src_ref=ring.at[0, c], dst_ref=ring.at[k, c],
            send_sem=out_sem.at[0, c, k], recv_sem=out_sem.at[1, c, k],
            device_id=dp_peer(k), device_id_type=pl.DeviceIdType.MESH,
        )

    g = g_ref[...]
    r_acc[0] = rate_ref[...]
    block = 128
    for first in range(0, t_ref.shape[1], block):
        product = dot(t_ref[:, first : first + block], g, 0, 0)
        for part in range(0, block, rows):
            row = first + part
            owner, inner = row // (m * piece), row % (m * piece)
            chunk, place = inner % piece // rows, 0
            for axis, bit, unused in orders[chunk % 2]:
                index = inner // piece if axis == "dp" else owner
                place = 2 * place + index // bit % 2
            acc[chunk, place] = product[part : part + rows]
    pl.semaphore_wait(barrier, len(friends))
    for c in range(chunks):
        copy(c, 0).start()
    rate_copy(0).start()
    for s in range(count):
        for c in range(chunks):
            copy(c, s).wait_recv()
            keep, give, size = starts[c % 2][s]
            value = acc[c, pl.ds(keep, size)] + got[c, pl.ds(offsets[s], size)]
            if s + 1 < count:
                acc[c, pl.ds(keep, size)] = value
                copy(c, s + 1).start()
            else:
                ring[0, c] = value[0]
                for k in range(1, m):
                    out_copy(c, k).start()
        rate_copy(s).wait_recv()
        r_acc[s + 1] = r_acc[s] + r_got[s]
        if s + 1 < count:
            rate_copy(s + 1).start()
    rate_out[...] = r_acc[count]
    for c in range(chunks):
        for k in range(m):
            if k > 0:
                out_copy(c, k).wait_recv()
            where = dp_peer(k)["dp"] if k > 0 else dp
            out_ref[pl.ds(where * piece + c * rows, rows)] = ring[k, c]
    for c in range(chunks):
        for s in range(count):
            copy(c, s).wait_send()
        for k in range(1, m):
            out_copy(c, k).wait_send()
    for s in range(count):
        rate_copy(s).wait_send()


def shards(layer_input, projection, ssm_input, step_logit, decay_rate, output_grad):
    tokens, x_rows, logit, grad_rows = layer_input[0], ssm_input[0], step_logit[0], output_grad[0]
    length, full = x_rows.shape
    heads = logit.shape[1]
    size = full // heads
    state = projection.shape[1] // 2
    groups = heads // HEADS
    width = HEADS * size
    count = lax.axis_size("seq")
    limit = 46 * 2**20
    away = pl.BlockSpec(memory_space=pltpu.HBM)
    vmem = pl.BlockSpec(memory_space=pltpu.VMEM)
    slots = pltpu.VMEM((groups, state, width), F32)
    rows_in = pltpu.VMEM((groups, length, width), F32)
    half = pltpu.VMEM((groups, state, width), BF16)
    square = pltpu.VMEM((length, length), F32)
    sums = pltpu.VMEM((length, state), F32)
    short = pltpu.VMEM((length, state), BF16)
    by_lane = pltpu.VMEM((length, 2 * heads), F32)
    cols = pltpu.VMEM((groups, length, 2 * heads), F32)
    strip = pltpu.VMEM((8, 2 * heads), F32)
    two = pltpu.VMEM((2, length, state), F32)
    members = lax.axis_size("dp")
    blocks = count * members
    piece = tokens.shape[1] // blocks
    levels = blocks.bit_length() - 1
    fused = piece % 128 == 0 and 2 * count <= groups
    rows = pltpu.VMEM((length, full), BF16)
    scratch = (
        [rows, pltpu.VMEM(projection.shape, BF16), rows, rows]
        + [pltpu.VMEM((heads, length), F32), pltpu.VMEM((1, heads), F32)]
        + [short] * 3
        + [pltpu.VMEM((state, length), BF16)] * 3
        + [cols] * 2
        + [pltpu.VMEM((groups, HEADS, length), F32), strip, strip, sums, sums]
        + [half] * 4
        + [square, square, sums, sums]
        + [by_lane, by_lane, pltpu.VMEM((heads, length), F32), two, two]
        + [rows_in] * 2
        + [slots] * 4
        + [pltpu.SemaphoreType.DMA((6,)), pltpu.SemaphoreType.DMA((2, 4))]
        + [pltpu.SemaphoreType.DMA((2, groups))]
        + [pltpu.SemaphoreType.DMA((2, PARTS * groups))] * 2
    )
    rate_shape = jax.ShapeDtypeStruct((8, 2 * heads), F32)
    weight_shape = jax.ShapeDtypeStruct((length, 2 * state), BF16)
    if fused:
        others = members - 1
        scratch += [pltpu.VMEM((others, count, length, piece), F32)] * 2
        scratch += [
            pltpu.VMEM((count, piece, members * length), BF16),
            pltpu.VMEM((2, length, state), F32),
            pltpu.VMEM((others, 2, length, state), F32),
            pltpu.VMEM((2, members * length, state), BF16),
            pltpu.VMEM((2, count, piece + 8, state), F32),
            pltpu.VMEM((2, count - 1, piece + 8, state), F32),
            pltpu.VMEM((2, members, piece + 8, state), F32),
            pltpu.SemaphoreType.DMA((2, others)),
            pltpu.SemaphoreType.DMA((2, 2 * others)),
            pltpu.SemaphoreType.DMA((2, 2 * (count - 1))),
            pltpu.SemaphoreType.DMA((2, 2 * members)),
        ]
        rate_shape = pltpu.VMEM((1, heads), F32)
        weight_shape = pltpu.VMEM((members * piece, 2 * state), F32)
    grad_x, grad_logit, rate_rows, weights = pl.pallas_call(
        functools.partial(layer_kernel, count, members, size, fused),
        in_specs=[away] * 6,
        out_specs=[vmem] * 4,
        out_shape=[
            rows,
            pltpu.VMEM((heads, length), F32),
            rate_shape,
            weight_shape,
        ],
        scratch_shapes=scratch,
        compiler_params=pltpu.CompilerParams(
            collective_id=0, has_side_effects=True, vmem_limit_bytes=limit
        ),
        name="layer_gradients",
    )(
        *(
            pltpu.with_memory_space_constraint(v, pltpu.HBM)
            for v in (tokens, projection, x_rows, grad_rows, logit.T, decay_rate[None, :])
        )
    )
    if fused:
        results = (grad_x, grad_logit, rate_rows, weights)
        grad_x, grad_logit, rate_rows, weights = pl.pallas_call(
            store_kernel,
            in_specs=[vmem] * 4,
            out_specs=[away] * 4,
            out_shape=[jax.ShapeDtypeStruct(v.shape, v.dtype) for v in results],
            scratch_shapes=[pltpu.SemaphoreType.DMA((4,))],
            name="store_results",
        )(*(pltpu.with_memory_space_constraint(v, pltpu.VMEM) for v in results))
        return (grad_x[None], grad_logit.T[None], rate_rows[0], weights)
    chunks = max(1, min(8, piece // 8))
    rows = piece // chunks
    weight_rows, rate_sum = pl.pallas_call(
        functools.partial(weight_kernel, count, members),
        in_specs=[vmem] * 3,
        out_specs=[vmem] * 2,
        out_shape=[
            jax.ShapeDtypeStruct((members * piece, 2 * state), F32),
            jax.ShapeDtypeStruct((8, 128), F32),
        ],
        scratch_shapes=[
            pltpu.VMEM((chunks, blocks, rows, 2 * state), F32),
            pltpu.VMEM((chunks, blocks, rows, 2 * state), F32),
            pltpu.VMEM((members, chunks, rows, 2 * state), F32),
            pltpu.VMEM((levels + 1, 8, 128), F32),
            pltpu.VMEM((levels, 8, 128), F32),
            pltpu.SemaphoreType.DMA((2, chunks, levels)),
            pltpu.SemaphoreType.DMA((2, chunks, members)),
            pltpu.SemaphoreType.DMA((2, levels)),
        ],
        compiler_params=pltpu.CompilerParams(
            collective_id=1, has_side_effects=True, vmem_limit_bytes=limit
        ),
        name="weight_gradient",
    )(tokens, weights, rate_rows)
    rate_sum = rate_sum[0, :heads]
    return (grad_x[None], grad_logit.T[None], rate_sum, weight_rows)


def solution(mesh):
    placed = (
        P("dp", "seq", None),
        P(),
        P("dp", "seq", None),
        P("dp", "seq", None),
        P(),
        P("dp", "seq", None),
    )
    return jax.shard_map(
        shards,
        mesh=mesh,
        in_specs=placed,
        out_specs=(P("dp", "seq", None), P("dp", "seq", None), P(), P("seq", None)),
        check_vma=False,
    )
```

```python
import functools

import jax
import jax.numpy as jnp
from jax import lax
from jax.experimental import pallas as pl
from jax.experimental.pallas import tpu as pltpu
from jax.sharding import PartitionSpec as P

F32 = jnp.float32
BF16 = jnp.bfloat16
HEADS = 2
LAG = 3
FIRST = 1
EARLY = 4
PARTS = 1


def dot(a, b, ca, cb):
    return lax.dot_general(a, b, (((ca,), (cb,)), ((), ())), preferred_element_type=F32)


def exact_dot(a, b, ca, cb):
    return lax.dot_general(
        a, b, (((ca,), (cb,)), ((), ())),
        preferred_element_type=F32, precision=lax.Precision.HIGHEST,
    )


def pair_columns(cols, j, size):
    lane = lax.broadcasted_iota(jnp.int32, (cols.shape[0], 2 * size), 1)
    return jnp.where(lane < size, cols[:, j : j + 1], cols[:, j + 1 : j + 2])


def flip(index, bits, limit):
    other, bit = index, 1
    while bit < limit:
        if bits & bit:
            other = other + bit - 2 * bit * lax.rem(lax.div(index, bit), 2)
        bit *= 2
    return other


def layer_kernel(
    n, m, size, fused, t_hbm, w_hbm, x_hbm, g_hbm, logit_hbm, rate_hbm,
    dx_ref, dlogit_ref, drate_ref, weight_ref, t_ref, w_ref, x_ref, g_ref, logit_ref, rate_ref,
    b_ref, c_ref, c_in, b_turned, c_turned, c_in_turned, cols1, cols2, rows_ref, span, span_in, cf, cf_in,
    e_own, e_other, f_own, f_other, scores, d_scores, d_b, d_c,
    sums1, sums2, row_sums, back, back_in,
    gs_snd, gs_in, e_in, f_in, e_snd, f_snd,
    load_sem, small_sem, gs_sem, e_sem, f_sem, *more,
):
    if fused:
        (
            tok_snd, tok_in, tok, gbc_snd, gbc_in, gbc, acc, got, out,
            tok_sem, gbc_sem, acc_sem, out_sem,
        ) = more
    chunks = gs_snd.shape[0]
    length, state = b_ref.shape
    heads = logit_ref.shape[0]
    width = HEADS * size
    nz = n // 2
    me = lax.axis_index("seq")
    odd = lax.rem(me, 2)
    z = lax.div(me, 2)
    partner = me + 1 - 2 * odd
    first, last = z == 0, z == nz - 1
    barrier = pltpu.get_barrier_semaphore()
    operands = (
        (logit_hbm, logit_ref), (rate_hbm, rate_ref),
        (g_hbm, g_ref), (t_hbm, t_ref), (w_hbm, w_ref), (x_hbm, x_ref),
    )
    load_logit, load_rate, load_g, load_t, load_w, load_x = (
        pltpu.make_async_copy(source, target, load_sem.at[i])
        for i, (source, target) in enumerate(operands)
    )

    def greet(who, axis="seq"):
        pl.semaphore_signal(
            barrier, inc=1, device_id={axis: who}, device_id_type=pl.DeviceIdType.MESH
        )

    load_logit.start()
    load_rate.start()
    load_g.start()
    load_t.start()
    load_w.start()
    load_x.start()
    greet(partner)
    pl.when(jnp.logical_not(first))(lambda: greet(me - 2))
    pl.when(jnp.logical_not(last))(lambda: greet(me + 2))
    greeters = 1
    if fused:
        for r in range(4, n, 2):
            greet(flip(me, r, n))
            greeters += 1
        for k in range(1, m):
            greet(flip(lax.axis_index("dp"), k, m), "dp")
            greeters += 1

    def send(src, dst, sems, k, who, axis="seq"):
        return pltpu.make_async_remote_copy(
            src_ref=src, dst_ref=dst, send_sem=sems.at[0, k], recv_sem=sems.at[1, k],
            device_id={axis: who}, device_id_type=pl.DeviceIdType.MESH,
        )

    def copy_span():
        return send(span, span_in, small_sem, 0, partner)

    def copy_c():
        return send(cf, cf_in, small_sem, 1, partner)

    def copy_back(i):
        return send(back.at[i], back_in.at[i], small_sem, 2 + i, partner)

    def copy_g(k):
        return send(gs_snd.at[k], gs_in.at[k], gs_sem, k, partner)

    part = state // PARTS

    def copy_e(k, i):
        rows = pl.ds(i * part, part)
        return send(e_snd.at[k, rows], e_in.at[k, rows], e_sem, PARTS * k + i, me + 2)

    def copy_f(k, i):
        rows = pl.ds(i * part, part)
        return send(f_snd.at[k, rows], f_in.at[k, rows], f_sem, PARTS * k + i, me - 2)

    def turn(value, k):
        lanes = value.shape[1]
        return pltpu.roll(value, lax.rem(lanes - HEADS * k, lanes), 1)

    def wide(k):
        return pl.ds(pl.multiple_of(k * width, width), width)

    load_logit.wait()
    load_rate.wait()
    logit, rate = logit_ref[...], rate_ref[...]
    dt_all = (jnp.maximum(logit, 0.0) + jnp.log1p(jnp.exp(-jnp.abs(logit)))).T
    row_at = lax.broadcasted_iota(jnp.int32, (length, length), 0)
    col_at = lax.broadcasted_iota(jnp.int32, (length, length), 1)
    until = (row_at >= col_at).astype(F32)
    log_decay = exact_dot(until, -rate * dt_all, 1, 0)
    to_end = jnp.exp(log_decay[length - 1 : length, :] - log_decay)
    grow_all = jnp.exp(log_decay)
    q1 = jnp.concatenate([log_decay, dt_all], axis=1)
    q2 = jnp.concatenate([to_end, grow_all], axis=1)
    span[...] = jnp.broadcast_to(q2[length - 1 : length, :], span.shape)
    def scale(k, unused):
        cols1[k] = turn(q1, k)
        cols = turn(q2, k)
        cols2[k] = cols
        gs_snd[k] = g_ref[:, wide(k)].astype(F32) * pair_columns(cols, heads, size)
        copy_g(k).start()
        return unused

    load_g.wait()
    end = jnp.logical_or(first, last)
    pl.when(end)(lambda: pl.semaphore_wait(barrier, min(nz - 1, 1) + greeters))
    pl.when(jnp.logical_not(end))(lambda: pl.semaphore_wait(barrier, 2 + greeters))
    copy_span().start()
    lax.fori_loop(0, FIRST, scale, 0)
    load_t.wait()
    load_w.wait()
    bc = dot(t_ref[...], w_ref[...], 1, 0).astype(BF16)
    b_ref[...] = bc[:, :state]
    c_ref[...] = bc[:, state:]
    cf[...] = bc[:, state:].astype(F32)
    copy_c().start()
    lax.fori_loop(FIRST, EARLY, scale, 0)
    b_turned[...] = b_ref[...].astype(F32).T.astype(BF16)
    c_turned[...] = cf[...].T.astype(BF16)
    by_head = q1.T
    for k in range(chunks):
        rows_ref[k] = by_head[HEADS * k : HEADS * (k + 1), :]
    load_x.wait()
    scores[...] = dot(b_ref[...], c_ref[...], 1, 1)
    for ref in (d_scores, d_b, d_c, sums1, sums2, row_sums, back):
        ref[...] = jnp.zeros_like(ref)
    copy_span().wait_recv()

    def receive_c():
        copy_c().wait_recv()
        c_in[...] = cf_in[...].astype(BF16)
        c_in_turned[...] = cf_in[...].T.astype(BF16)

    def spans(ref, k):
        return pair_columns(turn(ref[...], k)[:1, :], heads, size)

    def forward(k):
        weight = pair_columns(cols1[k], heads, size) * pair_columns(cols2[k], 0, size)
        near = dot(b_turned[...], (x_ref[:, wide(k)].astype(F32) * weight).astype(BF16), 1, 0)
        mine, theirs = spans(span, k), spans(span_in, k)

        @pl.when(first)
        def _():
            e_in[k] = jnp.zeros_like(e_in[k])

        for i in range(PARTS):
            rows = slice(i * part, (i + 1) * part)
            pl.when(jnp.logical_not(first))(lambda: copy_e(k, i).wait_recv())
            value = e_in[k, rows]

            @pl.when(odd == 0)
            def _():
                e_own[k, rows] = value.astype(BF16)
                middle = mine * value + near[rows]
                e_other[k, rows] = middle.astype(BF16)
                e_snd[k, rows] = theirs * middle

            @pl.when(odd == 1)
            def _():
                e_other[k, rows] = value.astype(BF16)
                middle = theirs * value
                e_own[k, rows] = middle.astype(BF16)
                e_snd[k, rows] = mine * middle + near[rows]

            pl.when(jnp.logical_not(last))(lambda: copy_e(k, i).start())

    def backward(k):
        copy_g(k).wait_recv()
        near = dot(c_turned[...], gs_snd[k].astype(BF16), 1, 0)
        far = dot(c_in_turned[...], gs_in[k].astype(BF16), 1, 0)
        mine, theirs = spans(span, k), spans(span_in, k)

        @pl.when(last)
        def _():
            f_in[k] = jnp.zeros_like(f_in[k])

        for i in range(PARTS):
            rows = slice(i * part, (i + 1) * part)
            pl.when(jnp.logical_not(last))(lambda: copy_f(k, i).wait_recv())
            value = f_in[k, rows]

            @pl.when(odd == 0)
            def _():
                f_other[k, rows] = value.astype(BF16)
                middle = theirs * value + far[rows]
                f_own[k, rows] = middle.astype(BF16)
                f_snd[k, rows] = mine * middle + near[rows]

            @pl.when(odd == 1)
            def _():
                f_own[k, rows] = value.astype(BF16)
                middle = mine * value + near[rows]
                f_other[k, rows] = middle.astype(BF16)
                f_snd[k, rows] = theirs * middle + far[rows]

            pl.when(jnp.logical_not(first))(lambda: copy_f(k, i).start())

    def gradients(k):
        cols, rows = cols1[k], rows_ref[k]
        k_st = scores[...]
        causal = col_at >= row_at
        low = lax.broadcasted_iota(jnp.int32, (length, width), 1) < size
        place = lax.broadcasted_iota(jnp.int32, sums1.shape, 1) - k * HEADS
        row_place = lax.broadcasted_iota(jnp.int32, row_sums.shape, 0) - k * HEADS
        res1, res2, res3, res_rows = sums1[...], sums2[...], back[1], row_sums[...]
        q_sum = d_scores[...]
        x2, g2 = x_ref[:, wide(k)], g_ref[:, wide(k)]
        x2f = x2.astype(F32)
        e2, f2, e3, f3 = e_own[k], f_own[k], e_other[k], f_other[k]
        gs, gs3 = gs_snd[k], gs_in[k]
        dt2 = pair_columns(cols, heads, size)
        end2 = pair_columns(cols2[k], 0, size)
        g_low = jnp.where(low, g2, jnp.zeros_like(g2))
        g_high = jnp.where(low, jnp.zeros_like(g2), g2)
        g_both = jnp.concatenate([g_low, g_high], axis=0)
        gram = dot(x2, g_both, 1, 1)
        weights = []
        for h in range(HEADS):
            gap = rows[h : h + 1, :] - cols[:, h : h + 1]
            decay = jnp.exp(jnp.where(causal, gap, -jnp.inf))
            mg = decay * gram[:, h * length : (h + 1) * length]
            dt = cols[:, heads + h : heads + h + 1]
            q_sum = q_sum + mg * dt
            raw = mg * k_st
            res_rows = jnp.where(row_place == h, jnp.sum(raw * dt, axis=0, keepdims=True), res_rows)
            res1 = jnp.where(place == h, jnp.sum(raw, axis=1, keepdims=True), res1)
            weights.append((decay * k_st).astype(BF16))
        z2 = dot(jnp.concatenate(weights, axis=1), g_both, 1, 0)
        z_in = dot(b_ref[...], f2, 1, 0) * end2
        dx_ref[:, wide(k)] = (dt2 * (z2 + z_in)).astype(dx_ref.dtype)
        xz = x2f * z_in
        gy = gs * dot(c_ref[...], e2, 1, 0)
        gy3 = gs3 * dot(c_in[...], e3, 1, 0)
        ef = jnp.sum(e2.astype(F32) * f2.astype(F32), axis=0, keepdims=True)
        ef3 = jnp.sum(e3.astype(F32) * f3.astype(F32), axis=0, keepdims=True)
        low_row = low[:1, :]

        def half(value, h, mask):
            keep = mask if h == 0 else jnp.logical_not(mask)
            return jnp.sum(jnp.where(keep, value, jnp.zeros_like(value)), axis=1, keepdims=True)

        for h in range(HEADS):
            res1 = jnp.where(place == h + heads, half(xz, h, low), res1)
            res2 = jnp.where(place == h, half(gy, h, low), res2)
            res2 = jnp.where(place == h + heads, half(ef, h, low_row), res2)
            res3 = jnp.where(place == h, half(gy3, h, low), res3)
            res3 = jnp.where(place == h + heads, half(ef3, h, low_row), res3)
        sums1[...] = res1
        sums2[...] = res2
        back[1] = res3
        row_sums[...] = res_rows
        d_scores[...] = q_sum
        d_b[...] += dot((x2f * (end2 * dt2)).astype(BF16), f2, 1, 1)
        d_c[...] += dot(gs.astype(BF16), e2, 1, 1)
        back[0] += dot(gs3.astype(BF16), e3, 1, 1)

    delay = LAG * lax.max(z, nz - 1 - z)

    def await_tokens():
        for k in range(1, m):
            copy_tokens(k).wait_recv()

    def place_tokens(s):
        for k in range(m):
            block = columns(s, k) if k == 0 else tok_in[k - 1, s]
            tok[s, :, k * length : (k + 1) * length] = block.T.astype(BF16)

    def step(t, unused):
        @pl.when(t + EARLY < chunks)
        def _():
            scale(t + EARLY, 0)

        kf = t - LAG * z

        pl.when(jnp.logical_and(kf >= 0, kf < chunks))(lambda: forward(kf))
        kb = t - LAG * (nz - 1 - z)
        pl.when(kb == 0)(receive_c)
        pl.when(jnp.logical_and(kb >= 0, kb < chunks))(lambda: backward(kb))
        kg = t - delay
        pl.when(jnp.logical_and(kg >= 0, kg < chunks))(lambda: gradients(kg))
        if fused:
            @pl.when(t < n)
            def _():
                spread(t, 0)

            @pl.when(t == n)
            def _():
                for k in range(1, m):
                    copy_tokens(k).start()

            block = t - (chunks + delay - n)
            pl.when(block == 0)(await_tokens)
            pl.when(block >= 0)(lambda: place_tokens(block))
        return unused

    if fused:
        dp = lax.axis_index("dp")
        piece = tok.shape[1]

        def columns(s, k):
            first_column = (s * m + flip(dp, k, m)) * piece
            return t_ref[:, pl.ds(pl.multiple_of(first_column, piece), piece)].astype(F32)

        def copy_tokens(k):
            return send(
                tok_snd.at[k - 1], tok_in.at[k - 1], tok_sem, k - 1, flip(dp, k, m), "dp"
            )

        def copy_gbc(i, k):
            return send(
                gbc_snd.at[i], gbc_in.at[k - 1, i], gbc_sem, (m - 1) * i + k - 1,
                flip(dp, k, m), "dp",
            )

        def copy_acc(i, r):
            who = partner if r % 2 else flip(me, r, n)
            rows = pl.ds(0, piece + 8 * i)
            return send(
                acc.at[i, r, rows], got.at[i, r - 1, rows], acc_sem, (n - 1) * i + r - 1, who
            )

        def copy_out(i, k):
            rows = pl.ds(0, piece + 8 * i)
            return send(
                out.at[i, 0, rows], out.at[i, k, rows], out_sem, m * i + k, flip(dp, k, m), "dp"
            )

        def tree(parts):
            while len(parts) > 1:
                parts = [p + q for p, q in zip(parts[::2], parts[1::2])]
            return parts[0]

        def spread(s, unused):
            for k in range(1, m):
                tok_snd[k - 1, s] = columns(s, k)
            return unused

    lax.fori_loop(0, chunks + delay, step, 0)
    copy_back(0).start()
    copy_back(1).start()
    dk = d_scores[...].astype(BF16)
    grad_b = (d_b[...] + dot(dk, c_ref[...], 1, 0)).astype(BF16)
    if fused:
        gbc_snd[0] = grad_b.astype(F32)
        for k in range(m - 1, 0, -1):
            copy_gbc(0, k).start()
        gbc[0, :length] = grad_b
    else:
        weight_ref[:, :state] = grad_b
    c_total = d_c[...] + dot(dk, b_ref[...], 0, 0)
    copy_back(0).wait_recv()
    grad_c = (c_total + back_in[0]).astype(BF16)
    if fused:
        gbc_snd[1] = grad_c.astype(F32)
        for k in range(m - 1, 0, -1):
            copy_gbc(1, k).start()
        gbc[1, :length] = grad_c
    else:
        weight_ref[:, state:] = grad_c
    copy_span().wait_send()
    copy_c().wait_send()

    def settle(k, unused):
        copy_g(k).wait_send()
        for i in range(PARTS):
            pl.when(jnp.logical_not(last))(lambda: copy_e(k, i).wait_send())
            pl.when(jnp.logical_not(first))(lambda: copy_f(k, i).wait_send())
        return unused

    lax.fori_loop(0, chunks, settle, 0)
    copy_back(1).wait_recv()
    total = sums2[...] + back_in[1]
    inside, x_in = sums1[:, :heads], sums1[:, heads:]
    g_in, both = total[:, :heads], span[:1, heads:] * total[:, heads:]
    dt_all = cols1[0, :, heads:]
    after = (row_at <= col_at).astype(F32)
    before = (row_at > col_at).astype(F32)
    d_log = (
        both
        + exact_dot(before, dt_all * x_in, 1, 0)
        + exact_dot(after, g_in - dt_all * inside, 1, 0)
        + exact_dot(after, row_sums[...], 1, 1)
    )
    d_rate = -jnp.sum(dt_all * d_log, axis=0, keepdims=True)
    d_rate = jnp.broadcast_to(
        jnp.concatenate([d_rate, jnp.zeros_like(d_rate)], axis=1), (8, 2 * heads)
    )
    if not fused:
        drate_ref[...] = d_rate
    d_step = inside + x_in - rate_ref[...] * d_log
    dlogit_ref[...] = d_step.T * jax.nn.sigmoid(logit_ref[...])
    copy_back(0).wait_send()
    copy_back(1).wait_send()
    if fused:
        for k in range(1, m):
            copy_tokens(k).wait_send()
        order = list(range(n - 2, -1, -2))
        for i in range(2):
            for k in range(1, m):
                copy_gbc(i, k).wait_recv()
                gbc[i, k * length : (k + 1) * length] = gbc_in[k - 1, i].astype(BF16)
            for r in [r + 1 for r in order] + order:
                acc[i, r, :piece] = dot(tok[flip(me, r, n)], gbc[i], 1, 0)
                if i == 1:
                    acc[i, r, piece:] = d_rate
                if r % 2:
                    copy_acc(i, r).start()

        def join(i, r):
            rows = slice(0, piece + 8 * i)
            copy_acc(i, r + 1).wait_recv()
            acc[i, r, rows] += got[i, r, rows]
            if r:
                copy_acc(i, r).start()

        def finish(i):
            rows = slice(0, piece + 8 * i)
            parts = [acc[i, 0, rows]]
            for r in range(2, n, 2):
                copy_acc(i, r).wait_recv()
                parts.append(got[i, r - 1, rows])
            out[i, 0, rows] = tree(parts)
            for k in range(m - 1, 0, -1):
                copy_out(i, k).start()

        for i in range(2):
            for k in range(1, m):
                copy_gbc(i, k).wait_send()
        for r in order:
            join(0, r)
        for r in order[: len(order) // 2]:
            join(1, r)
        finish(0)
        for r in order[len(order) // 2 :]:
            join(1, r)
        for r in range(1, n):
            copy_acc(0, r).wait_send()
        finish(1)
        for i in range(2):
            for k in range(m):
                if k:
                    copy_out(i, k).wait_recv()
                first_row = pl.multiple_of(flip(dp, k, m) * piece, piece)
                weight_ref[pl.ds(first_row, piece), i * state : (i + 1) * state] = out[i, k, :piece]
        drate_ref[...] = tree([out[1, k, piece:] for k in range(m)])[:1, :heads]
        for k in range(1, m):
            for i in range(2):
                copy_out(i, k).wait_send()
        for r in range(1, n):
            copy_acc(1, r).wait_send()


def store_kernel(*refs):
    copies = [pltpu.make_async_copy(refs[i], refs[4 + i], refs[8].at[i]) for i in range(4)]
    for copy in copies:
        copy.start()
    for copy in copies:
        copy.wait()


def weight_kernel(
    n, m, t_ref, g_ref, rate_ref, out_ref, rate_out,
    acc, got, ring, r_acc, r_got, sem, out_sem, r_sem,
):
    chunks, blocks, rows = acc.shape[0], acc.shape[1], acc.shape[2]
    piece = chunks * rows
    seq, dp = lax.axis_index("seq"), lax.axis_index("dp")
    dp_steps, seq_steps, bit = [], [], 1
    while bit < m:
        dp_steps.append(("dp", bit, lax.rem(lax.div(dp, bit), 2)))
        bit *= 2
    bit = 1
    while bit < n:
        seq_steps.append(("seq", bit, lax.rem(lax.div(seq, bit), 2)))
        bit *= 2
    count = len(dp_steps) + len(seq_steps)
    orders = (dp_steps + seq_steps, dp_steps[:1] + seq_steps + dp_steps[1:])

    def peer(c, s):
        axis, bit, mine = orders[c % 2][s]
        return {axis: lax.axis_index(axis) + bit - 2 * bit * mine}

    def dp_peer(k):
        other, bit = dp, 1
        while bit < m:
            if k & bit:
                other = other + bit - 2 * bit * lax.rem(lax.div(dp, bit), 2)
            bit *= 2
        return {"dp": other}

    barrier = pltpu.get_barrier_semaphore()
    friends = [dp_peer(k) for k in range(1, m)] + [
        peer(0, s) for s in range(len(dp_steps), count)
    ]
    for friend in friends:
        pl.semaphore_signal(
            barrier, inc=1, device_id=friend, device_id_type=pl.DeviceIdType.MESH
        )

    starts, offsets = [], []
    for order in orders:
        base, width, total = 0, blocks, 0
        starts.append([])
        for unused, unused, mine in order:
            width //= 2
            starts[-1].append((base + width * mine, base + width * (1 - mine), width))
            base = base + width * mine
            if len(starts) == 1:
                offsets.append(total)
                total += width

    def copy(c, s):
        keep, give, size = starts[c % 2][s]
        return pltpu.make_async_remote_copy(
            src_ref=acc.at[c, pl.ds(give, size)],
            dst_ref=got.at[c, pl.ds(offsets[s], size)],
            send_sem=sem.at[0, c, s], recv_sem=sem.at[1, c, s],
            device_id=peer(c, s), device_id_type=pl.DeviceIdType.MESH,
        )

    def rate_copy(s):
        return pltpu.make_async_remote_copy(
            src_ref=r_acc.at[s], dst_ref=r_got.at[s],
            send_sem=r_sem.at[0, s], recv_sem=r_sem.at[1, s],
            device_id=peer(0, s), device_id_type=pl.DeviceIdType.MESH,
        )

    def out_copy(c, k):
        return pltpu.make_async_remote_copy(
            src_ref=ring.at[0, c], dst_ref=ring.at[k, c],
            send_sem=out_sem.at[0, c, k], recv_sem=out_sem.at[1, c, k],
            device_id=dp_peer(k), device_id_type=pl.DeviceIdType.MESH,
        )

    g = g_ref[...]
    r_acc[0] = rate_ref[...]
    block = 128
    for first in range(0, t_ref.shape[1], block):
        product = dot(t_ref[:, first : first + block], g, 0, 0)
        for part in range(0, block, rows):
            row = first + part
            owner, inner = row // (m * piece), row % (m * piece)
            chunk, place = inner % piece // rows, 0
            for axis, bit, unused in orders[chunk % 2]:
                index = inner // piece if axis == "dp" else owner
                place = 2 * place + index // bit % 2
            acc[chunk, place] = product[part : part + rows]
    pl.semaphore_wait(barrier, len(friends))
    for c in range(chunks):
        copy(c, 0).start()
    rate_copy(0).start()
    for s in range(count):
        for c in range(chunks):
            copy(c, s).wait_recv()
            keep, give, size = starts[c % 2][s]
            value = acc[c, pl.ds(keep, size)] + got[c, pl.ds(offsets[s], size)]
            if s + 1 < count:
                acc[c, pl.ds(keep, size)] = value
                copy(c, s + 1).start()
            else:
                ring[0, c] = value[0]
                for k in range(1, m):
                    out_copy(c, k).start()
        rate_copy(s).wait_recv()
        r_acc[s + 1] = r_acc[s] + r_got[s]
        if s + 1 < count:
            rate_copy(s + 1).start()
    rate_out[...] = r_acc[count]
    for c in range(chunks):
        for k in range(m):
            if k > 0:
                out_copy(c, k).wait_recv()
            where = dp_peer(k)["dp"] if k > 0 else dp
            out_ref[pl.ds(where * piece + c * rows, rows)] = ring[k, c]
    for c in range(chunks):
        for s in range(count):
            copy(c, s).wait_send()
        for k in range(1, m):
            out_copy(c, k).wait_send()
    for s in range(count):
        rate_copy(s).wait_send()


def shards(layer_input, projection, ssm_input, step_logit, decay_rate, output_grad):
    tokens, x_rows, logit, grad_rows = layer_input[0], ssm_input[0], step_logit[0], output_grad[0]
    length, full = x_rows.shape
    heads = logit.shape[1]
    size = full // heads
    state = projection.shape[1] // 2
    groups = heads // HEADS
    width = HEADS * size
    count = lax.axis_size("seq")
    limit = 46 * 2**20
    away = pl.BlockSpec(memory_space=pltpu.HBM)
    vmem = pl.BlockSpec(memory_space=pltpu.VMEM)
    slots = pltpu.VMEM((groups, state, width), F32)
    rows_in = pltpu.VMEM((groups, length, width), F32)
    half = pltpu.VMEM((groups, state, width), BF16)
    square = pltpu.VMEM((length, length), F32)
    sums = pltpu.VMEM((length, state), F32)
    short = pltpu.VMEM((length, state), BF16)
    by_lane = pltpu.VMEM((length, 2 * heads), F32)
    cols = pltpu.VMEM((groups, length, 2 * heads), F32)
    strip = pltpu.VMEM((8, 2 * heads), F32)
    two = pltpu.VMEM((2, length, state), F32)
    members = lax.axis_size("dp")
    blocks = count * members
    piece = tokens.shape[1] // blocks
    levels = blocks.bit_length() - 1
    fused = piece % 128 == 0 and 2 * count <= groups
    rows = pltpu.VMEM((length, full), BF16)
    scratch = (
        [rows, pltpu.VMEM(projection.shape, BF16), rows, rows]
        + [pltpu.VMEM((heads, length), F32), pltpu.VMEM((1, heads), F32)]
        + [short] * 3
        + [pltpu.VMEM((state, length), BF16)] * 3
        + [cols] * 2
        + [pltpu.VMEM((groups, HEADS, length), F32), strip, strip, sums, sums]
        + [half] * 4
        + [square, square, sums, sums]
        + [by_lane, by_lane, pltpu.VMEM((heads, length), F32), two, two]
        + [rows_in] * 2
        + [slots] * 4
        + [pltpu.SemaphoreType.DMA((6,)), pltpu.SemaphoreType.DMA((2, 4))]
        + [pltpu.SemaphoreType.DMA((2, groups))]
        + [pltpu.SemaphoreType.DMA((2, PARTS * groups))] * 2
    )
    rate_shape = jax.ShapeDtypeStruct((8, 2 * heads), F32)
    weight_shape = jax.ShapeDtypeStruct((length, 2 * state), BF16)
    if fused:
        others = members - 1
        scratch += [pltpu.VMEM((others, count, length, piece), F32)] * 2
        scratch += [
            pltpu.VMEM((count, piece, members * length), BF16),
            pltpu.VMEM((2, length, state), F32),
            pltpu.VMEM((others, 2, length, state), F32),
            pltpu.VMEM((2, members * length, state), BF16),
            pltpu.VMEM((2, count, piece + 8, state), F32),
            pltpu.VMEM((2, count - 1, piece + 8, state), F32),
            pltpu.VMEM((2, members, piece + 8, state), F32),
            pltpu.SemaphoreType.DMA((2, others)),
            pltpu.SemaphoreType.DMA((2, 2 * others)),
            pltpu.SemaphoreType.DMA((2, 2 * (count - 1))),
            pltpu.SemaphoreType.DMA((2, 2 * members)),
        ]
        rate_shape = pltpu.VMEM((1, heads), F32)
        weight_shape = pltpu.VMEM((members * piece, 2 * state), F32)
    grad_x, grad_logit, rate_rows, weights = pl.pallas_call(
        functools.partial(layer_kernel, count, members, size, fused),
        in_specs=[away] * 6,
        out_specs=[vmem] * 4,
        out_shape=[
            rows,
            pltpu.VMEM((heads, length), F32),
            rate_shape,
            weight_shape,
        ],
        scratch_shapes=scratch,
        compiler_params=pltpu.CompilerParams(
            collective_id=0, has_side_effects=True, vmem_limit_bytes=limit
        ),
        name="layer_gradients",
    )(
        *(
            pltpu.with_memory_space_constraint(v, pltpu.HBM)
            for v in (tokens, projection, x_rows, grad_rows, logit.T, decay_rate[None, :])
        )
    )
    if fused:
        results = (grad_x, grad_logit, rate_rows, weights)
        grad_x, grad_logit, rate_rows, weights = pl.pallas_call(
            store_kernel,
            in_specs=[vmem] * 4,
            out_specs=[away] * 4,
            out_shape=[jax.ShapeDtypeStruct(v.shape, v.dtype) for v in results],
            scratch_shapes=[pltpu.SemaphoreType.DMA((4,))],
            name="store_results",
        )(*(pltpu.with_memory_space_constraint(v, pltpu.VMEM) for v in results))
        return (grad_x[None], grad_logit.T[None], rate_rows[0], weights)
    chunks = max(1, min(8, piece // 8))
    rows = piece // chunks
    weight_rows, rate_sum = pl.pallas_call(
        functools.partial(weight_kernel, count, members),
        in_specs=[vmem] * 3,
        out_specs=[vmem] * 2,
        out_shape=[
            jax.ShapeDtypeStruct((members * piece, 2 * state), F32),
            jax.ShapeDtypeStruct((8, 128), F32),
        ],
        scratch_shapes=[
            pltpu.VMEM((chunks, blocks, rows, 2 * state), F32),
            pltpu.VMEM((chunks, blocks, rows, 2 * state), F32),
            pltpu.VMEM((members, chunks, rows, 2 * state), F32),
            pltpu.VMEM((levels + 1, 8, 128), F32),
            pltpu.VMEM((levels, 8, 128), F32),
            pltpu.SemaphoreType.DMA((2, chunks, levels)),
            pltpu.SemaphoreType.DMA((2, chunks, members)),
            pltpu.SemaphoreType.DMA((2, levels)),
        ],
        compiler_params=pltpu.CompilerParams(
            collective_id=1, has_side_effects=True, vmem_limit_bytes=limit
        ),
        name="weight_gradient",
    )(tokens, weights, rate_rows)
    rate_sum = rate_sum[0, :heads]
    return (grad_x[None], grad_logit.T[None], rate_sum, weight_rows)


def solution(mesh):
    placed = (
        P("dp", "seq", None),
        P(),
        P("dp", "seq", None),
        P("dp", "seq", None),
        P(),
        P("dp", "seq", None),
    )
    return jax.shard_map(
        shards,
        mesh=mesh,
        in_specs=placed,
        out_specs=(P("dp", "seq", None), P("dp", "seq", None), P(), P("seq", None)),
        check_vma=False,
    )
```
